32 devices in a mesh: dp: 16 (over z, y, x), tensor: 2 (over core).
Axes of the slice: x: 2, y: 2, z: 4, core: 2. Of those that a mesh axis runs over, the one named last changes fastest.
Arguments:
- tokens: bfloat16 [8192, 768], P('dp'), may hold values from -6 to 6
- segments: int32 [8192], P('dp'), may hold values from 0 to 8191, as said below
- routes: int32 [8192, 2], P('dp'), may hold values from 0 to 7, as said below
- prev_logits: float32 [8192, 8], P('dp'), may hold values from -3 to 3
- attn_gain: float32 [768], replicated, may hold values from 0.5 to 1.5
- w_qkv: bfloat16 [3, 768, 768], P(None, None, 'tensor'), may hold values from -0.21875 to 0.21875
- w_out: bfloat16 [768, 768], P('tensor'), may hold values from -1.75 to 1.75
- ffn_gain: float32 [768], replicated, may hold values from 0.5 to 1.5
- w_router: bfloat16 [768, 8], replicated, may hold values from -0.109375 to 0.109375
- w_const: bfloat16 [768, 4], replicated, may hold values from -0.21875 to 0.21875
- v_const: float32 [2, 768], replicated, may hold values from -6 to 6
- w_gu: bfloat16 [4, 2, 768, 2048], P(None, None, None, 'tensor'), may hold values from -0.21875 to 0.21875
- w_down: bfloat16 [4, 2048, 768], P(None, 'tensor'), may hold values from -0.75 to 0.75
- cotangent: bfloat16 [8192, 768], P('dp'), may hold values from -6 to 6
Outputs:
- output: bfloat16 [8192, 768], P('dp')
- tokens_grad: float32 [8192, 768], P('dp')
- prev_grad: float32 [8192, 8], P('dp')
- attn_gain_grad: float32 [768], P('dp')
- w_qkv_grad: float32 [3, 768, 768], P(None, 'dp', 'tensor')
- w_out_grad: float32 [768, 768], P('tensor', 'dp')
- ffn_gain_grad: float32 [768], P('dp')
- w_router_grad: float32 [768, 8], P('dp')
- w_const_grad: float32 [768, 4], P('dp')
- v_const_grad: float32 [2, 768], P(None, 'dp')
- w_gu_grad: float32 [4, 2, 768, 2048], P(None, None, 'dp', 'tensor')
- w_down_grad: float32 [4, 2048, 768], P(None, 'tensor', 'dp')
The draws below stay inside these ranges and needn't reach their ends.
Inputs may be any that keep to these rules, and one draw needn't show every extreme that they name: `segments`: ids are non-decreasing along the tokens, and tokens of different packed sequences of 8192 tokens have different ids. `routes`: a token's two experts differ, and the first is a feed-forward expert, a number below 4.
All inputs are finite; a program needn't handle non-finite values.
Results may differ from the reference program's by a relative error of at most 0.019.
Values may be sent and summed in bfloat16 or wider, within the bound.
No kernel may reach another device: no remote copies, remote signals or barrier semaphores. Data moves between devices by JAX's collectives and lax.ppermute only.
A program may use at most 448 MiB of HBM per device.

```python
import math
import jax
import jax.numpy as jnp
from jax import lax

D = 768
H = 12
HD = 64
FF = 2048
E_FFN = 4
NCONST = 2
E_ALL = 8
SPAN = 16
TOK_DEV = 512
SEQ_LEN = 8192
SEQS = 1
TOKENS = 8192


def draw_segments(key, part):
    seq_count = TOKENS // SEQ_LEN
    key_one, key_two, key_three = jax.random.split(key, 3)
    leading = jax.random.randint(key_one, (seq_count, 1), 1, TOK_DEV)
    trailing = jax.random.randint(key_two, (seq_count, 1), 1, TOK_DEV)
    position = jnp.arange(SEQ_LEN, dtype=jnp.int32)[None, :]
    marked = jax.random.randint(key_three, (seq_count, SEQ_LEN), 0, 24) == 0
    outside = (position < leading) | (position >= SEQ_LEN - trailing)
    boundary = marked & outside | (position == leading) | (position == SEQ_LEN - trailing)
    boundary = boundary & (position > 0)
    running = jnp.cumsum(boundary.astype(jnp.int32), axis=1)
    last_running = running[:, SEQ_LEN - 1:SEQ_LEN]
    seq_index = jnp.arange(seq_count, dtype=jnp.int32)[:, None]
    lift = jnp.where(seq_index == seq_count - 1, SEQ_LEN - 1 - last_running, 0)
    base_ids = seq_index * SEQ_LEN
    return (base_ids + running + lift).reshape(-1).astype(jnp.int32)


def draw_routes(key, part):
    key_one, key_two, key_three, key_four, key_five = jax.random.split(key, 5)
    weight_table = jax.random.randint(key_one, (E_FFN,), 1, 6)
    cumulative = jnp.cumsum(weight_table)
    ticket = jax.random.randint(key_two, (TOKENS,), 0, 1 << 20) % cumulative[-1]
    first_route = jnp.sum((ticket[:, None] >= cumulative[None, :]).astype(jnp.int32), axis=1)
    step_ffn = jax.random.randint(key_three, (TOKENS,), 1, E_FFN)
    other_ffn = (first_route + step_ffn) % E_FFN
    zero_kind = E_FFN + jax.random.randint(key_four, (TOKENS,), 0, E_ALL - E_FFN)
    picked = jax.random.randint(key_five, (TOKENS,), 0, 8) == 0
    second_route = jnp.where(picked, zero_kind, other_ffn)
    return jnp.stack([first_route, second_route], axis=1).astype(jnp.int32)


def strengthened(array, stream_key, source, target, parts, factor):
    def block_of(dim):
        return (jnp.arange(array.shape[dim]) // (array.shape[dim] // parts)).reshape((-1,) + (1,) * (array.ndim - 1 - dim))

    near = jax.random.permutation(stream_key, parts)[block_of(target)]
    second = (block_of(target) + parts // 2) % parts
    return jnp.where((block_of(source) == near) | (block_of(source) == second), factor * array, array)


def level_of(stream_key, dims, cuts, least, top_value):
    gain = 1.0
    for dim, blocks in cuts:
        draws = jax.random.uniform(jax.random.fold_in(jax.random.fold_in(stream_key, 6), dim), (blocks,), jnp.float32, least / len(cuts), top_value / len(cuts))
        gain = gain * jnp.repeat(jnp.exp(draws), dims[dim] // blocks).reshape((-1,) + (1,) * (len(dims) - 1 - dim))
    return gain


def normal_values(own_key, shape, width, bound, cuts=(), kind=jnp.bfloat16):
    factor_of = level_of(own_key, shape, cuts, -0.22, 0.18) if cuts else 1.0
    drawn = jax.random.normal(own_key, shape, jnp.float32) * width * factor_of
    return jnp.minimum(jnp.maximum(drawn, -bound), bound).astype(kind)


def gaussian_with(rng, shape, deviation, reach, cuts, heavy, held_as=jnp.bfloat16):
    values = deviation * jax.random.normal(rng, shape, jnp.float32)
    if cuts:
        values = values * level_of(rng, shape, cuts, -0.22, 0.18)
    return jnp.clip(strengthened(values, jax.random.fold_in(rng, 3), *heavy), -reach, reach).astype(held_as)


def setup_inputs(seed: int = 0) -> dict:
    arg_keys = jax.random.split(jax.random.key(seed), 15)
    return {
        "tokens": normal_values(arg_keys[0], (TOKENS, D), 1.0, 6.0, ((0, 16),)),
        "segments": draw_segments(jax.random.fold_in(arg_keys[14], 71), 0),
        "routes": draw_routes(jax.random.fold_in(arg_keys[14], 71), 0),
        "prev_logits": normal_values(arg_keys[3], (TOKENS, E_ALL), 0.5, 3.0, ((0, 16),), jnp.float32),
        "attn_gain": jnp.clip(1.0 + 0.1 * jax.random.normal(arg_keys[4], (D,), jnp.float32), 0.5, 1.5),
        "w_qkv": normal_values(arg_keys[5], (3, D, H * HD), D ** -0.5, 0.21875, ((2, 2),)),
        "w_out": normal_values(arg_keys[6], (H * HD, D), (H * HD // 64) ** -0.5, 1.75, ((0, 2),)),
        "ffn_gain": jnp.clip(1.0 + 0.1 * jax.random.normal(arg_keys[7], (D,), jnp.float32), 0.5, 1.5),
        "w_router": normal_values(arg_keys[8], (D, E_ALL), (4 * D) ** -0.5, 0.109375),
        "w_const": normal_values(arg_keys[9], (D, 2 * NCONST), D ** -0.5, 0.21875),
        "v_const": normal_values(arg_keys[10], (NCONST, D), 1.0, 6.0, (), jnp.float32),
        "w_gu": normal_values(arg_keys[11], (E_FFN, 2, D, FF), D ** -0.5, 0.21875, ((3, 2),)),
        "w_down": normal_values(arg_keys[12], (E_FFN, FF, D), (FF // 32) ** -0.5, 0.75, ((1, 2),)),
        "cotangent": gaussian_with(arg_keys[13], (TOKENS, D), 1.0, 6.0, ((0, 16),), (0, 1, 16, 2.0)),
    }


EPSILON = 1e-05
HIGHEST = lax.Precision.HIGHEST

@jax.custom_vjp
def low(v):
    return lax.optimization_barrier(v.astype(jnp.bfloat16)).astype(jnp.float32)

@jax.custom_vjp
def low_back(v):
    return v

def low_keep(v):
    return (low(v), None)

def low_pass(kept, grad):
    return (grad,)

def back_keep(v):
    return (v, None)

def back_low(kept, grad):
    return (low(grad),)
low.defvjp(low_keep, low_pass)
low_back.defvjp(back_keep, back_low)

def rms_norm(values, gain_vec):
    inverse = lax.rsqrt(lax.optimization_barrier(jnp.mean(values * values, axis=-1, keepdims=True)) + EPSILON)
    return values * inverse * gain_vec

def rotary_tables(global_index, half_dim):
    position = (global_index % SEQ_LEN).astype(jnp.float32)
    inv_freq = jnp.exp(jnp.arange(half_dim).astype(jnp.float32) * (-math.log(10000.0) / half_dim))
    phases = position[:, None] * inv_freq[None, :]
    return (jnp.cos(phases)[:, None, :], jnp.sin(phases)[:, None, :])

def rotate(values, cosine_table, sine_table):
    half_dim = values.shape[-1] // 2
    first_half = values[..., :half_dim]
    second_half = values[..., half_dim:]
    return jnp.concatenate([first_half * cosine_table - second_half * sine_table, second_half * cosine_table + first_half * sine_table], axis=-1)

def sequence_attention(packed):
    queries, keys_rot, values_low, seg_ids = packed
    index_all = jnp.arange(SEQ_LEN, dtype=jnp.int32)
    inverse_root = 1.0 / math.sqrt(HD)

    def query_block(offset):
        block_query = lax.dynamic_slice_in_dim(queries, offset, TOK_DEV, 0)
        block_index = lax.dynamic_slice_in_dim(index_all, offset, TOK_DEV, 0)
        block_seg = lax.dynamic_slice_in_dim(seg_ids, offset, TOK_DEV, 0)
        raw_scores = jnp.einsum('qhd,khd->hqk', block_query, keys_rot, precision=HIGHEST) * inverse_root
        scores = low_back(raw_scores)
        allowed = (block_seg[:, None] == seg_ids[None, :]) & (index_all[None, :] <= block_index[:, None])
        expon = jnp.where(allowed[None], jnp.exp(jnp.where(allowed[None], scores, 0.0)), 0.0)
        weights_now = low(expon / lax.optimization_barrier(jnp.sum(expon, axis=-1, keepdims=True)))
        return jnp.einsum('hqk,khd->qhd', weights_now, values_low, precision=HIGHEST)
    offsets = (jnp.arange(SPAN) * TOK_DEV).astype(jnp.int32)
    blocks_out = lax.map(jax.checkpoint(query_block), offsets)
    return blocks_out.reshape(SEQ_LEN, H, HD)

def forward(tokens_in, attn_in, qkv_in, out_in, ffn_in, router_in, const_in, vconst_in, gu_in, down_in, prev_in, segments, routes):
    normed_attn = low(rms_norm(tokens_in, attn_in))
    qkv_proj = low_back(jnp.einsum('td,sdf->stf', normed_attn, qkv_in, precision=HIGHEST))
    cosine_table, sine_table = rotary_tables(jnp.arange(TOKENS, dtype=jnp.int32), HD // 2)
    shaped = (TOKENS, H, HD)
    queries = low(rotate(qkv_proj[0].reshape(shaped), cosine_table, sine_table))
    keys_rot = low(rotate(qkv_proj[1].reshape(shaped), cosine_table, sine_table))
    values_low = low(qkv_proj[2].reshape(shaped))
    grouped = (SEQS, SEQ_LEN, H, HD)
    heads_out = lax.map(sequence_attention, (queries.reshape(grouped), keys_rot.reshape(grouped), values_low.reshape(grouped), segments.reshape(SEQS, SEQ_LEN)))
    heads_low = low(low_back(heads_out.reshape(TOKENS, H * HD)))
    branch = low_back(jnp.dot(heads_low, out_in, precision=HIGHEST))
    residual = tokens_in + branch
    normed_ffn = rms_norm(residual, ffn_in)
    normed_low = low(normed_ffn)
    router_probs = jax.nn.softmax(jnp.dot(normed_low, router_in, precision=HIGHEST) + prev_in, axis=-1)
    route_hot = (routes[:, :, None] == jnp.arange(E_ALL, dtype=jnp.int32)[None, None, :]).astype(router_probs.dtype)
    gating = lax.optimization_barrier(jnp.sum(route_hot * router_probs[:, None, :], axis=-1))
    expert_weight = lax.optimization_barrier(jnp.sum(route_hot * gating[:, :, None], axis=1))

    def expert_branch(weights_pair):
        gate_up, down_proj = weights_pair
        both_parts = low_back(jnp.einsum('td,sdf->stf', normed_low, gate_up, precision=HIGHEST))
        hidden = low(jax.nn.silu(both_parts[0]) * both_parts[1])
        return low_back(jnp.dot(hidden, down_proj, precision=HIGHEST))
    expert_outs = lax.map(jax.checkpoint(expert_branch), (gu_in, down_in))
    ffn_out = jnp.einsum('te,etd->td', expert_weight[:, :E_FFN], expert_outs, precision=HIGHEST)
    blend_weights = jax.nn.softmax(jnp.dot(normed_low, const_in, precision=HIGHEST).reshape(TOKENS, NCONST, 2), axis=-1)
    const_out = blend_weights[..., 0:1] * normed_ffn[:, None, :] + blend_weights[..., 1:2] * vconst_in[None]
    const_mix = lax.optimization_barrier(jnp.sum(expert_weight[:, E_FFN + 2:, None] * const_out, axis=1))
    return residual + ffn_out + expert_weight[:, E_FFN + 1:E_FFN + 2] * normed_ffn + const_mix

def reference(tokens, segments, routes, prev_logits, attn_gain, w_qkv, w_out, ffn_gain, w_router, w_const, v_const, w_gu, w_down, cotangent):

    def layer_fn(tokens_in, attn_in, qkv_in, out_in, ffn_in, router_in, const_in, vconst_in, gu_in, down_in, prev_in):
        return forward(tokens_in, attn_in, qkv_in, out_in, ffn_in, router_in, const_in, vconst_in, gu_in, down_in, prev_in, segments, routes)
    result, pullback = jax.vjp(layer_fn, tokens.astype(jnp.float32), attn_gain, w_qkv.astype(jnp.float32), w_out.astype(jnp.float32), ffn_gain, w_router.astype(jnp.float32), w_const.astype(jnp.float32), v_const, w_gu.astype(jnp.float32), w_down.astype(jnp.float32), prev_logits)
    gradients = pullback(cotangent.astype(jnp.float32))
    return (result.astype(jnp.bfloat16), gradients[0], gradients[10], gradients[1], gradients[2], gradients[3], gradients[4], gradients[5], gradients[6], gradients[7], gradients[8], gradients[9])
```

```python
import functools
import math

import jax
import jax.numpy as jnp
import numpy as np
from jax import lax
from jax.experimental import pallas as pl
from jax.experimental.pallas import tpu as pltpu
from jax.sharding import Mesh
from jax.sharding import PartitionSpec as P

f32 = jnp.float32
bf = jnp.bfloat16
E_FFN = 4
NCONST = 2
E_ALL = 8
SPAN = 16
SEQ_LEN = 8192
EPSILON = 1e-05
HIGHEST = lax.Precision.HIGHEST
GROUP = ("z", "y", "x")
GATE_ROWS = 16


HD = 64
NEG = -1e30
WIDE = (4, 2, 1)


def dotf(a, b, ca, cb):
    return lax.dot_general(a, b, (((ca,), (cb,)), ((), ())), preferred_element_type=f32)


def key_places(t, blocks, half):
    r = lax.broadcasted_iota(jnp.int32, (blocks * 2 * half, half), 0)
    inside = r % (2 * half)
    return r - inside + jnp.where(inside < half, t * half + inside, (1 - t) * half + inside - half)


def fwd_kernel(nb, half, sc, start_ref, own_ref, oth_ref, o_ref, of_ref, lse_ref, ktm, vt):
    keys = 2 * half
    t = sc[0]

    def prep(j, _):
        at = pl.ds(pl.multiple_of(j * keys, keys), half)
        more = pl.ds(pl.multiple_of(j * keys + half, half), half)
        ktm[at, :] = own_ref[j, HD : 2 * HD, :].T
        ktm[more, :] = oth_ref[j, 0:HD, :].T
        vt[:, at] = own_ref[j, 2 * HD : 3 * HD, :]
        vt[:, more] = oth_ref[j, HD : 2 * HD, :]
        return 0

    lax.fori_loop(0, nb, prep, 0)
    lane = lax.broadcasted_iota(jnp.int32, (1, half), 1)

    def qblock(s, _):
        q = own_ref[s, 0:HD, :] * bf(0.125)
        start_row = start_ref[s]
        last_row = s * keys + t * half + lane
        lo, ml = sc[1 + s], jnp.minimum(sc[1 + nb + s], s)

        def scores(j, n):
            return dotf(ktm[pl.ds(pl.multiple_of(j * keys, keys), n * keys), :], q, 1, 0)

        def allowed(j, n):
            place = key_places(t, n, half) + j * keys
            return (place >= start_row) & (place <= last_row)

        def values(j, n):
            return vt[:, pl.ds(pl.multiple_of(j * keys, keys), n * keys)]

        def emit(o, lse):
            o_ref[s] = o.astype(bf)
            of_ref[s] = o
            lse_ref[s] = lse

        def plain(j, n, c, masked):
            l, acc = c
            p = jnp.exp(scores(j, n))
            if masked:
                p = jnp.where(allowed(j, n), p, 0.0)
            return l + jnp.sum(p, axis=0, keepdims=True), acc + dotf(values(j, n), p.astype(bf), 1, 0)

        c = (jnp.zeros((1, half), f32), jnp.zeros((HD, half), f32))
        c = plain(s, 1, c, True)
        for masked, first, end in ((True, lo, ml), (False, jnp.maximum(lo, ml), s)):
            for n in WIDE:
                count = jnp.maximum(end - first, 0) // n
                c = lax.fori_loop(0, count, lambda i, c: plain(first + i * n, n, c, masked), c)
                first = first + count * n
        l, acc = c
        emit(acc / l, jnp.log(l))
        fine = (jnp.min(l) > 1e-25) & (jnp.max(l) < 1e25)

        @pl.when(jnp.logical_not(fine))
        def _():
            def shifted(j, c):
                m, l, acc = c
                sco = jnp.where(allowed(j, 1), scores(j, 1), NEG)
                mn = jnp.maximum(m, jnp.max(sco, axis=0, keepdims=True))
                p = jnp.exp(sco - mn)
                al = jnp.exp(m - mn)
                return mn, l * al + jnp.sum(p, axis=0, keepdims=True), acc * al + dotf(values(j, 1), p.astype(bf), 1, 0)

            c = (jnp.full((1, half), NEG, f32), jnp.zeros((1, half), f32), jnp.zeros((HD, half), f32))
            c = shifted(s, c)
            m, l, acc = lax.fori_loop(lo, s, shifted, c)
            emit(acc / l, m + jnp.log(l))

        return 0

    lax.fori_loop(0, nb, qblock, 0)


def flash_fwd(sc, start, own, oth):
    nb, _, half = own.shape
    v = pl.BlockSpec(memory_space=pltpu.VMEM)
    return pl.pallas_call(
        functools.partial(fwd_kernel, nb, half),
        out_shape=(
            jax.ShapeDtypeStruct((nb, HD, half), bf),
            jax.ShapeDtypeStruct((nb, HD, half), f32),
            jax.ShapeDtypeStruct((nb, 1, half), f32),
        ),
        in_specs=[pl.BlockSpec(memory_space=pltpu.SMEM), v, v, v],
        out_specs=(v, v, v),
        scratch_shapes=[pltpu.VMEM((nb * 2 * half, HD), bf), pltpu.VMEM((HD, nb * 2 * half), bf)],
        compiler_params=pltpu.CompilerParams(vmem_limit_bytes=48 << 20),
        cost_estimate=pl.CostEstimate(flops=10**9, bytes_accessed=4 << 20, transcendentals=10**6),
        name="flash_fwd",
    )(sc, start, own, oth)


def bwd_kernel(
    nb, half, j0, j1, sc, start_ref, own_ref, oth_ref, do_ref, of_ref, lse_ref,
    dq_ref, dko_ref, dkx_ref, ktm, vtm, kt, qt, dot, dq_acc, dotm, qtm, stats,
):
    keys = 2 * half
    t = sc[0]

    def prep(j, _):
        k = j - j0
        ktm[k, 0:half, :] = own_ref[j, HD : 2 * HD, :].T
        ktm[k, half:keys, :] = oth_ref[j, 0:HD, :].T
        vtm[k, 0:half, :] = own_ref[j, 2 * HD : 3 * HD, :].T
        vtm[k, half:keys, :] = oth_ref[j, HD : 2 * HD, :].T
        kt[k, :, 0:half] = own_ref[j, HD : 2 * HD, :]
        kt[k, :, half:keys] = oth_ref[j, 0:HD, :]
        return 0

    lax.fori_loop(j0, j1, prep, 0)

    def prep_q(s, _):
        at = pl.ds(pl.multiple_of(s * half, half), half)
        q = own_ref[s, 0:HD, :] * bf(0.125)
        qt[:, at] = q
        qtm[at, :] = q.T
        dot[:, at] = do_ref[s]
        dotm[at, :] = do_ref[s].T
        dq_acc[:, at] = jnp.zeros((HD, half), f32)
        stats[0:1, at] = lse_ref[s]
        stats[1:2, at] = jnp.sum(do_ref[s].astype(f32) * of_ref[s], axis=0, keepdims=True)
        return 0

    lax.fori_loop(j0, nb, prep_q, 0)
    lane = lax.broadcasted_iota(jnp.int32, (1, half), 1)

    def kblock(j, _):
        k = j - j0
        kj, vj, ktj = ktm[k], vtm[k], kt[k]

        def tile(s, n, c, masked):
            dk, dv = c
            at = pl.ds(pl.multiple_of(s * half, half), n * half)
            sco = dotf(kj, qt[:, at], 1, 0)
            if masked:
                place = key_places(t, 1, half) + j * keys
                last_row = s * keys + t * half + lane
                sco = jnp.where((place >= start_ref[s]) & (place <= last_row), sco, NEG)
            p = jnp.exp(sco - stats[0:1, at])
            dp = dotf(vj, dot[:, at], 1, 0)
            ds = (p * (dp - stats[1:2, at])).astype(bf)
            dv = dv + dotf(p.astype(bf), dotm[at, :], 1, 0)
            dk = dk + dotf(ds, qtm[at, :], 1, 0)
            dq_acc[:, at] += dotf(ktj, ds, 1, 0)
            return dk, dv

        c = (jnp.zeros((keys, HD), f32), jnp.zeros((keys, HD), f32))
        c = tile(j, 1, c, True)
        mid, hi = sc[1 + 2 * nb + j], sc[1 + 3 * nb + j]
        first = j + 1
        for n in WIDE:
            count = jnp.maximum(mid - first, 0) // n
            c = lax.fori_loop(0, count, lambda i, c: tile(first + i * n, n, c, False), c)
            first = first + count * n
        dk, dv = lax.fori_loop(jnp.maximum(j + 1, mid), hi, lambda s, c: tile(s, 1, c, True), c)
        dk = dk.T
        dv = dv.T
        dko_ref[k, 0:HD, :] = dk[:, 0:half]
        dko_ref[k, HD : 2 * HD, :] = dv[:, 0:half]
        dkx_ref[k, 0:HD, :] = dk[:, half:keys].astype(bf)
        dkx_ref[k, HD : 2 * HD, :] = dv[:, half:keys].astype(bf)
        return 0

    lax.fori_loop(j0, j1, kblock, 0)

    def finish(s, _):
        at = pl.ds(pl.multiple_of(s * half, half), half)
        dq_ref[s] = (dq_acc[:, at] * 0.125).astype(bf)
        return 0

    def nothing(s, _):
        dq_ref[s] = jnp.zeros((HD, half), bf)
        return 0

    lax.fori_loop(0, j0, nothing, 0)
    lax.fori_loop(j0, nb, finish, 0)


def flash_bwd(sc, start, own, oth, do, of, lse, j0, j1):
    nb, _, half = own.shape
    v = pl.BlockSpec(memory_space=pltpu.VMEM)
    n = j1 - j0
    return pl.pallas_call(
        functools.partial(bwd_kernel, nb, half, j0, j1),
        out_shape=(
            jax.ShapeDtypeStruct((nb, HD, half), bf),
            jax.ShapeDtypeStruct((n, 2 * HD, half), f32),
            jax.ShapeDtypeStruct((n, 2 * HD, half), bf),
        ),
        in_specs=[pl.BlockSpec(memory_space=pltpu.SMEM)] + [v] * 6,
        out_specs=(v, v, v),
        scratch_shapes=[
            pltpu.VMEM((n, 2 * half, HD), bf),
            pltpu.VMEM((n, 2 * half, HD), bf),
            pltpu.VMEM((n, HD, 2 * half), bf),
            pltpu.VMEM((HD, nb * half), bf),
            pltpu.VMEM((HD, nb * half), bf),
            pltpu.VMEM((HD, nb * half), f32),
            pltpu.VMEM((nb * half, HD), bf),
            pltpu.VMEM((nb * half, HD), bf),
            pltpu.VMEM((8, nb * half), f32),
        ],
        compiler_params=pltpu.CompilerParams(vmem_limit_bytes=56 << 20),
        cost_estimate=pl.CostEstimate(flops=10**9, bytes_accessed=4 << 20, transcendentals=10**6),
        name="flash_bwd",
    )(sc, start, own, oth, do, of, lse)


def bounds(start_all, t, nb, HB):
    st=start_all.reshape(nb,2,HB)
    mine=lax.dynamic_index_in_dim(st,t,1,keepdims=False)
    first=mine[:,0]; last=mine[:,HB-1]
    B=2*HB
    lo=first//B
    ml=(last+B-1)//B
    j=jnp.arange(nb)
    mid=jnp.sum((last[None,:]<=j[:,None]*B).astype(jnp.int32),axis=1)
    hi=jnp.sum((lo[None,:]<=j[:,None]).astype(jnp.int32),axis=1)
    mid=jnp.minimum(mid,hi)
    sc=jnp.concatenate([jnp.full((1,),t,jnp.int32),lo,ml,mid,hi]).astype(jnp.int32)
    return sc,mine[:,None,:]


def ffn_kernel(e_ref, u_ref, wgu_ref, *refs):
    pieces = refs[:8]
    x_out_ref, g_ref, wh_ref, mine_ref, other_ref, held = refs[8:]
    half = u_ref.shape[1]
    width = x_out_ref.shape[2]
    hidden_units = wgu_ref.shape[3]
    e = e_ref[0]
    step = pl.program_id(0)
    for k in range(8):

        @pl.when(step == k)
        def _(k=k):
            held[...] = pieces[k][...]

    gates = held[half : half + GATE_ROWS, 0:half].astype(f32)
    row = lax.broadcasted_iota(jnp.int32, gates.shape, 0)
    gate_row = jnp.sum(jnp.where((row == e) | (row == e + E_FFN), gates, 0.0), axis=0, keepdims=True)
    gate = jnp.broadcast_to(gate_row, (8, half)).T[:, 0:1]
    x = held[0:half, :]
    x_out_ref[0] = x
    chunk = 256
    total = jnp.zeros((half, width), f32)
    dots = jnp.zeros((8, half), f32)
    ones = jnp.ones((8, chunk), bf)
    for first in range(0, hidden_units, chunk):
        cols = slice(first, first + chunk)
        g = dotf(x, wgu_ref[0, 0, :, cols], 1, 0)
        up = dotf(x, wgu_ref[0, 1, :, cols], 1, 0)
        raw = u_ref[0, :, cols].astype(f32)
        sig = jax.nn.sigmoid(g)
        silu = g * sig
        hid = silu * up
        hg = gate * raw
        dgate = (hg * up * (sig + silu * (1.0 - sig))).astype(bf)
        dup = (hg * silu).astype(bf)
        g_ref[0, :, cols] = dgate
        g_ref[0, :, slice(hidden_units + first, hidden_units + first + chunk)] = dup
        wh_ref[0, :, cols] = (gate * hid).astype(bf)
        dots = dots + dotf(ones, (hid * raw).astype(bf), 1, 1)
        total = total + dotf(dgate, wgu_ref[0, 0, :, cols], 1, 1) + dotf(dup, wgu_ref[0, 1, :, cols], 1, 1)
    drow = lax.broadcasted_iota(jnp.int32, (GATE_ROWS, half), 0)
    placed = jnp.where(drow == e, jnp.broadcast_to(dots[0:1, :], (GATE_ROWS, half)), 0.0).astype(bf)

    def put(ref):
        ref[0, 0:half, :] = total.astype(bf)
        ref[0, half : half + GATE_ROWS, :] = jnp.zeros((GATE_ROWS, width), bf)
        ref[0, half : half + GATE_ROWS, 0:half] = placed

    @pl.when(step < 4)
    def _():
        put(mine_ref)

    @pl.when(step >= 4)
    def _():
        put(other_ref)


def expert_pass(e, pieces, raw_all, wgu):
    rows, width = pieces[0].shape
    half = rows - GATE_ROWS
    hidden_units = wgu.shape[3]
    flops = 8 * half * width * hidden_units * 2 * 4
    return pl.pallas_call(
        ffn_kernel,
        out_shape=(
            jax.ShapeDtypeStruct((8, half, width), bf),
            jax.ShapeDtypeStruct((8, half, 2 * hidden_units), bf),
            jax.ShapeDtypeStruct((8, half, hidden_units), bf),
            jax.ShapeDtypeStruct((4, rows, width), bf),
            jax.ShapeDtypeStruct((4, rows, width), bf),
        ),
        grid_spec=pltpu.PrefetchScalarGridSpec(
            num_scalar_prefetch=1,
            grid=(8,),
            in_specs=[
                pl.BlockSpec((1, half, hidden_units), lambda i, e: (i, 0, 0)),
                pl.BlockSpec((1, 2, width, hidden_units), lambda i, e: (e[0], 0, 0, 0)),
            ]
            + [pl.BlockSpec((rows, width), lambda i, e: (0, 0))] * 8,
            out_specs=(
                pl.BlockSpec((1, half, width), lambda i, e: (i, 0, 0)),
                pl.BlockSpec((1, half, 2 * hidden_units), lambda i, e: (i, 0, 0)),
                pl.BlockSpec((1, half, hidden_units), lambda i, e: (i, 0, 0)),
                pl.BlockSpec((1, rows, width), lambda i, e: (jnp.minimum(i, 3), 0, 0)),
                pl.BlockSpec((1, rows, width), lambda i, e: (jnp.maximum(i - 4, 0), 0, 0)),
            ),
            scratch_shapes=[pltpu.VMEM((rows, width), bf)],
        ),
        compiler_params=pltpu.CompilerParams(vmem_limit_bytes=48 << 20),
        cost_estimate=pl.CostEstimate(flops=flops, bytes_accessed=40 << 20, transcendentals=2 << 20),
        name="expert_pass",
    )(e, raw_all, wgu, *pieces)


def hidden_cotangent_kernel(e_ref, w_ref, *refs):
    pieces, up_ref, raw_ref, held = refs[:8], refs[8], refs[9], refs[10]
    for k in range(8):

        @pl.when(pl.program_id(0) == k)
        def _(k=k):
            held[...] = pieces[k][...]

    rows = held[...]
    up_ref[0] = rows
    raw_ref[0] = dotf(rows, w_ref[0], 1, 1).astype(bf)


def hidden_cotangent(e, pieces, w_down):
    half, width = pieces[0].shape
    hidden_units = w_down.shape[1]
    return pl.pallas_call(
        hidden_cotangent_kernel,
        out_shape=(
            jax.ShapeDtypeStruct((8, half, width), bf),
            jax.ShapeDtypeStruct((8, half, hidden_units), bf),
        ),
        grid_spec=pltpu.PrefetchScalarGridSpec(
            num_scalar_prefetch=1,
            grid=(8,),
            in_specs=[pl.BlockSpec((1, hidden_units, width), lambda i, e: (e[0], 0, 0))]
            + [pl.BlockSpec((half, width), lambda i, e: (0, 0))] * 8,
            out_specs=(
                pl.BlockSpec((1, half, width), lambda i, e: (i, 0, 0)),
                pl.BlockSpec((1, half, hidden_units), lambda i, e: (i, 0, 0)),
            ),
            scratch_shapes=[pltpu.VMEM((half, width), bf)],
        ),
        compiler_params=pltpu.CompilerParams(vmem_limit_bytes=40 << 20),
        cost_estimate=pl.CostEstimate(flops=32 * 10**8, bytes_accessed=12 << 20, transcendentals=0),
        name="hidden_cotangent",
    )(e, w_down, *pieces)


def cot_rows_kernel(first_ref, x_ref, own_ref, other_ref, out_ref):
    heads = own_ref.shape[0] // HD
    out_ref[...] = jnp.zeros(out_ref.shape, bf)
    x = x_ref[...]
    for n, ref in enumerate((own_ref, other_ref)):
        rows = dotf(ref[...], x, 1, 1).astype(bf)
        for h in range(heads):
            out_ref[first_ref[n] + h] = rows[h * HD : (h + 1) * HD]


def cot_rows(first, x, own, other):
    v = pl.BlockSpec(memory_space=pltpu.VMEM)
    return pl.pallas_call(
        cot_rows_kernel,
        out_shape=jax.ShapeDtypeStruct((SPAN, HD, x.shape[0]), bf),
        in_specs=[pl.BlockSpec(memory_space=pltpu.SMEM), v, v, v],
        out_specs=v,
        compiler_params=pltpu.CompilerParams(vmem_limit_bytes=32 << 20),
        cost_estimate=pl.CostEstimate(flops=3 * 10**8, bytes_accessed=2 << 20, transcendentals=0),
        name="cot_rows",
    )(first, x, own, other)


def heads_kernel(first_ref, x_ref, gain_ref, w_ref, cos_ref, sin_ref, *refs):
    buffer_ref, normed_ref = refs[-2:]
    x = x_ref[...].astype(f32)
    inverse = lax.rsqrt(jnp.mean(x * x, axis=-1, keepdims=True) + EPSILON)
    normed = (x * inverse * gain_ref[...]).astype(bf)
    normed_ref[...] = normed
    cosine, sine = cos_ref[...], sin_ref[...]
    heads = w_ref.shape[2] // HD
    first = first_ref[0]
    buffer_ref[...] = refs[0][...] if len(refs) == 3 else jnp.zeros(buffer_ref.shape, bf)
    for s in range(3):
        rows = dotf(normed, w_ref[s], 1, 0).T
        for h in range(heads):
            part = rows[h * HD : (h + 1) * HD]
            if s < 2:
                one, two = part[: HD // 2], part[HD // 2 :]
                part = jnp.concatenate([one * cosine - two * sine, two * cosine + one * sine], axis=0)
            buffer_ref[first + h, s * HD : (s + 1) * HD, :] = part.astype(bf)


def head_rows(first, x, gain, w, cosine, sine, buffer=None):
    half, width = x.shape
    v = pl.BlockSpec(memory_space=pltpu.VMEM)
    given = [] if buffer is None else [buffer]
    return pl.pallas_call(
        heads_kernel,
        out_shape=(
            jax.ShapeDtypeStruct((SPAN, 3 * HD, half), bf),
            jax.ShapeDtypeStruct((half, width), bf),
        ),
        in_specs=[pl.BlockSpec(memory_space=pltpu.SMEM)] + [v] * 5 + [v] * len(given),
        out_specs=(v, v),
        compiler_params=pltpu.CompilerParams(vmem_limit_bytes=40 << 20),
        cost_estimate=pl.CostEstimate(flops=5 * 10**8, bytes_accessed=4 << 20, transcendentals=0),
        name="head_rows",
    )(first, x, gain.reshape(1, width), w, cosine, sine, *given)


def head_grad_kernel(at_ref, dq_ref, dq_more_ref, own_ref, own_more_ref, other_ref, other_more_ref, cos_ref, sin_ref, *refs):
    pieces, grad_ref = refs[:-1], refs[-1]
    width = pieces[0].shape[-1]

    def back(rows, cosine, sine):
        one, two = rows[: HD // 2], rows[HD // 2 :]
        return jnp.concatenate([one * cosine + two * sine, two * cosine - one * sine], axis=0)

    acc = jnp.zeros((3 * HD, width), f32)
    n = 0
    for ref in pieces:
        for i in np.ndindex(*ref.shape[:-2]):
            block = at_ref[n]
            cosine, sine = cos_ref[block], sin_ref[block]
            split = own_ref.shape[0]
            one, two = jnp.minimum(block, split - 1), jnp.maximum(block - split, 0)
            dkv = jnp.where(
                block < split,
                own_ref[one] + other_ref[one].astype(f32),
                own_more_ref[two] + other_more_ref[two].astype(f32),
            )
            rows = jnp.concatenate(
                [back(dq_ref[block].astype(f32) + dq_more_ref[block].astype(f32), cosine, sine), back(dkv[:HD], cosine, sine), dkv[HD:]], axis=0
            ).astype(bf)
            grad_ref[block, 0 : 3 * HD, :] = rows
            acc = acc + dotf(rows, ref[i], 1, 0)
            n += 1
    turned = acc.T.astype(bf)
    blocks = grad_ref.shape[0]
    rows = width // blocks
    for block in range(blocks):
        grad_ref[block, 3 * HD :, :] = jnp.zeros((rows, grad_ref.shape[2]), bf)
        grad_ref[block, 3 * HD :, 0 : 3 * HD] = turned[block * rows : (block + 1) * rows]


def head_grad(at, dq, own, other, cosine, sine, pieces):
    v = pl.BlockSpec(memory_space=pltpu.VMEM)
    width = pieces[0].shape[-1]
    blocks, _, half = dq[0].shape
    return pl.pallas_call(
        head_grad_kernel,
        out_shape=jax.ShapeDtypeStruct((blocks, 3 * HD + width // blocks, half), bf),
        in_specs=[pl.BlockSpec(memory_space=pltpu.SMEM)] + [v] * (8 + len(pieces)),
        out_specs=v,
        compiler_params=pltpu.CompilerParams(vmem_limit_bytes=48 << 20),
        cost_estimate=pl.CostEstimate(flops=12 * 10**8, bytes_accessed=12 << 20, transcendentals=0),
        name="head_grad",
    )(at, *dq, *own, *other, cosine, sine, *pieces)


def swap(value, axis):
    return lax.ppermute(value, axis, [(0, 1), (1, 0)])


def plane_diagonal(value):
    return lax.ppermute(value, ("y", "x"), [(i, 3 - i) for i in range(4)])


def plane_gather(piece):
    mine = [piece, swap(piece, "x"), swap(piece, "y"), plane_diagonal(piece)]
    return mine + [swap(p, "t") for p in mine]


def plane_scatter(mine, other, before, later):
    other = swap(other, "t")
    held = [(mine[k].astype(f32) + other[k].astype(f32)).astype(bf) for k in range(4)]
    held, before, later = lax.optimization_barrier((held, before, later))
    parts = (held[0], swap(held[1], "x"), swap(held[2], "y"), plane_diagonal(held[3]))
    return sum(p.astype(f32) for p in parts), later


def over_z(value, distance):
    return lax.ppermute(value, "z", [(i, i ^ distance) for i in range(4)])


def chunk_of(chunks, at):
    return lax.dynamic_index_in_dim(chunks, jnp.clip(at, 0, 3), 0, keepdims=False)


def chain_send(sums, ahead, right, left):
    z = lax.axis_index("z")

    def joined(at, got):
        chunks = jnp.concatenate([chunk_of(chunks, at) for chunks in sums], axis=1)
        return (chunks.astype(f32) + got.astype(f32)).astype(bf)

    return joined(z + ahead, right), joined(z - ahead, left)


def chain_first(chunks):
    z = lax.axis_index("z")
    return chunk_of(chunks, jnp.where(z == 0, 3, 0))


def chain_ends(sent):
    return lax.ppermute(sent, "z", [(0, 1), (3, 2)])


def chain_move(sent, count):
    right = lax.ppermute(sent[0], "z", [(i, i + 1) for i in range(count)])
    left = lax.ppermute(sent[1], "z", [(3 - i, 2 - i) for i in range(count)])
    return right, left


def total(parts):
    first, rest = parts
    return first.astype(f32) + sum(p.astype(f32) for p in rest)


def plane_rows(chunks):
    b = lax.axis_index(("y", "x"))
    pick = lambda d: lax.dynamic_index_in_dim(chunks, b ^ d, 0, keepdims=False)
    return pick(0), [swap(pick(1), "x"), swap(pick(2), "y"), plane_diagonal(pick(3))]


def after(value, *others):
    return lax.optimization_barrier((value, others))[0]


def over_sequences(rows):
    if lax.axis_size("s") == 1:
        return rows
    return lax.psum_scatter(rows, "s", scatter_dimension=0, tiled=True)


def first_tokens(segments):
    def gathered(value, moved, places):
        low, high = places
        first = jnp.where(low == 0, jnp.stack([value, moved[0]]), jnp.stack([moved[0], value]))
        second = jnp.where(low == 0, jnp.stack([moved[1], moved[2]]), jnp.stack([moved[2], moved[1]]))
        return jnp.where(high == 0, jnp.stack([first, second]), jnp.stack([second, first]))

    z = lax.axis_index("z")
    plane = [swap(segments, "x"), swap(segments, "y"), plane_diagonal(segments)]
    ids = gathered(segments, plane, (lax.axis_index("x"), lax.axis_index("y"))).reshape(-1)
    ids = gathered(ids, [over_z(ids, d) for d in (1, 2, 3)], (z % 2, z // 2)).reshape(-1)
    count = ids.shape[0]
    index = jnp.arange(count, dtype=jnp.int32)
    before = jnp.concatenate([ids[:1], ids[:-1]])
    opens = jnp.where(ids != before, index, 0).reshape(-1, 256)
    n = opens.shape[0]
    lane = jnp.arange(256, dtype=jnp.int32)
    within = jnp.max(jnp.where(lane[None, None, :] <= lane[None, :, None], opens[:, None, :], 0), axis=-1)
    block = jnp.arange(n, dtype=jnp.int32)
    top = jnp.max(opens, axis=1)
    carry = jnp.max(jnp.where(block[None, :] < block[:, None], top[None, :], 0), axis=1)
    return jnp.maximum(within, carry[:, None]).reshape(-1)


def rotary_tables(position, half_dim):
    inv_freq = jnp.exp(jnp.arange(half_dim).astype(f32) * (-math.log(10000.0) / half_dim))
    phases = inv_freq[:, None] * position.astype(f32)[None, :]
    return jnp.cos(phases), jnp.sin(phases)


def rotate(values, cosine, sine):
    half_dim = values.shape[-2] // 2
    one, two = values[..., :half_dim, :], values[..., half_dim:, :]
    return jnp.concatenate([one * cosine - two * sine, two * cosine + one * sine], axis=-2)


def norm_forward(values, gain):
    inverse = lax.rsqrt(jnp.mean(values * values, axis=-1, keepdims=True) + EPSILON)
    return values * inverse * gain, inverse


def norm_backward(values, inverse, gain, upstream):
    scaled = upstream * gain
    inner = jnp.mean(scaled * values, axis=-1, keepdims=True)
    return (
        inverse * scaled - values * inverse * inverse * inverse * inner,
        jnp.sum(upstream * values * inverse, axis=0),
    )


def local(
    tokens,
    segments,
    routes,
    prev_logits,
    attn_gain,
    w_qkv,
    w_out,
    ffn_gain,
    w_router,
    w_const,
    v_const,
    w_gu,
    w_down,
    cotangent,
):
    tok_count, width = tokens.shape
    half = tok_count // 2
    features = w_qkv.shape[2]
    heads = features // HD
    t = lax.axis_index("t")
    place = lax.axis_index(GROUP)
    expert = lax.axis_index(("y", "x"))

    def mine(value):
        return lax.dynamic_slice_in_dim(value, t * half, half, 0)

    def both_halves(value):
        other = swap(value, "t")
        whole = jnp.zeros((tok_count,) + value.shape[1:], value.dtype)
        whole = lax.dynamic_update_slice_in_dim(whole, value, t * half, 0)
        return lax.dynamic_update_slice_in_dim(whole, other, (1 - t) * half, 0)

    w_qkv_other = swap(w_qkv, "t")
    w_out_other = swap(w_out, "t")
    inputs = mine(tokens).astype(f32)
    upstream_low = mine(cotangent)
    upstream = upstream_low.astype(f32)
    my_routes = jnp.transpose(mine(routes))
    my_prev = jnp.transpose(mine(prev_logits))
    kinds = jnp.arange(E_ALL, dtype=jnp.int32)[:, None]
    hot = (my_routes[0:1] == kinds).astype(f32) + (my_routes[1:2] == kinds).astype(f32)
    position = (place * tok_count + t * half + jnp.arange(half, dtype=jnp.int32)) % SEQ_LEN
    cosine, sine = rotary_tables(position, HD // 2)
    tokens_mine = mine(tokens)
    first = (t * heads).astype(jnp.int32).reshape(1)
    other_first = ((1 - t) * heads).astype(jnp.int32).reshape(1)
    buffer, normed_low = head_rows(first, tokens_mine, attn_gain, w_qkv, cosine, sine)
    buffer, _ = head_rows(other_first, tokens_mine, attn_gain, w_qkv_other, cosine, sine, buffer)

    def of_heads(buffer):
        return (
            lax.dynamic_slice_in_dim(buffer, t * heads, heads, 0),
            lax.dynamic_slice_in_dim(buffer, (1 - t) * heads, heads, 0),
        )

    def exchange(buffer):
        return lax.all_to_all(buffer, GROUP, 0, 0, tiled=True)

    upstream_sent, segments, buffer = lax.optimization_barrier((upstream_low, segments, buffer))
    start_all = first_tokens(segments)
    sc, start_rows = bounds(start_all, t, SPAN, half)
    own = exchange(buffer)
    oth = swap(own[:, HD:], "t")
    up_pieces = plane_gather(upstream_sent)
    expert_at = expert.astype(jnp.int32).reshape(1)
    normed_sent, own_q, up_pieces = lax.optimization_barrier((normed_low, own, up_pieces))
    along_z = [normed_sent] + [over_z(normed_sent, d) for d in (1, 2, 3)]
    heads_rows, heads_full, lse = flash_fwd(sc, start_rows, own_q, oth)
    heads_rows, along_z, up_pieces = lax.optimization_barrier((heads_rows, along_z, up_pieces))
    back = exchange(heads_rows)
    up_all, raw_all = hidden_cotangent(expert_at, up_pieces, w_down)
    back, raw_all = lax.optimization_barrier((back, raw_all))
    heads_own, heads_other = (v.reshape(features, half) for v in of_heads(back))
    branch = dotf(heads_own, w_out, 0, 0) + dotf(heads_other, w_out_other, 0, 0)
    residual = inputs + branch
    normed_ffn, inverse_ffn = norm_forward(residual, ffn_gain)
    ffn_low = normed_ffn.astype(bf)
    w_small = jnp.concatenate([w_router, w_const], axis=1)
    logits = dotf(w_small, ffn_low, 0, 1)
    router_probs = jax.nn.softmax(logits[:E_ALL] + my_prev, axis=0)
    expert_weight = router_probs * hot
    gate_rows = expert_weight[:E_FFN]
    gate_high = gate_rows.astype(bf)
    gate_low = (gate_rows - gate_high.astype(f32)).astype(bf)
    gate_block = jnp.pad(
        jnp.concatenate([gate_high, gate_low]), ((0, GATE_ROWS - 2 * E_FFN), (0, width - half))
    )
    x_all = plane_gather(jnp.concatenate([ffn_low, gate_block]))
    pair_a, pair_b = after((jnp.stack(along_z[:2]), jnp.stack(along_z[2:])), x_all)
    pair_ax, pair_by = swap(pair_a, "x"), swap(pair_b, "y")
    x_only, g_all, weighted, dx_mine, dx_other = expert_pass(expert_at, x_all, raw_all, w_gu)
    dx_mine, dx_other, pair_ax, pair_by = lax.optimization_barrier((dx_mine, dx_other, pair_ax, pair_by))
    hidden_units = w_down.shape[1]
    down_part = jnp.einsum("ptd,ptf->df", up_all, weighted, preferred_element_type=f32).astype(bf)
    received, (weighted, g_all) = plane_scatter(dx_mine, dx_other, down_part, (weighted, g_all))
    gu_part = jnp.einsum("ptd,ptf->df", x_only, g_all, preferred_element_type=f32).astype(bf)
    expert_part = over_sequences(jnp.concatenate([gu_part, down_part], axis=1))
    slab = expert_part.shape[0] // SPAN
    expert_part = expert_part.reshape(4, 4 * slab, 3 * hidden_units)
    expert_first = chain_first(expert_part)
    wdown_mine = lax.dynamic_index_in_dim(w_down, expert, 0, keepdims=False)
    out_mine = jnp.einsum("ptf,fd->ptd", weighted[:4], wdown_mine, preferred_element_type=f32).astype(bf)
    out_beside = jnp.einsum("ptf,fd->ptd", weighted[4:], wdown_mine, preferred_element_type=f32).astype(bf)
    received, expert_part, expert_first, out_mine, out_beside = lax.optimization_barrier(
        (received, expert_part, expert_first, out_mine, out_beside)
    )
    expert_got = chain_ends(expert_first)
    out_beside = swap(out_beside, "t")

    pairs = logits[E_ALL:].reshape(NCONST, 2, half)
    blend_one = jax.nn.sigmoid(pairs[:, 0] - pairs[:, 1])
    blend_two = jax.nn.sigmoid(pairs[:, 1] - pairs[:, 0])
    const_weight = expert_weight[E_FFN + 2 :]
    kept = expert_weight[E_FFN + 1 : E_FFN + 2] + jnp.sum(const_weight * blend_one, axis=0, keepdims=True)
    added = const_weight * blend_two
    columns = jnp.transpose(jnp.concatenate([kept, added]))
    kept_column, added_columns = columns[:, 0:1], columns[:, 1:]

    dx = received[:half]
    gating_ffn = received[half : half + E_FFN, :half]
    copy_dot = jnp.sum(upstream * normed_ffn, axis=-1)[None, :]
    vector_dot = lax.dot_general(v_const, upstream, (((1,), (1,)), ((), ())), precision=HIGHEST)
    const_dot = blend_one * copy_dot + blend_two * vector_dot
    dots = jnp.concatenate([gating_ffn, jnp.zeros((1, half), f32), copy_dot, const_dot])
    probs_grad = dots * hot
    prev_grad = router_probs * (probs_grad - jnp.sum(router_probs * probs_grad, axis=0, keepdims=True))
    grad_one = const_weight * copy_dot
    grad_two = const_weight * vector_dot
    inner = blend_one * grad_one + blend_two * grad_two
    const_grad = jnp.stack([blend_one * (grad_one - inner), blend_two * (grad_two - inner)], axis=1)
    logit_grad = jnp.concatenate([prev_grad, const_grad.reshape(2 * NCONST, half)])
    normed_grad = (
        dx
        + lax.dot_general(logit_grad, w_small.astype(f32), (((0,), (1,)), ((), ())), precision=HIGHEST)
        + kept_column * upstream
    )
    norm_grad, ffn_gain_part = norm_backward(residual, inverse_ffn, ffn_gain, normed_grad)
    residual_grad = upstream + norm_grad
    branch_cot = residual_grad.astype(bf)

    cot = cot_rows(jnp.concatenate([first, other_first]), branch_cot, w_out, w_out_other)
    small = jnp.concatenate(
        [
            ffn_gain_part[None],
            jnp.dot(logit_grad, ffn_low.astype(f32), precision=HIGHEST),
            jnp.dot(added, upstream, precision=HIGHEST),
        ]
    )
    small = jnp.transpose(jnp.pad(small, ((0, 128 - small.shape[0]), (0, 0)))).astype(bf)
    out_own = dotf(branch_cot, heads_own, 0, 1).astype(bf)
    out_other = dotf(branch_cot, heads_other, 0, 1).astype(bf)
    out_part = (out_own.astype(f32) + swap(out_other, "t").astype(f32)).astype(bf)
    out_part = over_sequences(jnp.concatenate([out_part, small], axis=1))
    out_part = out_part.reshape(4, 4 * slab, out_part.shape[1])
    got_out = chain_ends(chain_first(out_part))
    got = jnp.concatenate([expert_got, got_out], axis=1)
    sums = (expert_part, out_part)
    sent_parts = chain_send(sums, 2, got, got)
    held = [(out_mine[k].astype(f32) + out_beside[k].astype(f32)).astype(bf) for k in range(4)]

    t_late = after(t, heads_rows)
    all_position = (jnp.arange(SPAN, dtype=jnp.int32)[:, None] * tok_count + t_late * half)[:, :, None] + jnp.arange(half, dtype=jnp.int32)
    all_cosine, all_sine = rotary_tables(all_position.reshape(-1), HD // 2)
    by_block = lambda table: jnp.transpose(table.reshape(HD // 2, SPAN, half), (1, 0, 2))
    all_cosine, all_sine = by_block(all_cosine), by_block(all_sine)
    cot = exchange(cot)
    stack_a, stack_b = jnp.stack([pair_a, pair_ax]), jnp.stack([pair_b, pair_by])
    cot, held, stack_a, stack_b, sent_parts, all_cosine, all_sine = lax.optimization_barrier(
        (cot, held, stack_a, stack_b, sent_parts, all_cosine, all_sine)
    )
    pair_ya, pair_xb = swap(stack_a, "y"), swap(stack_b, "x")
    got = chain_move(sent_parts, 2)
    split = 5
    dq_one, own_one, oth_one = flash_bwd(sc, start_rows, own, oth, cot, heads_full, lse, 0, split)
    cot, oth_one, pair_ya, pair_xb, got = lax.optimization_barrier((cot, oth_one, pair_ya, pair_xb, got))
    oth_one = swap(oth_one, "t")
    sent_parts = chain_send(sums, 1, *got)
    cot, sent_parts, oth_one = lax.optimization_barrier((cot, sent_parts, oth_one))
    got = chain_move(sent_parts, 3)
    moved_out = [swap(held[1], "x"), swap(held[2], "y"), plane_diagonal(held[3])]
    dq_two, own_two, oth_two = flash_bwd(sc, start_rows, own, oth, cot, heads_full, lse, split, SPAN)
    oth_two, got, moved_out = lax.optimization_barrier((oth_two, got, moved_out))
    oth_two = swap(oth_two, "t")
    near = (0, 4, 8, 12, 1, 5, 10, 14, 2, 6, 3, 7, 9, 13, 11, 15)
    at = jnp.bitwise_xor(place, jnp.array(near, jnp.int32)).astype(jnp.int32)
    pieces = [pair_a, pair_b, pair_ax, pair_by, pair_ya, pair_xb]
    sent = head_grad(at, (dq_one, dq_two), (own_one, own_two), (oth_one, oth_two), all_cosine, all_sine, pieces)
    if lax.axis_size("s") > 1:
        head_part = over_sequences(sent[:, 3 * HD :, : 3 * HD].reshape(width, 3 * HD))
        head_part = jnp.pad(head_part.reshape(SPAN, slab, 3 * HD), ((0, 0), (0, 0), (0, half - 3 * HD)))
        sent = jnp.concatenate([sent[:, : 3 * HD], head_part], axis=1)
    sent, sums, got, held, moved_out, prev_grad, w_qkv, w_qkv_other = lax.optimization_barrier(
        (sent, sums, got, held, moved_out, prev_grad, w_qkv, w_qkv_other)
    )
    ffn_sum = sum(v.astype(f32) for v in [held[0]] + moved_out)
    arrived = exchange(sent)

    def feature_rows(w):
        return jnp.transpose(w.reshape(3, width, heads, HD), (2, 0, 3, 1)).reshape(3 * features, width)

    w_rows, w_rows_other = feature_rows(w_qkv), feature_rows(w_qkv_other)
    prev_both = both_halves(jnp.transpose(prev_grad))
    mixture = residual + ffn_sum + kept_column * normed_ffn + jnp.dot(added_columns, v_const, precision=HIGHEST)
    output = both_halves(mixture.astype(bf))
    kept_parts = jnp.concatenate([chunk_of(chunks, lax.axis_index("z")) for chunks in sums], axis=1)
    parts = (kept_parts.astype(f32) + got[0].astype(f32) + got[1].astype(f32)).astype(bf)
    parts = parts.reshape(4, slab, parts.shape[1])
    own_rows, got_rows = plane_rows(parts)
    columns_ffn = 3 * hidden_units
    ranks = jnp.bitwise_xor(expert, jnp.arange(4))
    by_distance = jnp.stack([rows[:, :columns_ffn] for rows in [own_rows] + got_rows])
    expert_rows = jnp.stack([lax.dynamic_index_in_dim(by_distance, ranks[k], 0, keepdims=False) for k in range(4)]).astype(f32)
    out_done = sum(rows[:, columns_ffn:].astype(f32) for rows in [own_rows] + got_rows)
    small = out_done[:, features:]
    small = small + swap(small, "t")
    w_gu_grad = jnp.transpose(
        expert_rows[:, :, : 2 * hidden_units].reshape(E_FFN, slab, 2, hidden_units), (0, 2, 1, 3)
    )
    w_down_grad = jnp.transpose(expert_rows[:, :, 2 * hidden_units :], (0, 2, 1))
    w_out_grad = jnp.transpose(out_done[:, :features])

    arrived, w_rows, w_rows_other, prev_both, output, w_gu_grad, w_down_grad, w_out_grad, small = (
        lax.optimization_barrier(
            (arrived, w_rows, w_rows_other, prev_both, output, w_gu_grad, w_down_grad, w_out_grad, small)
        )
    )
    arrived_own, arrived_other = of_heads(arrived)
    back_own, back_other = arrived_own[:, : 3 * HD], arrived_other[:, : 3 * HD]
    part_own, part_other = arrived_own[:, 3 * HD :, : 3 * HD], arrived_other[:, 3 * HD :, : 3 * HD]
    head_sum = part_own.astype(f32) + swap(part_other, "t").astype(f32)
    w_qkv_grad = jnp.transpose(head_sum.reshape(heads, slab, 3, HD), (2, 1, 0, 3)).reshape(3, slab, features)
    d_first = (lax.axis_index("s") * SPAN + place) * slab
    w_slab = lax.dynamic_slice_in_dim(w_qkv, d_first, slab, 1).astype(f32)
    gain_part = jnp.sum(w_slab * w_qkv_grad, axis=(0, 2))
    attn_gain_grad = (gain_part + swap(gain_part, "t")) / lax.dynamic_slice_in_dim(attn_gain, d_first, slab, 0)

    grad_own, grad_other = (v.reshape(3 * features, half) for v in (back_own, back_other))
    attn_grad = dotf(grad_own, w_rows, 0, 0) + dotf(grad_other, w_rows_other, 0, 0)
    inverse_attn = lax.rsqrt(jnp.mean(inputs * inputs, axis=-1, keepdims=True) + EPSILON)
    token_norm_grad, _ = norm_backward(inputs, inverse_attn, attn_gain, attn_grad)
    tokens_grad = both_halves(residual_grad + token_norm_grad)
    return (
        output,
        tokens_grad,
        prev_both,
        attn_gain_grad,
        w_qkv_grad,
        w_out_grad,
        small[:, 0],
        small[:, 1 : 1 + E_ALL],
        small[:, 9 : 9 + 2 * NCONST],
        jnp.transpose(small[:, 13 : 13 + NCONST]),
        w_gu_grad,
        w_down_grad,
    )


def solution(mesh):
    dp = mesh.shape["dp"]
    devices = mesh.devices.reshape(dp // SPAN, 4, 2, 2, mesh.shape["tensor"])
    inner = Mesh(devices, ("s", "z", "y", "x", "t"))
    d = ("s", "z", "y", "x")
    return jax.shard_map(
        local,
        mesh=inner,
        in_specs=(
            P(d, None),
            P(d),
            P(d, None),
            P(d, None),
            P(),
            P(None, None, "t"),
            P("t", None),
            P(),
            P(),
            P(),
            P(),
            P(None, None, None, "t"),
            P(None, "t", None),
            P(d, None),
        ),
        out_specs=(
            P(d, None),
            P(d, None),
            P(d, None),
            P(d),
            P(None, d, "t"),
            P("t", d),
            P(d),
            P(d, None),
            P(d, None),
            P(None, d),
            P(None, None, d, "t"),
            P(None, "t", d),
        ),
        check_vma=False,
    )
```

```python
import functools
import math

import jax
import jax.numpy as jnp
import numpy as np
from jax import lax
from jax.experimental import pallas as pl
from jax.experimental.pallas import tpu as pltpu
from jax.sharding import Mesh
from jax.sharding import PartitionSpec as P

f32 = jnp.float32
bf = jnp.bfloat16
E_FFN = 4
NCONST = 2
E_ALL = 8
SPAN = 16
SEQ_LEN = 8192
EPSILON = 1e-05
HIGHEST = lax.Precision.HIGHEST
GROUP = ("z", "y", "x")
GATE_ROWS = 16


HD = 64
NEG = -1e30
WIDE = (4, 2, 1)


def dotf(a, b, ca, cb):
    return lax.dot_general(a, b, (((ca,), (cb,)), ((), ())), preferred_element_type=f32)


def key_places(t, blocks, half):
    r = lax.broadcasted_iota(jnp.int32, (blocks * 2 * half, half), 0)
    inside = r % (2 * half)
    return r - inside + jnp.where(inside < half, t * half + inside, (1 - t) * half + inside - half)


def fwd_kernel(nb, half, sc, start_ref, own_ref, oth_ref, o_ref, of_ref, lse_ref, ktm, vt):
    keys = 2 * half
    t = sc[0]

    def prep(j, _):
        at = pl.ds(pl.multiple_of(j * keys, keys), half)
        more = pl.ds(pl.multiple_of(j * keys + half, half), half)
        ktm[at, :] = own_ref[j, HD : 2 * HD, :].T
        ktm[more, :] = oth_ref[j, 0:HD, :].T
        vt[:, at] = own_ref[j, 2 * HD : 3 * HD, :]
        vt[:, more] = oth_ref[j, HD : 2 * HD, :]
        return 0

    lax.fori_loop(0, nb, prep, 0)
    lane = lax.broadcasted_iota(jnp.int32, (1, half), 1)

    def qblock(s, _):
        q = own_ref[s, 0:HD, :] * bf(0.125)
        start_row = start_ref[s]
        last_row = s * keys + t * half + lane
        lo, ml = sc[1 + s], jnp.minimum(sc[1 + nb + s], s)

        def scores(j, n):
            return dotf(ktm[pl.ds(pl.multiple_of(j * keys, keys), n * keys), :], q, 1, 0)

        def allowed(j, n):
            place = key_places(t, n, half) + j * keys
            return (place >= start_row) & (place <= last_row)

        def values(j, n):
            return vt[:, pl.ds(pl.multiple_of(j * keys, keys), n * keys)]

        def emit(o, lse):
            o_ref[s] = o.astype(bf)
            of_ref[s] = o
            lse_ref[s] = lse

        def plain(j, n, c, masked):
            l, acc = c
            p = jnp.exp(scores(j, n))
            if masked:
                p = jnp.where(allowed(j, n), p, 0.0)
            return l + jnp.sum(p, axis=0, keepdims=True), acc + dotf(values(j, n), p.astype(bf), 1, 0)

        c = (jnp.zeros((1, half), f32), jnp.zeros((HD, half), f32))
        c = plain(s, 1, c, True)
        for masked, first, end in ((True, lo, ml), (False, jnp.maximum(lo, ml), s)):
            for n in WIDE:
                count = jnp.maximum(end - first, 0) // n
                c = lax.fori_loop(0, count, lambda i, c: plain(first + i * n, n, c, masked), c)
                first = first + count * n
        l, acc = c
        emit(acc / l, jnp.log(l))
        fine = (jnp.min(l) > 1e-25) & (jnp.max(l) < 1e25)

        @pl.when(jnp.logical_not(fine))
        def _():
            def shifted(j, c):
                m, l, acc = c
                sco = jnp.where(allowed(j, 1), scores(j, 1), NEG)
                mn = jnp.maximum(m, jnp.max(sco, axis=0, keepdims=True))
                p = jnp.exp(sco - mn)
                al = jnp.exp(m - mn)
                return mn, l * al + jnp.sum(p, axis=0, keepdims=True), acc * al + dotf(values(j, 1), p.astype(bf), 1, 0)

            c = (jnp.full((1, half), NEG, f32), jnp.zeros((1, half), f32), jnp.zeros((HD, half), f32))
            c = shifted(s, c)
            m, l, acc = lax.fori_loop(lo, s, shifted, c)
            emit(acc / l, m + jnp.log(l))

        return 0

    lax.fori_loop(0, nb, qblock, 0)


def flash_fwd(sc, start, own, oth):
    nb, _, half = own.shape
    v = pl.BlockSpec(memory_space=pltpu.VMEM)
    return pl.pallas_call(
        functools.partial(fwd_kernel, nb, half),
        out_shape=(
            jax.ShapeDtypeStruct((nb, HD, half), bf),
            jax.ShapeDtypeStruct((nb, HD, half), f32),
            jax.ShapeDtypeStruct((nb, 1, half), f32),
        ),
        in_specs=[pl.BlockSpec(memory_space=pltpu.SMEM), v, v, v],
        out_specs=(v, v, v),
        scratch_shapes=[pltpu.VMEM((nb * 2 * half, HD), bf), pltpu.VMEM((HD, nb * 2 * half), bf)],
        compiler_params=pltpu.CompilerParams(vmem_limit_bytes=48 << 20),
        cost_estimate=pl.CostEstimate(flops=10**9, bytes_accessed=4 << 20, transcendentals=10**6),
        name="flash_fwd",
    )(sc, start, own, oth)


def bwd_kernel(
    nb, half, j0, j1, sc, start_ref, own_ref, oth_ref, do_ref, of_ref, lse_ref,
    dq_ref, dko_ref, dkx_ref, ktm, vtm, kt, qt, dot, dq_acc, dotm, qtm, stats,
):
    keys = 2 * half
    t = sc[0]

    def prep(j, _):
        k = j - j0
        ktm[k, 0:half, :] = own_ref[j, HD : 2 * HD, :].T
        ktm[k, half:keys, :] = oth_ref[j, 0:HD, :].T
        vtm[k, 0:half, :] = own_ref[j, 2 * HD : 3 * HD, :].T
        vtm[k, half:keys, :] = oth_ref[j, HD : 2 * HD, :].T
        kt[k, :, 0:half] = own_ref[j, HD : 2 * HD, :]
        kt[k, :, half:keys] = oth_ref[j, 0:HD, :]
        return 0

    lax.fori_loop(j0, j1, prep, 0)

    def prep_q(s, _):
        at = pl.ds(pl.multiple_of(s * half, half), half)
        q = own_ref[s, 0:HD, :] * bf(0.125)
        qt[:, at] = q
        qtm[at, :] = q.T
        dot[:, at] = do_ref[s]
        dotm[at, :] = do_ref[s].T
        dq_acc[:, at] = jnp.zeros((HD, half), f32)
        stats[0:1, at] = lse_ref[s]
        stats[1:2, at] = jnp.sum(do_ref[s].astype(f32) * of_ref[s], axis=0, keepdims=True)
        return 0

    lax.fori_loop(j0, nb, prep_q, 0)
    lane = lax.broadcasted_iota(jnp.int32, (1, half), 1)

    def kblock(j, _):
        k = j - j0
        kj, vj, ktj = ktm[k], vtm[k], kt[k]

        def tile(s, n, c, masked):
            dk, dv = c
            at = pl.ds(pl.multiple_of(s * half, half), n * half)
            sco = dotf(kj, qt[:, at], 1, 0)
            if masked:
                place = key_places(t, 1, half) + j * keys
                last_row = s * keys + t * half + lane
                sco = jnp.where((place >= start_ref[s]) & (place <= last_row), sco, NEG)
            p = jnp.exp(sco - stats[0:1, at])
            dp = dotf(vj, dot[:, at], 1, 0)
            ds = (p * (dp - stats[1:2, at])).astype(bf)
            dv = dv + dotf(p.astype(bf), dotm[at, :], 1, 0)
            dk = dk + dotf(ds, qtm[at, :], 1, 0)
            dq_acc[:, at] += dotf(ktj, ds, 1, 0)
            return dk, dv

        c = (jnp.zeros((keys, HD), f32), jnp.zeros((keys, HD), f32))
        c = tile(j, 1, c, True)
        mid, hi = sc[1 + 2 * nb + j], sc[1 + 3 * nb + j]
        first = j + 1
        for n in WIDE:
            count = jnp.maximum(mid - first, 0) // n
            c = lax.fori_loop(0, count, lambda i, c: tile(first + i * n, n, c, False), c)
            first = first + count * n
        dk, dv = lax.fori_loop(jnp.maximum(j + 1, mid), hi, lambda s, c: tile(s, 1, c, True), c)
        dk = dk.T
        dv = dv.T
        dko_ref[k, 0:HD, :] = dk[:, 0:half]
        dko_ref[k, HD : 2 * HD, :] = dv[:, 0:half]
        dkx_ref[k, 0:HD, :] = dk[:, half:keys].astype(bf)
        dkx_ref[k, HD : 2 * HD, :] = dv[:, half:keys].astype(bf)
        return 0

    lax.fori_loop(j0, j1, kblock, 0)

    def finish(s, _):
        at = pl.ds(pl.multiple_of(s * half, half), half)
        dq_ref[s] = (dq_acc[:, at] * 0.125).astype(bf)
        return 0

    def nothing(s, _):
        dq_ref[s] = jnp.zeros((HD, half), bf)
        return 0

    lax.fori_loop(0, j0, nothing, 0)
    lax.fori_loop(j0, nb, finish, 0)


def flash_bwd(sc, start, own, oth, do, of, lse, j0=0, j1=SPAN):
    nb, _, half = own.shape
    v = pl.BlockSpec(memory_space=pltpu.VMEM)
    n = j1 - j0
    return pl.pallas_call(
        functools.partial(bwd_kernel, nb, half, j0, j1),
        out_shape=(
            jax.ShapeDtypeStruct((nb, HD, half), bf),
            jax.ShapeDtypeStruct((n, 2 * HD, half), f32),
            jax.ShapeDtypeStruct((n, 2 * HD, half), bf),
        ),
        in_specs=[pl.BlockSpec(memory_space=pltpu.SMEM)] + [v] * 6,
        out_specs=(v, v, v),
        scratch_shapes=[
            pltpu.VMEM((n, 2 * half, HD), bf),
            pltpu.VMEM((n, 2 * half, HD), bf),
            pltpu.VMEM((n, HD, 2 * half), bf),
            pltpu.VMEM((HD, nb * half), bf),
            pltpu.VMEM((HD, nb * half), bf),
            pltpu.VMEM((HD, nb * half), f32),
            pltpu.VMEM((nb * half, HD), bf),
            pltpu.VMEM((nb * half, HD), bf),
            pltpu.VMEM((8, nb * half), f32),
        ],
        compiler_params=pltpu.CompilerParams(vmem_limit_bytes=56 << 20),
        cost_estimate=pl.CostEstimate(flops=10**9, bytes_accessed=4 << 20, transcendentals=10**6),
        name="flash_bwd",
    )(sc, start, own, oth, do, of, lse)


def bounds(start_all, t, nb, HB):
    st=start_all.reshape(nb,2,HB)
    mine=lax.dynamic_index_in_dim(st,t,1,keepdims=False)
    first=mine[:,0]; last=mine[:,HB-1]
    B=2*HB
    lo=first//B
    ml=(last+B-1)//B
    j=jnp.arange(nb)
    mid=jnp.sum((last[None,:]<=j[:,None]*B).astype(jnp.int32),axis=1)
    hi=jnp.sum((lo[None,:]<=j[:,None]).astype(jnp.int32),axis=1)
    mid=jnp.minimum(mid,hi)
    sc=jnp.concatenate([jnp.full((1,),t,jnp.int32),lo,ml,mid,hi]).astype(jnp.int32)
    return sc,mine[:,None,:]


def ffn_kernel(e_ref, u_ref, wgu_ref, wd_ref, *refs):
    pieces = refs[:8]
    x_out_ref, g_ref, wh_ref, mine_ref, other_ref, out_mine_ref, out_other_ref, held = refs[8:]
    half = u_ref.shape[1]
    width = x_out_ref.shape[2]
    hidden_units = wgu_ref.shape[3]
    e = e_ref[0]
    step = pl.program_id(0)
    for k in range(8):

        @pl.when(step == k)
        def _(k=k):
            held[...] = pieces[k][...]

    gates = held[half : half + GATE_ROWS, 0:half].astype(f32)
    row = lax.broadcasted_iota(jnp.int32, gates.shape, 0)
    gate_row = jnp.sum(jnp.where((row == e) | (row == e + E_FFN), gates, 0.0), axis=0, keepdims=True)
    gate = jnp.broadcast_to(gate_row, (8, half)).T[:, 0:1]
    x = held[0:half, :]
    x_out_ref[0] = x
    chunk = 256
    dots = jnp.zeros((8, half), f32)
    ones = jnp.ones((8, chunk), bf)
    for first in range(0, hidden_units, chunk):
        cols = slice(first, first + chunk)
        g = dotf(x, wgu_ref[0, 0, :, cols], 1, 0)
        up = dotf(x, wgu_ref[0, 1, :, cols], 1, 0)
        raw = u_ref[0, :, cols].astype(f32)
        sig = 0.5 * jnp.tanh(0.5 * g) + 0.5
        silu = g * sig
        hid = silu * up
        hg = gate * raw
        g_ref[0, :, cols] = (hg * up * (sig + silu * (1.0 - sig))).astype(bf)
        g_ref[0, :, slice(hidden_units + first, hidden_units + first + chunk)] = (hg * silu).astype(bf)
        wh_ref[0, :, cols] = (gate * hid).astype(bf)
        dots = dots + dotf(ones, (hid * raw).astype(bf), 1, 1)
    total = dotf(g_ref[0, :, 0:hidden_units], wgu_ref[0, 0], 1, 1)
    total = total + dotf(g_ref[0, :, hidden_units : 2 * hidden_units], wgu_ref[0, 1], 1, 1)
    result = dotf(wh_ref[0], wd_ref[0], 1, 0)
    drow = lax.broadcasted_iota(jnp.int32, (GATE_ROWS, half), 0)
    placed = jnp.where(drow == e, jnp.broadcast_to(dots[0:1, :], (GATE_ROWS, half)), 0.0).astype(bf)

    def put(ref):
        ref[0, 0:half, :] = total.astype(bf)
        ref[0, half : half + GATE_ROWS, :] = jnp.zeros((GATE_ROWS, width), bf)
        ref[0, half : half + GATE_ROWS, 0:half] = placed

    @pl.when(step < 4)
    def _():
        put(mine_ref)
        out_mine_ref[0] = result.astype(bf)

    @pl.when(step >= 4)
    def _():
        put(other_ref)
        out_other_ref[0] = result.astype(bf)


def expert_pass(e, pieces, raw_all, wgu, wdown):
    rows, width = pieces[0].shape
    half = rows - GATE_ROWS
    hidden_units = wgu.shape[3]
    flops = 8 * half * width * hidden_units * 2 * 4
    return pl.pallas_call(
        ffn_kernel,
        out_shape=(
            jax.ShapeDtypeStruct((8, half, width), bf),
            jax.ShapeDtypeStruct((8, half, 2 * hidden_units), bf),
            jax.ShapeDtypeStruct((8, half, hidden_units), bf),
            jax.ShapeDtypeStruct((4, rows, width), bf),
            jax.ShapeDtypeStruct((4, rows, width), bf),
            jax.ShapeDtypeStruct((4, half, width), bf),
            jax.ShapeDtypeStruct((4, half, width), bf),
        ),
        grid_spec=pltpu.PrefetchScalarGridSpec(
            num_scalar_prefetch=1,
            grid=(8,),
            in_specs=[
                pl.BlockSpec((1, half, hidden_units), lambda i, e: (i, 0, 0)),
                pl.BlockSpec((1, 2, width, hidden_units), lambda i, e: (e[0], 0, 0, 0)),
                pl.BlockSpec((1, hidden_units, width), lambda i, e: (e[0], 0, 0)),
            ]
            + [pl.BlockSpec((rows, width), lambda i, e: (0, 0))] * 8,
            out_specs=(
                pl.BlockSpec((1, half, width), lambda i, e: (i, 0, 0)),
                pl.BlockSpec((1, half, 2 * hidden_units), lambda i, e: (i, 0, 0)),
                pl.BlockSpec((1, half, hidden_units), lambda i, e: (i, 0, 0)),
                pl.BlockSpec((1, rows, width), lambda i, e: (jnp.minimum(i, 3), 0, 0)),
                pl.BlockSpec((1, rows, width), lambda i, e: (jnp.maximum(i - 4, 0), 0, 0)),
                pl.BlockSpec((1, half, width), lambda i, e: (jnp.minimum(i, 3), 0, 0)),
                pl.BlockSpec((1, half, width), lambda i, e: (jnp.maximum(i - 4, 0), 0, 0)),
            ),
            scratch_shapes=[pltpu.VMEM((rows, width), bf)],
        ),
        compiler_params=pltpu.CompilerParams(vmem_limit_bytes=48 << 20),
        cost_estimate=pl.CostEstimate(flops=flops, bytes_accessed=40 << 20, transcendentals=2 << 20),
        name="expert_pass",
    )(e, raw_all, wgu, wdown, *pieces)


def hidden_cotangent_kernel(at_ref, w_ref, rows_ref, up_ref, raw_ref):
    rows = rows_ref[0]
    up_ref[0] = rows
    raw_ref[0] = dotf(rows, w_ref[0], 1, 1).astype(bf)


def hidden_cotangent(at, rows, w_down):
    pieces, half, width = rows.shape
    hidden_units = w_down.shape[1]
    return pl.pallas_call(
        hidden_cotangent_kernel,
        out_shape=(
            jax.ShapeDtypeStruct((pieces, half, width), bf),
            jax.ShapeDtypeStruct((pieces, half, hidden_units), bf),
        ),
        grid_spec=pltpu.PrefetchScalarGridSpec(
            num_scalar_prefetch=1,
            grid=(pieces,),
            in_specs=[
                pl.BlockSpec((1, hidden_units, width), lambda i, at: (at[0], 0, 0)),
                pl.BlockSpec((1, half, width), lambda i, at: (at[1 + i], 0, 0)),
            ],
            out_specs=(
                pl.BlockSpec((1, half, width), lambda i, at: (i, 0, 0)),
                pl.BlockSpec((1, half, hidden_units), lambda i, at: (i, 0, 0)),
            ),
        ),
        compiler_params=pltpu.CompilerParams(vmem_limit_bytes=40 << 20),
        cost_estimate=pl.CostEstimate(flops=32 * 10**8, bytes_accessed=12 << 20, transcendentals=0),
        name="hidden_cotangent",
    )(at, w_down, rows)


def exact(a, b, ca, cb):
    return lax.dot_general(a, b, (((ca,), (cb,)), ((), ())), precision=HIGHEST, preferred_element_type=f32)


def back_rows_kernel(
    first_ref, p0, p1, p2, p3, residual_ref, up_ref, gain_ref, rows_ref, small_ref, const_ref, own_ref, other_ref,
    grad_ref, low_ref, cot_ref, logit_ref, gain_out_ref,
):
    half, width = residual_ref.shape
    dx = p0[...].astype(f32) + p1[...].astype(f32) + p2[...].astype(f32) + p3[...].astype(f32)
    gating = dx[half : half + E_ALL, 0:half]
    dx = dx[0:half]
    residual, gain = residual_ref[...], gain_ref[...]
    up = up_ref[...].astype(f32)
    inverse = lax.rsqrt(jnp.mean(residual * residual, axis=-1, keepdims=True) + EPSILON)
    probs, hot = rows_ref[0:8], rows_ref[8:16]
    blend_one, blend_two, const_weight = rows_ref[16:18], rows_ref[18:20], rows_ref[20:22]
    kept = rows_ref[22:23]
    copy_dot = exact(jnp.ones((8, width), f32), up * (residual * inverse * gain), 1, 1)[0:1]
    vector_dot = exact(const_ref[...], up, 1, 1)[0:NCONST]
    const_dot = blend_one * copy_dot + blend_two * vector_dot
    row = lax.broadcasted_iota(jnp.int32, (8, half), 0)
    dots = jnp.where(row < E_FFN, gating, 0.0)
    dots = jnp.where(row == E_FFN + 1, copy_dot, dots)
    for c in range(NCONST):
        dots = jnp.where(row == E_FFN + 2 + c, const_dot[c : c + 1], dots)
    probs_grad = dots * hot
    logit_ref[0:8] = probs * (probs_grad - jnp.sum(probs * probs_grad, axis=0, keepdims=True))
    grad_one = const_weight * copy_dot
    grad_two = const_weight * vector_dot
    inner = blend_one * grad_one + blend_two * grad_two
    grad_one = blend_one * (grad_one - inner)
    grad_two = blend_two * (grad_two - inner)
    const_grad = jnp.zeros((8, half), f32)
    for c in range(NCONST):
        const_grad = jnp.where(row == 2 * c, grad_one[c : c + 1], const_grad)
        const_grad = jnp.where(row == 2 * c + 1, grad_two[c : c + 1], const_grad)
    logit_ref[8:16] = const_grad
    kept_column = jnp.broadcast_to(kept, (8, half)).T[:, 0:1]
    normed_grad = dx + exact(logit_ref[...], small_ref[...], 0, 0) + kept_column * up
    gain_out_ref[...] = jnp.sum(normed_grad * residual * inverse, axis=0, keepdims=True)
    scaled = normed_grad * gain
    mean = jnp.mean(scaled * residual, axis=-1, keepdims=True)
    grad = up + inverse * scaled - residual * (inverse * inverse * inverse * mean)
    grad_ref[...] = grad
    low = grad.astype(bf)
    low_ref[...] = low
    heads = own_ref.shape[0] // HD
    cot_ref[...] = jnp.zeros(cot_ref.shape, bf)
    for n, ref in enumerate((own_ref, other_ref)):
        rows = dotf(ref[...], low, 1, 1).astype(bf)
        for h in range(heads):
            cot_ref[first_ref[n] + h] = rows[h * HD : (h + 1) * HD]


def back_rows(first, parts, residual, up, gain, rows, small, const, own, other):
    half, width = residual.shape
    v = pl.BlockSpec(memory_space=pltpu.VMEM)
    return pl.pallas_call(
        back_rows_kernel,
        out_shape=(
            jax.ShapeDtypeStruct((half, width), f32),
            jax.ShapeDtypeStruct((half, width), bf),
            jax.ShapeDtypeStruct((SPAN, HD, half), bf),
            jax.ShapeDtypeStruct((16, half), f32),
            jax.ShapeDtypeStruct((1, width), f32),
        ),
        in_specs=[pl.BlockSpec(memory_space=pltpu.SMEM)] + [v] * 12,
        out_specs=(v,) * 5,
        compiler_params=pltpu.CompilerParams(vmem_limit_bytes=40 << 20),
        cost_estimate=pl.CostEstimate(flops=4 * 10**8, bytes_accessed=5 << 20, transcendentals=0),
        name="back_rows",
    )(first, *parts, residual, up, gain.reshape(1, width), rows, small, const, own, other)


def token_rows_kernel(first_ref, arrived_ref, own_ref, other_ref, grad_ref, x_ref, gain_ref, out_ref, rows):
    per_head = 3 * HD
    heads = own_ref.shape[0] // per_head
    upstream = jnp.zeros(out_ref.shape, f32)
    for n, ref in enumerate((own_ref, other_ref)):
        for h in range(heads):
            rows[h * per_head : (h + 1) * per_head, :] = arrived_ref[first_ref[n] + h, 0:per_head, :]
        upstream = upstream + dotf(rows[...], ref[...], 0, 0)
    x = x_ref[...].astype(f32)
    inverse = lax.rsqrt(jnp.mean(x * x, axis=-1, keepdims=True) + EPSILON)
    scaled = upstream * gain_ref[...]
    mean = jnp.mean(scaled * x, axis=-1, keepdims=True)
    out_ref[...] = grad_ref[...] + inverse * scaled - x * (inverse * inverse * inverse * mean)


def token_rows(first, arrived, own, other, grad, x, gain):
    half, width = x.shape
    v = pl.BlockSpec(memory_space=pltpu.VMEM)
    return pl.pallas_call(
        token_rows_kernel,
        out_shape=jax.ShapeDtypeStruct((half, width), f32),
        in_specs=[pl.BlockSpec(memory_space=pltpu.SMEM)] + [v] * 6,
        out_specs=v,
        scratch_shapes=[pltpu.VMEM((own.shape[0], half), bf)],
        compiler_params=pltpu.CompilerParams(vmem_limit_bytes=60 << 20),
        cost_estimate=pl.CostEstimate(flops=10**9, bytes_accessed=6 << 20, transcendentals=0),
        name="token_rows",
    )(first, arrived, own, other, grad, x, gain.reshape(1, width))


def heads_kernel(first_ref, x_ref, gain_ref, w_ref, cos_ref, sin_ref, *refs):
    buffer_ref, normed_ref = refs[-2:]
    x = x_ref[...].astype(f32)
    inverse = lax.rsqrt(jnp.mean(x * x, axis=-1, keepdims=True) + EPSILON)
    normed = (x * inverse * gain_ref[...]).astype(bf)
    normed_ref[...] = normed
    cosine, sine = cos_ref[...], sin_ref[...]
    heads = w_ref.shape[2] // HD
    first = first_ref[0]
    buffer_ref[...] = refs[0][...] if len(refs) == 3 else jnp.zeros(buffer_ref.shape, bf)
    for s in range(3):
        rows = dotf(normed, w_ref[s], 1, 0).T
        for h in range(heads):
            part = rows[h * HD : (h + 1) * HD]
            if s < 2:
                one, two = part[: HD // 2], part[HD // 2 :]
                part = jnp.concatenate([one * cosine - two * sine, two * cosine + one * sine], axis=0)
            buffer_ref[first + h, s * HD : (s + 1) * HD, :] = part.astype(bf)


def head_rows(first, x, gain, w, cosine, sine, buffer=None):
    half, width = x.shape
    v = pl.BlockSpec(memory_space=pltpu.VMEM)
    given = [] if buffer is None else [buffer]
    return pl.pallas_call(
        heads_kernel,
        out_shape=(
            jax.ShapeDtypeStruct((SPAN, 3 * HD, half), bf),
            jax.ShapeDtypeStruct((half, width), bf),
        ),
        in_specs=[pl.BlockSpec(memory_space=pltpu.SMEM)] + [v] * 5 + [v] * len(given),
        out_specs=(v, v),
        compiler_params=pltpu.CompilerParams(vmem_limit_bytes=40 << 20),
        cost_estimate=pl.CostEstimate(flops=5 * 10**8, bytes_accessed=4 << 20, transcendentals=0),
        name="head_rows",
    )(first, x, gain.reshape(1, width), w, cosine, sine, *given)


def head_grad_kernel(at_ref, dq_ref, own_ref, other_ref, cos_ref, sin_ref, *refs):
    pieces, out_ref, turned_rows = refs[:-2], refs[-2], refs[-1]
    half, width = pieces[0].shape[-2:]
    blocks = out_ref.shape[0]

    def back(rows, block):
        one, two = rows[: HD // 2], rows[HD // 2 :]
        cosine, sine = cos_ref[block], sin_ref[block]
        return jnp.concatenate([one * cosine + two * sine, two * cosine - one * sine], axis=0)

    acc = jnp.zeros((3 * HD, width), f32)
    n = 0
    for ref in pieces:
        places = list(np.ndindex(*ref.shape[:-2]))
        for k in range(len(places)):
            block = at_ref[n]
            dkv = own_ref[block] + other_ref[block].astype(f32)
            rows = jnp.concatenate(
                [back(dq_ref[block].astype(f32), block), back(dkv[:HD], block), dkv[HD:]], axis=0
            ).astype(bf)
            out_ref[block, 0 : 3 * HD, :] = rows
            turned_rows[:, k * half : (k + 1) * half] = rows
            n += 1
        count = len(places) * half
        acc = acc + dotf(turned_rows[:, 0:count], ref[...].reshape(count, width), 1, 0)
    turned = acc.T.astype(bf)
    rows = turned.shape[0] // blocks
    for block in range(blocks):
        out_ref[block, 3 * HD :, :] = jnp.zeros((rows, out_ref.shape[2]), bf)
        out_ref[block, 3 * HD :, 0 : 3 * HD] = turned[block * rows : (block + 1) * rows]


def head_grad(at, dq, own, other, cosine, sine, pieces):
    v = pl.BlockSpec(memory_space=pltpu.VMEM)
    half, width = pieces[0].shape[-2:]
    blocks = dq.shape[0]
    return pl.pallas_call(
        head_grad_kernel,
        out_shape=jax.ShapeDtypeStruct((blocks, 3 * HD + width // blocks, half), bf),
        in_specs=[pl.BlockSpec(memory_space=pltpu.SMEM)] + [v] * (5 + len(pieces)),
        out_specs=v,
        scratch_shapes=[pltpu.VMEM((3 * HD, 4 * half), bf)],
        compiler_params=pltpu.CompilerParams(vmem_limit_bytes=48 << 20),
        cost_estimate=pl.CostEstimate(flops=12 * 10**8, bytes_accessed=12 << 20, transcendentals=0),
        name="head_grad",
    )(at, dq, own, other, cosine, sine, *pieces)


def swap(value, axis):
    return lax.ppermute(value, axis, [(0, 1), (1, 0)])


def plane_diagonal(value):
    return lax.ppermute(value, ("y", "x"), [(i, 3 - i) for i in range(4)])


def plane_gather(piece):
    mine = [piece, swap(piece, "x"), swap(piece, "y"), plane_diagonal(piece)]
    return mine + [swap(p, "t") for p in mine]


def plane_scatter(mine, other, later):
    held = [(mine[k].astype(f32) + other[k].astype(f32)).astype(bf) for k in range(4)]
    held, later = lax.optimization_barrier((held, later))
    return [held[0], swap(held[1], "x"), swap(held[2], "y"), plane_diagonal(held[3])], later


def over_z(value, distance):
    return lax.ppermute(value, "z", [(i, i ^ distance) for i in range(4)])


def total(parts):
    first, rest = parts
    return first.astype(f32) + sum(p.astype(f32) for p in rest)


def plane_rows(chunks):
    b = lax.axis_index(("y", "x"))
    pick = lambda d: lax.dynamic_index_in_dim(chunks, b ^ d, 0, keepdims=False)
    return pick(0), [swap(pick(1), "x"), swap(pick(2), "y"), plane_diagonal(pick(3))]


def after(value, *others):
    return lax.optimization_barrier((value, others))[0]


def over_sequences(rows):
    if lax.axis_size("s") == 1:
        return rows
    return lax.psum_scatter(rows, "s", scatter_dimension=0, tiled=True)


def first_tokens(segments):
    def gathered(value, moved, places):
        low, high = places
        first = jnp.where(low == 0, jnp.stack([value, moved[0]]), jnp.stack([moved[0], value]))
        second = jnp.where(low == 0, jnp.stack([moved[1], moved[2]]), jnp.stack([moved[2], moved[1]]))
        return jnp.where(high == 0, jnp.stack([first, second]), jnp.stack([second, first]))

    z = lax.axis_index("z")
    plane = [swap(segments, "x"), swap(segments, "y"), plane_diagonal(segments)]
    ids = gathered(segments, plane, (lax.axis_index("x"), lax.axis_index("y"))).reshape(-1)
    ids = gathered(ids, [over_z(ids, d) for d in (1, 2, 3)], (z % 2, z // 2)).reshape(-1)
    count = ids.shape[0]
    index = jnp.arange(count, dtype=jnp.int32)
    before = jnp.concatenate([ids[:1], ids[:-1]])
    opens = jnp.where(ids != before, index, 0).reshape(-1, 256)
    n = opens.shape[0]
    lane = jnp.arange(256, dtype=jnp.int32)
    within = jnp.max(jnp.where(lane[None, None, :] <= lane[None, :, None], opens[:, None, :], 0), axis=-1)
    block = jnp.arange(n, dtype=jnp.int32)
    top = jnp.max(opens, axis=1)
    carry = jnp.max(jnp.where(block[None, :] < block[:, None], top[None, :], 0), axis=1)
    return jnp.maximum(within, carry[:, None]).reshape(-1)


def rotary_tables(position, half_dim):
    inv_freq = jnp.exp(jnp.arange(half_dim).astype(f32) * (-math.log(10000.0) / half_dim))
    phases = inv_freq[:, None] * position.astype(f32)[None, :]
    return jnp.cos(phases), jnp.sin(phases)


def rotate(values, cosine, sine):
    half_dim = values.shape[-2] // 2
    one, two = values[..., :half_dim, :], values[..., half_dim:, :]
    return jnp.concatenate([one * cosine - two * sine, two * cosine + one * sine], axis=-2)


def norm_forward(values, gain):
    inverse = lax.rsqrt(jnp.mean(values * values, axis=-1, keepdims=True) + EPSILON)
    return values * inverse * gain, inverse


def norm_backward(values, inverse, gain, upstream):
    scaled = upstream * gain
    inner = jnp.mean(scaled * values, axis=-1, keepdims=True)
    return (
        inverse * scaled - values * inverse * inverse * inverse * inner,
        jnp.sum(upstream * values * inverse, axis=0),
    )


def local(
    tokens,
    segments,
    routes,
    prev_logits,
    attn_gain,
    w_qkv,
    w_out,
    ffn_gain,
    w_router,
    w_const,
    v_const,
    w_gu,
    w_down,
    cotangent,
):
    tok_count, width = tokens.shape
    half = tok_count // 2
    features = w_qkv.shape[2]
    heads = features // HD
    t = lax.axis_index("t")
    place = lax.axis_index(GROUP)
    expert = lax.axis_index(("y", "x"))

    def mine(value):
        return lax.dynamic_slice_in_dim(value, t * half, half, 0)

    def both_halves(value):
        other = swap(value, "t")
        whole = jnp.zeros((tok_count,) + value.shape[1:], value.dtype)
        whole = lax.dynamic_update_slice_in_dim(whole, value, t * half, 0)
        return lax.dynamic_update_slice_in_dim(whole, other, (1 - t) * half, 0)

    w_qkv_other = swap(w_qkv, "t")
    w_out_other = swap(w_out, "t")
    inputs = mine(tokens).astype(f32)
    upstream_low = mine(cotangent)
    upstream = upstream_low.astype(f32)
    my_routes = jnp.transpose(mine(routes))
    my_prev = jnp.transpose(mine(prev_logits))
    kinds = jnp.arange(E_ALL, dtype=jnp.int32)[:, None]
    hot = (my_routes[0:1] == kinds).astype(f32) + (my_routes[1:2] == kinds).astype(f32)
    position = (place * tok_count + t * half + jnp.arange(half, dtype=jnp.int32)) % SEQ_LEN
    cosine, sine = rotary_tables(position, HD // 2)
    tokens_mine = mine(tokens)
    first = (t * heads).astype(jnp.int32).reshape(1)
    other_first = ((1 - t) * heads).astype(jnp.int32).reshape(1)
    buffer, normed_low = head_rows(first, tokens_mine, attn_gain, w_qkv, cosine, sine)
    buffer, _ = head_rows(other_first, tokens_mine, attn_gain, w_qkv_other, cosine, sine, buffer)

    def of_heads(buffer):
        return (
            lax.dynamic_slice_in_dim(buffer, t * heads, heads, 0),
            lax.dynamic_slice_in_dim(buffer, (1 - t) * heads, heads, 0),
        )

    def exchange(buffer):
        return lax.all_to_all(buffer, GROUP, 0, 0, tiled=True)

    upstream_sent, segments, buffer = lax.optimization_barrier((upstream_low, segments, buffer))
    start_all = first_tokens(segments)
    sc, start_rows = bounds(start_all, t, SPAN, half)
    own = exchange(buffer)
    oth = swap(own[:, HD:], "t")
    up_gathered = lax.all_gather(upstream_sent, ("y", "x", "t"))
    piece_rank = jnp.bitwise_xor(2 * expert + t, jnp.array((0, 2, 4, 6, 1, 3, 5, 7), jnp.int32))
    expert_at = expert.astype(jnp.int32).reshape(1)
    normed_sent, own_q, sc, start_rows = lax.optimization_barrier((normed_low, own, sc, start_rows))
    along_z = [normed_sent] + [over_z(normed_sent, d) for d in (1, 2, 3)]
    heads_rows, heads_full, lse = flash_fwd(sc, start_rows, own_q, oth)
    heads_rows, up_gathered, along_z = lax.optimization_barrier((heads_rows, up_gathered, along_z))
    back = exchange(heads_rows)
    up_all, raw_all = hidden_cotangent(
        jnp.concatenate([expert_at, piece_rank.astype(jnp.int32)]), up_gathered, w_down
    )
    back, raw_all = lax.optimization_barrier((back, raw_all))
    heads_own, heads_other = (v.reshape(features, half) for v in of_heads(back))
    branch = dotf(heads_own, w_out, 0, 0) + dotf(heads_other, w_out_other, 0, 0)
    residual = inputs + branch
    normed_ffn, inverse_ffn = norm_forward(residual, ffn_gain)
    ffn_low = normed_ffn.astype(bf)
    w_small = jnp.concatenate([w_router, w_const], axis=1)
    logits = dotf(w_small, ffn_low, 0, 1)
    router_probs = jax.nn.softmax(logits[:E_ALL] + my_prev, axis=0)
    expert_weight = router_probs * hot
    gate_rows = expert_weight[:E_FFN]
    gate_high = gate_rows.astype(bf)
    gate_low = (gate_rows - gate_high.astype(f32)).astype(bf)
    gate_block = jnp.pad(
        jnp.concatenate([gate_high, gate_low]), ((0, GATE_ROWS - 2 * E_FFN), (0, width - half))
    )
    x_all = plane_gather(jnp.concatenate([ffn_low, gate_block]))

    def feature_rows(w):
        return jnp.transpose(w.reshape(3, width, heads, HD), (2, 0, 3, 1)).reshape(3 * features, width)

    w_held, w_other_held, t_late = after((w_qkv, w_qkv_other, t), ffn_low)
    w_rows, w_rows_other = feature_rows(w_held), feature_rows(w_other_held)
    all_position = (jnp.arange(SPAN, dtype=jnp.int32)[:, None] * tok_count + t_late * half)[:, :, None] + jnp.arange(half, dtype=jnp.int32)
    all_cosine, all_sine = rotary_tables(all_position.reshape(-1), HD // 2)
    by_block = lambda table: jnp.transpose(table.reshape(HD // 2, SPAN, half), (1, 0, 2))
    all_cosine, all_sine = by_block(all_cosine), by_block(all_sine)
    pair_a, pair_b = jnp.stack(along_z[:2]), jnp.stack(along_z[2:])
    near = (0, 4, 8, 12, 1, 5, 10, 14, 2, 6, 3, 7, 9, 13, 11, 15)
    at = jnp.bitwise_xor(place, jnp.array(near, jnp.int32)).astype(jnp.int32)
    x_all, w_rows, w_rows_other, all_cosine, all_sine, pair_a, pair_b, at = lax.optimization_barrier(
        (x_all, w_rows, w_rows_other, all_cosine, all_sine, pair_a, pair_b, at)
    )
    pair_ax, pair_by = swap(pair_a, "x"), swap(pair_b, "y")
    x_only, g_all, weighted, dx_mine, dx_other, out_mine, out_beside = expert_pass(
        expert_at, x_all, raw_all, w_gu, w_down
    )
    dx_mine, dx_other, pair_ax, pair_by = lax.optimization_barrier((dx_mine, dx_other, pair_ax, pair_by))
    dx_other = swap(dx_other, "t")
    hidden_units = w_down.shape[1]
    received, (weighted, g_all) = plane_scatter(dx_mine, dx_other, (weighted, g_all))
    down_part = jnp.einsum("ptd,ptf->df", up_all, weighted, preferred_element_type=f32).astype(bf)
    gu_part = jnp.einsum("ptd,ptf->df", x_only, g_all, preferred_element_type=f32).astype(bf)
    expert_part = over_sequences(jnp.concatenate([gu_part, down_part], axis=1))
    slab = expert_part.shape[0] // SPAN
    received, expert_part = lax.optimization_barrier((received, expert_part))
    expert_sum = lax.psum_scatter(expert_part, "z", scatter_dimension=0, tiled=True)

    pairs = logits[E_ALL:].reshape(NCONST, 2, half)
    blend_one = jax.nn.sigmoid(pairs[:, 0] - pairs[:, 1])
    blend_two = jax.nn.sigmoid(pairs[:, 1] - pairs[:, 0])
    const_weight = expert_weight[E_FFN + 2 :]
    kept = expert_weight[E_FFN + 1 : E_FFN + 2] + jnp.sum(const_weight * blend_one, axis=0, keepdims=True)
    added = const_weight * blend_two
    columns = jnp.transpose(jnp.concatenate([kept, added]))
    kept_column, added_columns = columns[:, 0:1], columns[:, 1:]

    pad_rows = lambda v, n: jnp.pad(v, ((0, n - v.shape[0]), (0, 0)))
    row_pack = pad_rows(jnp.concatenate([router_probs, hot, blend_one, blend_two, const_weight, kept]), 24)
    small_rows = pad_rows(jnp.transpose(w_small).astype(f32), 16)
    residual_grad, branch_cot, cot, logit_grad, ffn_gain_part = back_rows(
        jnp.concatenate([first, other_first]),
        received,
        residual,
        upstream_low,
        ffn_gain,
        row_pack,
        small_rows,
        pad_rows(v_const, 8),
        w_out,
        w_out_other,
    )
    logit_grad = logit_grad[: E_ALL + 2 * NCONST]
    prev_grad = logit_grad[:E_ALL]
    out_beside, added = after((out_beside, added), cot)
    small = jnp.concatenate(
        [
            ffn_gain_part,
            jnp.dot(logit_grad, ffn_low.astype(f32), precision=HIGHEST),
            jnp.dot(added, upstream, precision=HIGHEST),
        ]
    )
    small = jnp.transpose(jnp.pad(small, ((0, 128 - small.shape[0]), (0, 0)))).astype(bf)
    out_own = dotf(branch_cot, heads_own, 0, 1).astype(bf)
    out_other = dotf(branch_cot, heads_other, 0, 1).astype(bf)
    out_part = (out_own.astype(f32) + swap(out_other, "t").astype(f32)).astype(bf)
    out_part = over_sequences(jnp.concatenate([out_part, small], axis=1))
    out_z = lax.psum_scatter(out_part, "z", scatter_dimension=0, tiled=True)
    out_beside = swap(out_beside, "t")
    held = [(out_mine[k].astype(f32) + out_beside[k].astype(f32)).astype(bf) for k in range(4)]

    cot = exchange(cot)
    stack_a, stack_b = jnp.stack([pair_a, pair_ax]), jnp.stack([pair_b, pair_by])
    cot, held, out_part, stack_a, stack_b = lax.optimization_barrier((cot, held, out_part, stack_a, stack_b))
    pair_ya, pair_xb = swap(stack_a, "y"), swap(stack_b, "x")
    moved_out = [swap(held[1], "x"), swap(held[2], "y"), plane_diagonal(held[3])]
    dq, dkv_own, dkv_oth = flash_bwd(sc, start_rows, own, oth, cot, heads_full, lse)
    dkv_oth, pair_ya, pair_xb, moved_out = lax.optimization_barrier((dkv_oth, pair_ya, pair_xb, moved_out))
    dkv_oth = swap(dkv_oth, "t")
    sent = head_grad(
        at, dq, dkv_own, dkv_oth, all_cosine, all_sine, [pair_a, pair_b, pair_ax, pair_by, pair_ya, pair_xb]
    )
    if lax.axis_size("s") > 1:
        head_part = over_sequences(sent[:, 3 * HD :, : 3 * HD].reshape(width, 3 * HD))
        head_part = jnp.pad(head_part.reshape(SPAN, slab, 3 * HD), ((0, 0), (0, 0), (0, half - 3 * HD)))
        sent = jnp.concatenate([sent[:, : 3 * HD], head_part], axis=1)
    sent, held, expert_sum, prev_grad = lax.optimization_barrier((sent, held, expert_sum, prev_grad))
    arrived = exchange(sent)
    d_first = (lax.axis_index("s") * SPAN + place) * slab

    prev_both = both_halves(jnp.transpose(prev_grad))
    parts = jnp.concatenate([expert_sum, out_z], axis=1)
    own_rows, got_rows = plane_rows(parts.reshape(4, slab, parts.shape[1]))
    held, moved_out = after((held, moved_out), parts)
    ffn_sum = sum(v.astype(f32) for v in [held[0]] + moved_out)
    mixture = residual + ffn_sum + kept_column * normed_ffn + jnp.dot(added_columns, v_const, precision=HIGHEST)
    output = both_halves(mixture.astype(bf))
    columns_ffn = 3 * hidden_units
    by_distance = jnp.stack([rows[:, :columns_ffn] for rows in [own_rows] + got_rows])
    expert_rows = jnp.stack([lax.dynamic_index_in_dim(by_distance, expert ^ k, 0, keepdims=False) for k in range(4)]).astype(f32)
    out_done = sum(rows[:, columns_ffn:].astype(f32) for rows in [own_rows] + got_rows)
    w_gu_grad = jnp.transpose(
        expert_rows[:, :, : 2 * hidden_units].reshape(E_FFN, slab, 2, hidden_units), (0, 2, 1, 3)
    )
    w_down_grad = jnp.transpose(expert_rows[:, :, 2 * hidden_units :], (0, 2, 1))
    arrived, prev_both, output, w_gu_grad, w_down_grad, out_done = lax.optimization_barrier(
        (arrived, prev_both, output, w_gu_grad, w_down_grad, out_done)
    )
    w_out_grad = jnp.transpose(out_done[:, :features])
    small = out_done[:, features:]
    small = small + swap(small, "t")
    arrived_own, arrived_other = of_heads(arrived)
    part_own, part_other = arrived_own[:, 3 * HD :, : 3 * HD], arrived_other[:, 3 * HD :, : 3 * HD]
    head_sum = part_own.astype(f32) + swap(part_other, "t").astype(f32)
    w_qkv_grad = jnp.transpose(head_sum.reshape(heads, slab, 3, HD), (2, 1, 0, 3)).reshape(3, slab, features)
    w_slab = lax.dynamic_slice_in_dim(w_qkv, d_first, slab, 1).astype(f32)
    gain_part = jnp.sum(w_slab * w_qkv_grad, axis=(0, 2))
    attn_gain_grad = (gain_part + swap(gain_part, "t")) / lax.dynamic_slice_in_dim(attn_gain, d_first, slab, 0)

    tokens_grad = both_halves(
        token_rows(
            jnp.concatenate([first, other_first]), arrived, w_rows, w_rows_other, residual_grad, tokens_mine, attn_gain
        )
    )
    return (
        output,
        tokens_grad,
        prev_both,
        attn_gain_grad,
        w_qkv_grad,
        w_out_grad,
        small[:, 0],
        small[:, 1 : 1 + E_ALL],
        small[:, 9 : 9 + 2 * NCONST],
        jnp.transpose(small[:, 13 : 13 + NCONST]),
        w_gu_grad,
        w_down_grad,
    )


def solution(mesh):
    dp = mesh.shape["dp"]
    devices = mesh.devices.reshape(dp // SPAN, 4, 2, 2, mesh.shape["tensor"])
    inner = Mesh(devices, ("s", "z", "y", "x", "t"))
    d = ("s", "z", "y", "x")
    return jax.shard_map(
        local,
        mesh=inner,
        in_specs=(
            P(d, None),
            P(d),
            P(d, None),
            P(d, None),
            P(),
            P(None, None, "t"),
            P("t", None),
            P(),
            P(),
            P(),
            P(),
            P(None, None, None, "t"),
            P(None, "t", None),
            P(d, None),
        ),
        out_specs=(
            P(d, None),
            P(d, None),
            P(d, None),
            P(d),
            P(None, d, "t"),
            P("t", d),
            P(d),
            P(d, None),
            P(d, None),
            P(None, d),
            P(None, None, d, "t"),
            P(None, "t", d),
        ),
        check_vma=False,
    )
```

```python
import functools
import math

import jax
import jax.numpy as jnp
import numpy as np
from jax import lax
from jax.experimental import pallas as pl
from jax.experimental.pallas import tpu as pltpu
from jax.sharding import Mesh
from jax.sharding import PartitionSpec as P

f32 = jnp.float32
bf = jnp.bfloat16
E_FFN = 4
NCONST = 2
E_ALL = 8
SPAN = 16
SEQ_LEN = 8192
EPSILON = 1e-05
HIGHEST = lax.Precision.HIGHEST
GROUP = ("z", "y", "x")
GATE_ROWS = 16


HD = 64
NEG = -1e30
WIDE = (4, 2, 1)


def dotf(a, b, ca, cb):
    return lax.dot_general(a, b, (((ca,), (cb,)), ((), ())), preferred_element_type=f32)


def key_places(t, blocks, half):
    r = lax.broadcasted_iota(jnp.int32, (blocks * 2 * half, half), 0)
    inside = r % (2 * half)
    return r - inside + jnp.where(inside < half, t * half + inside, (1 - t) * half + inside - half)


def fwd_kernel(nb, half, sc, start_ref, own_ref, oth_ref, o_ref, of_ref, lse_ref, ktm, vt):
    keys = 2 * half
    t = sc[0]

    def prep(j, _):
        at = pl.ds(pl.multiple_of(j * keys, keys), half)
        more = pl.ds(pl.multiple_of(j * keys + half, half), half)
        ktm[at, :] = own_ref[j, HD : 2 * HD, :].T
        ktm[more, :] = oth_ref[j, 0:HD, :].T
        vt[:, at] = own_ref[j, 2 * HD : 3 * HD, :]
        vt[:, more] = oth_ref[j, HD : 2 * HD, :]
        return 0

    lax.fori_loop(0, nb, prep, 0)
    lane = lax.broadcasted_iota(jnp.int32, (1, half), 1)

    def qblock(s, _):
        q = own_ref[s, 0:HD, :] * bf(0.125)
        start_row = start_ref[s]
        last_row = s * keys + t * half + lane
        lo, ml = sc[1 + s], jnp.minimum(sc[1 + nb + s], s)

        def scores(j, n):
            return dotf(ktm[pl.ds(pl.multiple_of(j * keys, keys), n * keys), :], q, 1, 0)

        def allowed(j, n):
            place = key_places(t, n, half) + j * keys
            return (place >= start_row) & (place <= last_row)

        def values(j, n):
            return vt[:, pl.ds(pl.multiple_of(j * keys, keys), n * keys)]

        def emit(o, lse):
            o_ref[s] = o.astype(bf)
            of_ref[s] = o
            lse_ref[s] = lse

        def plain(j, n, c, masked):
            l, acc = c
            p = jnp.exp(scores(j, n))
            if masked:
                p = jnp.where(allowed(j, n), p, 0.0)
            return l + jnp.sum(p, axis=0, keepdims=True), acc + dotf(values(j, n), p.astype(bf), 1, 0)

        c = (jnp.zeros((1, half), f32), jnp.zeros((HD, half), f32))
        c = plain(s, 1, c, True)
        for masked, first, end in ((True, lo, ml), (False, jnp.maximum(lo, ml), s)):
            for n in WIDE:
                count = jnp.maximum(end - first, 0) // n
                c = lax.fori_loop(0, count, lambda i, c: plain(first + i * n, n, c, masked), c)
                first = first + count * n
        l, acc = c
        emit(acc / l, jnp.log(l))
        fine = (jnp.min(l) > 1e-25) & (jnp.max(l) < 1e25)

        @pl.when(jnp.logical_not(fine))
        def _():
            def shifted(j, c):
                m, l, acc = c
                sco = jnp.where(allowed(j, 1), scores(j, 1), NEG)
                mn = jnp.maximum(m, jnp.max(sco, axis=0, keepdims=True))
                p = jnp.exp(sco - mn)
                al = jnp.exp(m - mn)
                return mn, l * al + jnp.sum(p, axis=0, keepdims=True), acc * al + dotf(values(j, 1), p.astype(bf), 1, 0)

            c = (jnp.full((1, half), NEG, f32), jnp.zeros((1, half), f32), jnp.zeros((HD, half), f32))
            c = shifted(s, c)
            m, l, acc = lax.fori_loop(lo, s, shifted, c)
            emit(acc / l, m + jnp.log(l))

        return 0

    lax.fori_loop(0, nb, qblock, 0)


def flash_fwd(sc, start, own, oth):
    nb, _, half = own.shape
    v = pl.BlockSpec(memory_space=pltpu.VMEM)
    return pl.pallas_call(
        functools.partial(fwd_kernel, nb, half),
        out_shape=(
            jax.ShapeDtypeStruct((nb, HD, half), bf),
            jax.ShapeDtypeStruct((nb, HD, half), f32),
            jax.ShapeDtypeStruct((nb, 1, half), f32),
        ),
        in_specs=[pl.BlockSpec(memory_space=pltpu.SMEM), v, v, v],
        out_specs=(v, v, v),
        scratch_shapes=[pltpu.VMEM((nb * 2 * half, HD), bf), pltpu.VMEM((HD, nb * 2 * half), bf)],
        compiler_params=pltpu.CompilerParams(vmem_limit_bytes=48 << 20),
        cost_estimate=pl.CostEstimate(flops=10**9, bytes_accessed=4 << 20, transcendentals=10**6),
        name="flash_fwd",
    )(sc, start, own, oth)


def bwd_kernel(
    nb, half, j0, j1, sc, start_ref, own_ref, oth_ref, do_ref, of_ref, lse_ref,
    dq_ref, dko_ref, dkx_ref, ktm, vtm, kt, qt, dot, dq_acc, dotm, qtm, stats,
):
    keys = 2 * half
    t = sc[0]

    def prep(j, _):
        k = j - j0
        ktm[k, 0:half, :] = own_ref[j, HD : 2 * HD, :].T
        ktm[k, half:keys, :] = oth_ref[j, 0:HD, :].T
        vtm[k, 0:half, :] = own_ref[j, 2 * HD : 3 * HD, :].T
        vtm[k, half:keys, :] = oth_ref[j, HD : 2 * HD, :].T
        kt[k, :, 0:half] = own_ref[j, HD : 2 * HD, :]
        kt[k, :, half:keys] = oth_ref[j, 0:HD, :]
        return 0

    lax.fori_loop(j0, j1, prep, 0)

    def prep_q(s, _):
        at = pl.ds(pl.multiple_of(s * half, half), half)
        q = own_ref[s, 0:HD, :] * bf(0.125)
        qt[:, at] = q
        qtm[at, :] = q.T
        dot[:, at] = do_ref[s]
        dotm[at, :] = do_ref[s].T
        dq_acc[:, at] = jnp.zeros((HD, half), f32)
        stats[0:1, at] = lse_ref[s]
        stats[1:2, at] = jnp.sum(do_ref[s].astype(f32) * of_ref[s], axis=0, keepdims=True)
        return 0

    lax.fori_loop(j0, nb, prep_q, 0)
    lane = lax.broadcasted_iota(jnp.int32, (1, half), 1)

    def kblock(j, _):
        k = j - j0
        kj, vj, ktj = ktm[k], vtm[k], kt[k]

        def tile(s, n, c, masked):
            dk, dv = c
            at = pl.ds(pl.multiple_of(s * half, half), n * half)
            sco = dotf(kj, qt[:, at], 1, 0)
            if masked:
                place = key_places(t, 1, half) + j * keys
                last_row = s * keys + t * half + lane
                sco = jnp.where((place >= start_ref[s]) & (place <= last_row), sco, NEG)
            p = jnp.exp(sco - stats[0:1, at])
            dp = dotf(vj, dot[:, at], 1, 0)
            ds = (p * (dp - stats[1:2, at])).astype(bf)
            dv = dv + dotf(p.astype(bf), dotm[at, :], 1, 0)
            dk = dk + dotf(ds, qtm[at, :], 1, 0)
            dq_acc[:, at] += dotf(ktj, ds, 1, 0)
            return dk, dv

        c = (jnp.zeros((keys, HD), f32), jnp.zeros((keys, HD), f32))
        c = tile(j, 1, c, True)
        mid, hi = sc[1 + 2 * nb + j], sc[1 + 3 * nb + j]
        first = j + 1
        for n in WIDE:
            count = jnp.maximum(mid - first, 0) // n
            c = lax.fori_loop(0, count, lambda i, c: tile(first + i * n, n, c, False), c)
            first = first + count * n
        dk, dv = lax.fori_loop(jnp.maximum(j + 1, mid), hi, lambda s, c: tile(s, 1, c, True), c)
        dk = dk.T
        dv = dv.T
        dko_ref[k, 0:HD, :] = dk[:, 0:half]
        dko_ref[k, HD : 2 * HD, :] = dv[:, 0:half]
        dkx_ref[k, 0:HD, :] = dk[:, half:keys].astype(bf)
        dkx_ref[k, HD : 2 * HD, :] = dv[:, half:keys].astype(bf)
        return 0

    lax.fori_loop(j0, j1, kblock, 0)

    def finish(s, _):
        at = pl.ds(pl.multiple_of(s * half, half), half)
        dq_ref[s] = (dq_acc[:, at] * 0.125).astype(bf)
        return 0

    def nothing(s, _):
        dq_ref[s] = jnp.zeros((HD, half), bf)
        return 0

    lax.fori_loop(0, j0, nothing, 0)
    lax.fori_loop(j0, nb, finish, 0)


def flash_bwd(sc, start, own, oth, do, of, lse, j0=0, j1=SPAN):
    nb, _, half = own.shape
    v = pl.BlockSpec(memory_space=pltpu.VMEM)
    n = j1 - j0
    return pl.pallas_call(
        functools.partial(bwd_kernel, nb, half, j0, j1),
        out_shape=(
            jax.ShapeDtypeStruct((nb, HD, half), bf),
            jax.ShapeDtypeStruct((n, 2 * HD, half), f32),
            jax.ShapeDtypeStruct((n, 2 * HD, half), bf),
        ),
        in_specs=[pl.BlockSpec(memory_space=pltpu.SMEM)] + [v] * 6,
        out_specs=(v, v, v),
        scratch_shapes=[
            pltpu.VMEM((n, 2 * half, HD), bf),
            pltpu.VMEM((n, 2 * half, HD), bf),
            pltpu.VMEM((n, HD, 2 * half), bf),
            pltpu.VMEM((HD, nb * half), bf),
            pltpu.VMEM((HD, nb * half), bf),
            pltpu.VMEM((HD, nb * half), f32),
            pltpu.VMEM((nb * half, HD), bf),
            pltpu.VMEM((nb * half, HD), bf),
            pltpu.VMEM((8, nb * half), f32),
        ],
        compiler_params=pltpu.CompilerParams(vmem_limit_bytes=56 << 20),
        cost_estimate=pl.CostEstimate(flops=10**9, bytes_accessed=4 << 20, transcendentals=10**6),
        name="flash_bwd",
    )(sc, start, own, oth, do, of, lse)


def bounds(start_all, t, nb, HB):
    st=start_all.reshape(nb,2,HB)
    mine=lax.dynamic_index_in_dim(st,t,1,keepdims=False)
    first=mine[:,0]; last=mine[:,HB-1]
    B=2*HB
    lo=first//B
    ml=(last+B-1)//B
    j=jnp.arange(nb)
    mid=jnp.sum((last[None,:]<=j[:,None]*B).astype(jnp.int32),axis=1)
    hi=jnp.sum((lo[None,:]<=j[:,None]).astype(jnp.int32),axis=1)
    mid=jnp.minimum(mid,hi)
    sc=jnp.concatenate([jnp.full((1,),t,jnp.int32),lo,ml,mid,hi]).astype(jnp.int32)
    return sc,mine[:,None,:]


def ffn_kernel(e_ref, u_ref, wgu_ref, wd_ref, *refs):
    pieces = refs[:8]
    x_out_ref, g_ref, wh_ref, mine_ref, other_ref, out_mine_ref, out_other_ref, held = refs[8:]
    half = u_ref.shape[1]
    width = x_out_ref.shape[2]
    hidden_units = wgu_ref.shape[3]
    e = e_ref[0]
    step = pl.program_id(0)
    for k in range(8):

        @pl.when(step == k)
        def _(k=k):
            held[...] = pieces[k][...]

    gates = held[half : half + GATE_ROWS, 0:half].astype(f32)
    row = lax.broadcasted_iota(jnp.int32, gates.shape, 0)
    gate_row = jnp.sum(jnp.where((row == e) | (row == e + E_FFN), gates, 0.0), axis=0, keepdims=True)
    gate = jnp.broadcast_to(gate_row, (8, half)).T[:, 0:1]
    x = held[0:half, :]
    x_out_ref[0] = x
    g = dotf(x, wgu_ref[0, 0], 1, 0)
    up = dotf(x, wgu_ref[0, 1], 1, 0)
    raw = u_ref[0].astype(f32)
    sig = 0.5 * jnp.tanh(0.5 * g) + 0.5
    silu = g * sig
    hid = silu * up
    hg = gate * raw
    g_ref[0, :, 0:hidden_units] = (hg * up * (sig + silu * (1.0 - sig))).astype(bf)
    g_ref[0, :, hidden_units : 2 * hidden_units] = (hg * silu).astype(bf)
    wh_ref[0] = (gate * hid).astype(bf)
    dots = jnp.broadcast_to(jnp.sum(hid * raw, axis=-1, keepdims=True), (half, 128)).T[0:8]
    total = dotf(g_ref[0, :, 0:hidden_units], wgu_ref[0, 0], 1, 1)
    total = total + dotf(g_ref[0, :, hidden_units : 2 * hidden_units], wgu_ref[0, 1], 1, 1)
    result = dotf(wh_ref[0], wd_ref[0], 1, 0)
    drow = lax.broadcasted_iota(jnp.int32, (GATE_ROWS, half), 0)
    placed = jnp.where(drow == e, jnp.broadcast_to(dots[0:1, :], (GATE_ROWS, half)), 0.0).astype(bf)

    def put(ref):
        ref[0, 0:half, :] = total.astype(bf)
        ref[0, half : half + GATE_ROWS, :] = jnp.zeros((GATE_ROWS, width), bf)
        ref[0, half : half + GATE_ROWS, 0:half] = placed

    @pl.when(step < 4)
    def _():
        put(mine_ref)
        out_mine_ref[0] = result.astype(bf)

    @pl.when(step >= 4)
    def _():
        put(other_ref)
        out_other_ref[0] = result.astype(bf)


def expert_pass(e, pieces, raw_all, wgu, wdown):
    rows, width = pieces[0].shape
    half = rows - GATE_ROWS
    hidden_units = wgu.shape[3]
    flops = 8 * half * width * hidden_units * 2 * 4
    return pl.pallas_call(
        ffn_kernel,
        out_shape=(
            jax.ShapeDtypeStruct((8, half, width), bf),
            jax.ShapeDtypeStruct((8, half, 2 * hidden_units), bf),
            jax.ShapeDtypeStruct((8, half, hidden_units), bf),
            jax.ShapeDtypeStruct((4, rows, width), bf),
            jax.ShapeDtypeStruct((4, rows, width), bf),
            jax.ShapeDtypeStruct((4, half, width), bf),
            jax.ShapeDtypeStruct((4, half, width), bf),
        ),
        grid_spec=pltpu.PrefetchScalarGridSpec(
            num_scalar_prefetch=1,
            grid=(8,),
            in_specs=[
                pl.BlockSpec((1, half, hidden_units), lambda i, e: (i, 0, 0)),
                pl.BlockSpec((1, 2, width, hidden_units), lambda i, e: (e[0], 0, 0, 0)),
                pl.BlockSpec((1, hidden_units, width), lambda i, e: (e[0], 0, 0)),
            ]
            + [pl.BlockSpec((rows, width), lambda i, e: (0, 0))] * 8,
            out_specs=(
                pl.BlockSpec((1, half, width), lambda i, e: (i, 0, 0)),
                pl.BlockSpec((1, half, 2 * hidden_units), lambda i, e: (i, 0, 0)),
                pl.BlockSpec((1, half, hidden_units), lambda i, e: (i, 0, 0)),
                pl.BlockSpec((1, rows, width), lambda i, e: (jnp.minimum(i, 3), 0, 0)),
                pl.BlockSpec((1, rows, width), lambda i, e: (jnp.maximum(i - 4, 0), 0, 0)),
                pl.BlockSpec((1, half, width), lambda i, e: (jnp.minimum(i, 3), 0, 0)),
                pl.BlockSpec((1, half, width), lambda i, e: (jnp.maximum(i - 4, 0), 0, 0)),
            ),
            scratch_shapes=[pltpu.VMEM((rows, width), bf)],
        ),
        compiler_params=pltpu.CompilerParams(vmem_limit_bytes=48 << 20),
        cost_estimate=pl.CostEstimate(flops=flops, bytes_accessed=40 << 20, transcendentals=2 << 20),
        name="expert_pass",
    )(e, raw_all, wgu, wdown, *pieces)


def hidden_cotangent_kernel(at_ref, w_ref, rows_ref, up_ref, raw_ref):
    rows = rows_ref[0]
    up_ref[0] = rows
    raw_ref[0] = dotf(rows, w_ref[0], 1, 1).astype(bf)


def hidden_cotangent(at, rows, w_down):
    pieces, half, width = rows.shape
    hidden_units = w_down.shape[1]
    return pl.pallas_call(
        hidden_cotangent_kernel,
        out_shape=(
            jax.ShapeDtypeStruct((pieces, half, width), bf),
            jax.ShapeDtypeStruct((pieces, half, hidden_units), bf),
        ),
        grid_spec=pltpu.PrefetchScalarGridSpec(
            num_scalar_prefetch=1,
            grid=(pieces,),
            in_specs=[
                pl.BlockSpec((1, hidden_units, width), lambda i, at: (at[0], 0, 0)),
                pl.BlockSpec((1, half, width), lambda i, at: (at[1 + i], 0, 0)),
            ],
            out_specs=(
                pl.BlockSpec((1, half, width), lambda i, at: (i, 0, 0)),
                pl.BlockSpec((1, half, hidden_units), lambda i, at: (i, 0, 0)),
            ),
        ),
        compiler_params=pltpu.CompilerParams(vmem_limit_bytes=40 << 20),
        cost_estimate=pl.CostEstimate(flops=32 * 10**8, bytes_accessed=12 << 20, transcendentals=0),
        name="hidden_cotangent",
    )(at, w_down, rows)


def exact(a, b, ca, cb):
    return lax.dot_general(a, b, (((ca,), (cb,)), ((), ())), precision=HIGHEST, preferred_element_type=f32)


def back_rows_kernel(
    first_ref, p0, p1, p2, p3, residual_ref, up_ref, gain_ref, rows_ref, small_ref, const_ref, own_ref, other_ref,
    grad_ref, low_ref, cot_ref, logit_ref, gain_out_ref,
):
    half, width = residual_ref.shape
    dx = p0[...].astype(f32) + p1[...].astype(f32) + p2[...].astype(f32) + p3[...].astype(f32)
    gating = dx[half : half + E_ALL, 0:half]
    dx = dx[0:half]
    residual, gain = residual_ref[...], gain_ref[...]
    up = up_ref[...].astype(f32)
    inverse = lax.rsqrt(jnp.mean(residual * residual, axis=-1, keepdims=True) + EPSILON)
    probs, hot = rows_ref[0:8], rows_ref[8:16]
    blend_one, blend_two, const_weight = rows_ref[16:18], rows_ref[18:20], rows_ref[20:22]
    kept = rows_ref[22:23]
    copy_dot = exact(jnp.ones((8, width), f32), up * (residual * inverse * gain), 1, 1)[0:1]
    vector_dot = exact(const_ref[...], up, 1, 1)[0:NCONST]
    const_dot = blend_one * copy_dot + blend_two * vector_dot
    row = lax.broadcasted_iota(jnp.int32, (8, half), 0)
    dots = jnp.where(row < E_FFN, gating, 0.0)
    dots = jnp.where(row == E_FFN + 1, copy_dot, dots)
    for c in range(NCONST):
        dots = jnp.where(row == E_FFN + 2 + c, const_dot[c : c + 1], dots)
    probs_grad = dots * hot
    logit_ref[0:8] = probs * (probs_grad - jnp.sum(probs * probs_grad, axis=0, keepdims=True))
    grad_one = const_weight * copy_dot
    grad_two = const_weight * vector_dot
    inner = blend_one * grad_one + blend_two * grad_two
    grad_one = blend_one * (grad_one - inner)
    grad_two = blend_two * (grad_two - inner)
    const_grad = jnp.zeros((8, half), f32)
    for c in range(NCONST):
        const_grad = jnp.where(row == 2 * c, grad_one[c : c + 1], const_grad)
        const_grad = jnp.where(row == 2 * c + 1, grad_two[c : c + 1], const_grad)
    logit_ref[8:16] = const_grad
    kept_column = jnp.broadcast_to(kept, (8, half)).T[:, 0:1]
    normed_grad = dx + exact(logit_ref[...], small_ref[...], 0, 0) + kept_column * up
    gain_out_ref[...] = jnp.sum(normed_grad * residual * inverse, axis=0, keepdims=True)
    scaled = normed_grad * gain
    mean = jnp.mean(scaled * residual, axis=-1, keepdims=True)
    grad = up + inverse * scaled - residual * (inverse * inverse * inverse * mean)
    grad_ref[...] = grad
    low = grad.astype(bf)
    low_ref[...] = low
    heads = own_ref.shape[0] // HD
    cot_ref[...] = jnp.zeros(cot_ref.shape, bf)
    for n, ref in enumerate((own_ref, other_ref)):
        rows = dotf(ref[...], low, 1, 1).astype(bf)
        for h in range(heads):
            cot_ref[first_ref[n] + h] = rows[h * HD : (h + 1) * HD]


def back_rows(first, parts, residual, up, gain, rows, small, const, own, other):
    half, width = residual.shape
    v = pl.BlockSpec(memory_space=pltpu.VMEM)
    return pl.pallas_call(
        back_rows_kernel,
        out_shape=(
            jax.ShapeDtypeStruct((half, width), f32),
            jax.ShapeDtypeStruct((half, width), bf),
            jax.ShapeDtypeStruct((SPAN, HD, half), bf),
            jax.ShapeDtypeStruct((16, half), f32),
            jax.ShapeDtypeStruct((1, width), f32),
        ),
        in_specs=[pl.BlockSpec(memory_space=pltpu.SMEM)] + [v] * 12,
        out_specs=(v,) * 5,
        compiler_params=pltpu.CompilerParams(vmem_limit_bytes=60 << 20),
        cost_estimate=pl.CostEstimate(flops=4 * 10**8, bytes_accessed=5 << 20, transcendentals=0),
        name="back_rows",
    )(first, *parts, residual, up, gain.reshape(1, width), rows, small, const, own, other)


def token_rows_kernel(first_ref, arrived_ref, own_ref, other_ref, grad_ref, x_ref, gain_ref, whole_ref, out_ref, rows):
    heads = own_ref.shape[2] // HD
    upstream = jnp.zeros(out_ref.shape, f32)
    for n, ref in enumerate((own_ref, other_ref)):
        for s in range(3):
            for h in range(heads):
                rows[h * HD : (h + 1) * HD, :] = arrived_ref[first_ref[n] + h, s * HD : (s + 1) * HD, :]
            upstream = upstream + dotf(rows[...], ref[s], 0, 1)
    x = x_ref[...].astype(f32)
    inverse = lax.rsqrt(jnp.mean(x * x, axis=-1, keepdims=True) + EPSILON)
    scaled = upstream * gain_ref[...]
    mean = jnp.mean(scaled * x, axis=-1, keepdims=True)
    out = grad_ref[...] + inverse * scaled - x * (inverse * inverse * inverse * mean)
    out_ref[...] = out
    whole_ref[pl.ds(pl.multiple_of(first_ref[2], out.shape[0]), out.shape[0]), :] = out


def token_rows(first, arrived, own, other, grad, x, gain):
    half, width = x.shape
    v = pl.BlockSpec(memory_space=pltpu.VMEM)
    return pl.pallas_call(
        token_rows_kernel,
        out_shape=(jax.ShapeDtypeStruct((2 * half, width), f32), jax.ShapeDtypeStruct((half, width), f32)),
        in_specs=[pl.BlockSpec(memory_space=pltpu.SMEM)] + [v] * 6,
        out_specs=(v, v),
        scratch_shapes=[pltpu.VMEM((own.shape[2], half), bf)],
        compiler_params=pltpu.CompilerParams(vmem_limit_bytes=60 << 20),
        cost_estimate=pl.CostEstimate(flops=10**9, bytes_accessed=6 << 20, transcendentals=0),
        name="token_rows",
    )(first, arrived, own, other, grad, x, gain.reshape(1, width))


def heads_kernel(first_ref, x_ref, gain_ref, w_ref, cos_ref, sin_ref, *refs):
    buffer_ref, normed_ref = refs[-2:]
    x = x_ref[...].astype(f32)
    inverse = lax.rsqrt(jnp.mean(x * x, axis=-1, keepdims=True) + EPSILON)
    normed = (x * inverse * gain_ref[...]).astype(bf)
    normed_ref[...] = normed
    cosine, sine = cos_ref[...], sin_ref[...]
    heads = w_ref.shape[2] // HD
    first = first_ref[0]
    buffer_ref[...] = refs[0][...] if len(refs) == 3 else jnp.zeros(buffer_ref.shape, bf)
    for s in range(3):
        rows = dotf(normed, w_ref[s], 1, 0).T
        for h in range(heads):
            part = rows[h * HD : (h + 1) * HD]
            if s < 2:
                one, two = part[: HD // 2], part[HD // 2 :]
                part = jnp.concatenate([one * cosine - two * sine, two * cosine + one * sine], axis=0)
            buffer_ref[first + h, s * HD : (s + 1) * HD, :] = part.astype(bf)


def head_rows(first, x, gain, w, cosine, sine, buffer=None):
    half, width = x.shape
    v = pl.BlockSpec(memory_space=pltpu.VMEM)
    given = [] if buffer is None else [buffer]
    return pl.pallas_call(
        heads_kernel,
        out_shape=(
            jax.ShapeDtypeStruct((SPAN, 3 * HD, half), bf),
            jax.ShapeDtypeStruct((half, width), bf),
        ),
        in_specs=[pl.BlockSpec(memory_space=pltpu.SMEM)] + [v] * 5 + [v] * len(given),
        out_specs=(v, v),
        compiler_params=pltpu.CompilerParams(vmem_limit_bytes=40 << 20),
        cost_estimate=pl.CostEstimate(flops=5 * 10**8, bytes_accessed=4 << 20, transcendentals=0),
        name="head_rows",
    )(first, x, gain.reshape(1, width), w, cosine, sine, *given)


def head_grad_kernel(at_ref, dq_ref, own_ref, other_ref, cos_ref, sin_ref, w_ref, *refs):
    pieces, out_ref, turned_rows = refs[:-2], refs[-2], refs[-1]
    half, width = pieces[0].shape[-2:]
    blocks = out_ref.shape[0]

    def back(rows, block):
        one, two = rows[: HD // 2], rows[HD // 2 :]
        cosine, sine = cos_ref[block], sin_ref[block]
        return jnp.concatenate([one * cosine + two * sine, two * cosine - one * sine], axis=0)

    acc = jnp.zeros((3 * HD, width), f32)
    n = 0
    for ref in pieces:
        places = list(np.ndindex(*ref.shape[:-2]))
        for k in range(len(places)):
            block = at_ref[n]
            dkv = own_ref[block] + other_ref[block].astype(f32)
            rows = jnp.concatenate(
                [back(dq_ref[block].astype(f32), block), back(dkv[:HD], block), dkv[HD:]], axis=0
            ).astype(bf)
            out_ref[block, 0 : 3 * HD, :] = rows
            turned_rows[:, k * half : (k + 1) * half] = rows
            n += 1
        count = len(places) * half
        acc = acc + dotf(turned_rows[:, 0:count], ref[...].reshape(count, width), 1, 0)
    gain_row = jnp.sum(acc * w_ref[...].astype(f32), axis=0, keepdims=True)
    turned = jnp.concatenate([acc, jnp.broadcast_to(gain_row, (8, width))], axis=0).T.astype(bf)
    rows = turned.shape[0] // blocks
    for block in range(blocks):
        out_ref[block, 3 * HD :, :] = jnp.zeros((rows, out_ref.shape[2]), bf)
        out_ref[block, 3 * HD :, 0 : 3 * HD + 8] = turned[block * rows : (block + 1) * rows]


def head_grad(at, dq, own, other, cosine, sine, w_head, pieces):
    v = pl.BlockSpec(memory_space=pltpu.VMEM)
    half, width = pieces[0].shape[-2:]
    blocks = dq.shape[0]
    return pl.pallas_call(
        head_grad_kernel,
        out_shape=jax.ShapeDtypeStruct((blocks, 3 * HD + width // blocks, half), bf),
        in_specs=[pl.BlockSpec(memory_space=pltpu.SMEM)] + [v] * (6 + len(pieces)),
        out_specs=v,
        scratch_shapes=[pltpu.VMEM((3 * HD, 4 * half), bf)],
        compiler_params=pltpu.CompilerParams(vmem_limit_bytes=60 << 20),
        cost_estimate=pl.CostEstimate(flops=12 * 10**8, bytes_accessed=12 << 20, transcendentals=0),
        name="head_grad",
    )(at, dq, own, other, cosine, sine, w_head, *pieces)


def finish_kernel(e_ref, *refs):
    parts, (gu_ref, down_ref, sum_ref) = refs[:4], refs[4:]
    units = down_ref.shape[1]
    rest = 3 * units
    rows = [p[...].astype(f32) for p in parts]
    sum_ref[...] = rows[0][:, rest:] + rows[1][:, rest:] + rows[2][:, rest:] + rows[3][:, rest:]
    for k in range(E_FFN):
        distance = e_ref[0] ^ k
        low = jnp.where(distance == 0, rows[0][:, :rest], rows[1][:, :rest])
        high = jnp.where(distance == 2, rows[2][:, :rest], rows[3][:, :rest])
        one = jnp.where(distance < 2, low, high)
        gu_ref[k, 0] = one[:, 0:units]
        gu_ref[k, 1] = one[:, units : 2 * units]
        down_ref[k] = one[:, 2 * units :].T


def finish(e, parts, units):
    slab, columns = parts[0].shape
    v = pl.BlockSpec(memory_space=pltpu.VMEM)
    return pl.pallas_call(
        finish_kernel,
        out_shape=(
            jax.ShapeDtypeStruct((E_FFN, 2, slab, units), f32),
            jax.ShapeDtypeStruct((E_FFN, units, slab), f32),
            jax.ShapeDtypeStruct((slab, columns - 3 * units), f32),
        ),
        in_specs=[pl.BlockSpec(memory_space=pltpu.SMEM)] + [v] * 4,
        out_specs=(v, v, v),
        compiler_params=pltpu.CompilerParams(vmem_limit_bytes=40 << 20),
        cost_estimate=pl.CostEstimate(flops=10**5, bytes_accessed=10**5, transcendentals=0),
        name="finish",
    )(e, *parts)


def swap(value, axis):
    return lax.ppermute(value, axis, [(0, 1), (1, 0)])


def plane_diagonal(value):
    return lax.ppermute(value, ("y", "x"), [(i, 3 - i) for i in range(4)])


def plane_gather(piece):
    mine = [piece, swap(piece, "x"), swap(piece, "y"), plane_diagonal(piece)]
    return mine + [swap(p, "t") for p in mine]


def plane_scatter(mine, other, later):
    held = [(mine[k].astype(f32) + other[k].astype(f32)).astype(bf) for k in range(4)]
    held, later = lax.optimization_barrier((held, later))
    return [held[0], swap(held[1], "x"), swap(held[2], "y"), plane_diagonal(held[3])], later


def over_z(value, distance):
    return lax.ppermute(value, "z", [(i, i ^ distance) for i in range(4)])


def total(parts):
    first, rest = parts
    return first.astype(f32) + sum(p.astype(f32) for p in rest)


def plane_rows(chunks):
    b = lax.axis_index(("y", "x"))
    pick = lambda d: lax.dynamic_index_in_dim(chunks, b ^ d, 0, keepdims=False)
    return pick(0), [swap(pick(1), "x"), swap(pick(2), "y"), plane_diagonal(pick(3))]


def after(value, *others):
    return lax.optimization_barrier((value, others))[0]


def over_sequences(rows):
    if lax.axis_size("s") == 1:
        return rows
    return lax.psum_scatter(rows, "s", scatter_dimension=0, tiled=True)


def first_tokens(segments):
    def gathered(value, moved, places):
        low, high = places
        first = jnp.where(low == 0, jnp.stack([value, moved[0]]), jnp.stack([moved[0], value]))
        second = jnp.where(low == 0, jnp.stack([moved[1], moved[2]]), jnp.stack([moved[2], moved[1]]))
        return jnp.where(high == 0, jnp.stack([first, second]), jnp.stack([second, first]))

    z = lax.axis_index("z")
    plane = [swap(segments, "x"), swap(segments, "y"), plane_diagonal(segments)]
    ids = gathered(segments, plane, (lax.axis_index("x"), lax.axis_index("y"))).reshape(-1)
    ids = gathered(ids, [over_z(ids, d) for d in (1, 2, 3)], (z % 2, z // 2)).reshape(-1)
    count = ids.shape[0]
    index = jnp.arange(count, dtype=jnp.int32)
    before = jnp.concatenate([ids[:1], ids[:-1]])
    opens = jnp.where(ids != before, index, 0).reshape(-1, 256)
    n = opens.shape[0]
    lane = jnp.arange(256, dtype=jnp.int32)
    within = jnp.max(jnp.where(lane[None, None, :] <= lane[None, :, None], opens[:, None, :], 0), axis=-1)
    block = jnp.arange(n, dtype=jnp.int32)
    top = jnp.max(opens, axis=1)
    carry = jnp.max(jnp.where(block[None, :] < block[:, None], top[None, :], 0), axis=1)
    return jnp.maximum(within, carry[:, None]).reshape(-1)


def rotary_tables(position, half_dim):
    inv_freq = jnp.exp(jnp.arange(half_dim).astype(f32) * (-math.log(10000.0) / half_dim))
    phases = inv_freq[:, None] * position.astype(f32)[None, :]
    return jnp.cos(phases), jnp.sin(phases)


def rotate(values, cosine, sine):
    half_dim = values.shape[-2] // 2
    one, two = values[..., :half_dim, :], values[..., half_dim:, :]
    return jnp.concatenate([one * cosine - two * sine, two * cosine + one * sine], axis=-2)


def norm_forward(values, gain):
    inverse = lax.rsqrt(jnp.mean(values * values, axis=-1, keepdims=True) + EPSILON)
    return values * inverse * gain, inverse


def norm_backward(values, inverse, gain, upstream):
    scaled = upstream * gain
    inner = jnp.mean(scaled * values, axis=-1, keepdims=True)
    return (
        inverse * scaled - values * inverse * inverse * inverse * inner,
        jnp.sum(upstream * values * inverse, axis=0),
    )


def local(
    tokens,
    segments,
    routes,
    prev_logits,
    attn_gain,
    w_qkv,
    w_out,
    ffn_gain,
    w_router,
    w_const,
    v_const,
    w_gu,
    w_down,
    cotangent,
):
    tok_count, width = tokens.shape
    half = tok_count // 2
    features = w_qkv.shape[2]
    heads = features // HD
    t = lax.axis_index("t")
    place = lax.axis_index(GROUP)
    expert = lax.axis_index(("y", "x"))

    def mine(value):
        return lax.dynamic_slice_in_dim(value, t * half, half, 0)

    def both_halves(value):
        other = swap(value, "t")
        whole = jnp.zeros((tok_count,) + value.shape[1:], value.dtype)
        whole = lax.dynamic_update_slice_in_dim(whole, value, t * half, 0)
        return lax.dynamic_update_slice_in_dim(whole, other, (1 - t) * half, 0)

    w_qkv_other = swap(w_qkv, "t")
    w_out_other = swap(w_out, "t")
    inputs = mine(tokens).astype(f32)
    upstream_low = mine(cotangent)
    upstream = upstream_low.astype(f32)
    my_routes = jnp.transpose(mine(routes))
    my_prev = jnp.transpose(mine(prev_logits))
    kinds = jnp.arange(E_ALL, dtype=jnp.int32)[:, None]
    hot = (my_routes[0:1] == kinds).astype(f32) + (my_routes[1:2] == kinds).astype(f32)
    position = (place * tok_count + t * half + jnp.arange(half, dtype=jnp.int32)) % SEQ_LEN
    cosine, sine = rotary_tables(position, HD // 2)
    tokens_mine = mine(tokens)
    first = (t * heads).astype(jnp.int32).reshape(1)
    other_first = ((1 - t) * heads).astype(jnp.int32).reshape(1)
    buffer, normed_low = head_rows(first, tokens_mine, attn_gain, w_qkv, cosine, sine)
    buffer, _ = head_rows(other_first, tokens_mine, attn_gain, w_qkv_other, cosine, sine, buffer)

    def of_heads(buffer):
        return (
            lax.dynamic_slice_in_dim(buffer, t * heads, heads, 0),
            lax.dynamic_slice_in_dim(buffer, (1 - t) * heads, heads, 0),
        )

    def exchange(buffer):
        return lax.all_to_all(buffer, GROUP, 0, 0, tiled=True)

    upstream_sent, segments, buffer = lax.optimization_barrier((upstream_low, segments, buffer))
    start_all = first_tokens(segments)
    sc, start_rows = bounds(start_all, t, SPAN, half)
    own = exchange(buffer)
    oth = swap(own[:, HD:], "t")
    up_gathered = lax.all_gather(upstream_sent, ("y", "x", "t"))
    piece_rank = jnp.bitwise_xor(2 * expert + t, jnp.array((0, 2, 4, 6, 1, 3, 5, 7), jnp.int32))
    expert_at = expert.astype(jnp.int32).reshape(1)
    normed_sent, own_q, sc, start_rows = lax.optimization_barrier((normed_low, own, sc, start_rows))
    along_z = [normed_sent] + [over_z(normed_sent, d) for d in (1, 2, 3)]
    heads_rows, heads_full, lse = flash_fwd(sc, start_rows, own_q, oth)
    heads_rows, up_gathered, along_z = lax.optimization_barrier((heads_rows, up_gathered, along_z))
    back = exchange(heads_rows)
    up_all, raw_all = hidden_cotangent(
        jnp.concatenate([expert_at, piece_rank.astype(jnp.int32)]), up_gathered, w_down
    )
    back, raw_all = lax.optimization_barrier((back, raw_all))
    heads_own, heads_other = (v.reshape(features, half) for v in of_heads(back))
    branch = dotf(heads_own, w_out, 0, 0) + dotf(heads_other, w_out_other, 0, 0)
    residual = inputs + branch
    normed_ffn, inverse_ffn = norm_forward(residual, ffn_gain)
    ffn_low = normed_ffn.astype(bf)
    w_small = jnp.concatenate([w_router, w_const], axis=1)
    logits = dotf(w_small, ffn_low, 0, 1)
    router_probs = jax.nn.softmax(logits[:E_ALL] + my_prev, axis=0)
    expert_weight = router_probs * hot
    gate_rows = expert_weight[:E_FFN]
    gate_high = gate_rows.astype(bf)
    gate_low = (gate_rows - gate_high.astype(f32)).astype(bf)
    gate_block = jnp.pad(
        jnp.concatenate([gate_high, gate_low]), ((0, GATE_ROWS - 2 * E_FFN), (0, width - half))
    )
    x_all = plane_gather(jnp.concatenate([ffn_low, gate_block]))
    w_held, w_other_held, t_late = after((w_qkv, w_qkv_other, t), ffn_low)
    all_position = (jnp.arange(SPAN, dtype=jnp.int32)[:, None] * tok_count + t_late * half)[:, :, None] + jnp.arange(half, dtype=jnp.int32)
    all_cosine, all_sine = rotary_tables(all_position.reshape(-1), HD // 2)
    by_block = lambda table: jnp.transpose(table.reshape(HD // 2, SPAN, half), (1, 0, 2))
    all_cosine, all_sine = by_block(all_cosine), by_block(all_sine)
    pair_a, pair_b = jnp.stack(along_z[:2]), jnp.stack(along_z[2:])
    near = (0, 4, 8, 12, 1, 5, 10, 14, 2, 6, 3, 7, 9, 13, 11, 15)
    at = jnp.bitwise_xor(place, jnp.array(near, jnp.int32)).astype(jnp.int32)
    head_first = jnp.minimum(place, 2 * heads - 1) % heads * HD
    of_head = lambda w: lax.dynamic_slice_in_dim(w, head_first, HD, 2)
    w_head = jnp.where(jnp.minimum(place // heads, 1) == t, of_head(w_held), of_head(w_other_held))
    w_head = jnp.swapaxes(w_head, 1, 2).reshape(3 * HD, width)
    x_all, all_cosine, all_sine, pair_a, pair_b, at, w_head = lax.optimization_barrier(
        (x_all, all_cosine, all_sine, pair_a, pair_b, at, w_head)
    )
    pair_ax, pair_by = swap(pair_a, "x"), swap(pair_b, "y")
    x_only, g_all, weighted, dx_mine, dx_other, out_mine, out_beside = expert_pass(
        expert_at, x_all, raw_all, w_gu, w_down
    )
    dx_mine, dx_other, pair_ax, pair_by = lax.optimization_barrier((dx_mine, dx_other, pair_ax, pair_by))
    dx_other = swap(dx_other, "t")
    hidden_units = w_down.shape[1]
    received, (weighted, g_all) = plane_scatter(dx_mine, dx_other, (weighted, g_all))
    down_part = jnp.einsum("ptd,ptf->df", up_all, weighted, preferred_element_type=f32).astype(bf)
    gu_part = jnp.einsum("ptd,ptf->df", x_only, g_all, preferred_element_type=f32).astype(bf)
    expert_part = over_sequences(jnp.concatenate([gu_part, down_part], axis=1))
    slab = expert_part.shape[0] // SPAN
    received, expert_part = lax.optimization_barrier((received, expert_part))
    expert_sum = lax.psum_scatter(expert_part, "z", scatter_dimension=0, tiled=True)

    pairs = logits[E_ALL:].reshape(NCONST, 2, half)
    blend_one = jax.nn.sigmoid(pairs[:, 0] - pairs[:, 1])
    blend_two = jax.nn.sigmoid(pairs[:, 1] - pairs[:, 0])
    const_weight = expert_weight[E_FFN + 2 :]
    kept = expert_weight[E_FFN + 1 : E_FFN + 2] + jnp.sum(const_weight * blend_one, axis=0, keepdims=True)
    added = const_weight * blend_two
    columns = jnp.transpose(jnp.concatenate([kept, added]))
    kept_column, added_columns = columns[:, 0:1], columns[:, 1:]

    pad_rows = lambda v, n: jnp.pad(v, ((0, n - v.shape[0]), (0, 0)))
    row_pack = pad_rows(jnp.concatenate([router_probs, hot, blend_one, blend_two, const_weight, kept]), 24)
    small_rows = pad_rows(jnp.transpose(w_small).astype(f32), 16)
    residual_grad, branch_cot, cot, logit_grad, ffn_gain_part = back_rows(
        jnp.concatenate([first, other_first]),
        received,
        residual,
        upstream_low,
        ffn_gain,
        row_pack,
        small_rows,
        pad_rows(v_const, 8),
        w_out,
        w_out_other,
    )
    logit_grad = logit_grad[: E_ALL + 2 * NCONST]
    prev_grad = logit_grad[:E_ALL]
    out_beside, added = after((out_beside, added), cot)
    small = jnp.concatenate(
        [
            ffn_gain_part,
            jnp.dot(logit_grad, ffn_low.astype(f32), precision=HIGHEST),
            jnp.dot(added, upstream, precision=HIGHEST),
        ]
    )
    small = jnp.transpose(jnp.pad(small, ((0, 128 - small.shape[0]), (0, 0)))).astype(bf)
    out_own = dotf(branch_cot, heads_own, 0, 1).astype(bf)
    out_other = dotf(branch_cot, heads_other, 0, 1).astype(bf)
    out_part = (out_own.astype(f32) + swap(out_other, "t").astype(f32)).astype(bf)
    out_part = over_sequences(jnp.concatenate([out_part, small], axis=1))
    out_z = lax.psum_scatter(out_part, "z", scatter_dimension=0, tiled=True)
    out_beside = swap(out_beside, "t")
    held = [(out_mine[k].astype(f32) + out_beside[k].astype(f32)).astype(bf) for k in range(4)]

    cot = exchange(cot)
    stack_a, stack_b = jnp.stack([pair_a, pair_ax]), jnp.stack([pair_b, pair_by])
    cot, held, out_part, stack_a, stack_b = lax.optimization_barrier((cot, held, out_part, stack_a, stack_b))
    pair_ya, pair_xb = swap(stack_a, "y"), swap(stack_b, "x")
    moved_out = [swap(held[1], "x"), swap(held[2], "y"), plane_diagonal(held[3])]
    dq, dkv_own, dkv_oth = flash_bwd(sc, start_rows, own, oth, cot, heads_full, lse)
    dkv_oth, pair_ya, pair_xb, moved_out = lax.optimization_barrier((dkv_oth, pair_ya, pair_xb, moved_out))
    dkv_oth = swap(dkv_oth, "t")
    sent = head_grad(
        at, dq, dkv_own, dkv_oth, all_cosine, all_sine, w_head, [pair_a, pair_b, pair_ax, pair_by, pair_ya, pair_xb]
    )
    if lax.axis_size("s") > 1:
        head_part = over_sequences(sent[:, 3 * HD :].reshape(width, half))
        sent = jnp.concatenate([sent[:, : 3 * HD], head_part.reshape(SPAN, slab, half)], axis=1)
    sent, held, expert_sum, out_z, prev_grad = lax.optimization_barrier((sent, held, expert_sum, out_z, prev_grad))
    arrived = exchange(sent)
    d_first = (lax.axis_index("s") * SPAN + place) * slab

    prev_both = both_halves(jnp.transpose(prev_grad))
    parts = jnp.concatenate([expert_sum, out_z], axis=1)
    own_rows, got_rows = plane_rows(parts.reshape(4, slab, parts.shape[1]))
    held, moved_out = after((held, moved_out), parts)
    ffn_sum = sum(v.astype(f32) for v in [held[0]] + moved_out)
    mixture = residual + ffn_sum + kept_column * normed_ffn + jnp.dot(added_columns, v_const, precision=HIGHEST)
    output = both_halves(mixture.astype(bf))
    w_gu_grad, w_down_grad, out_done = finish(expert_at, [own_rows] + got_rows, hidden_units)
    token_at = jnp.concatenate([first, other_first, (t * half).astype(jnp.int32).reshape(1)])
    arrived, prev_both, output, w_gu_grad, w_down_grad, out_done, token_at = lax.optimization_barrier(
        (arrived, prev_both, output, w_gu_grad, w_down_grad, out_done, token_at)
    )
    w_out_grad = jnp.transpose(out_done[:, :features])
    small = out_done[:, features:]
    small = small + swap(small, "t")
    arrived_own, arrived_other = of_heads(arrived)
    part_own, part_other = arrived_own[:, 3 * HD :, : 3 * HD], arrived_other[:, 3 * HD :, : 3 * HD]
    head_sum = part_own.astype(f32) + swap(part_other, "t").astype(f32)
    w_qkv_grad = jnp.transpose(head_sum.reshape(heads, slab, 3, HD), (2, 1, 0, 3)).reshape(3, slab, features)
    gain_part = jnp.sum(arrived[: 2 * heads, 3 * HD :, 3 * HD].astype(f32), axis=0)
    attn_gain_grad = (gain_part + swap(gain_part, "t")) / lax.dynamic_slice_in_dim(attn_gain, d_first, slab, 0)

    tokens_grad, grad_half = token_rows(
        token_at, arrived, w_qkv, w_qkv_other, residual_grad, tokens_mine, attn_gain
    )
    tokens_grad = lax.dynamic_update_slice_in_dim(tokens_grad, swap(grad_half, "t"), (1 - t) * half, 0)
    return (
        output,
        tokens_grad,
        prev_both,
        attn_gain_grad,
        w_qkv_grad,
        w_out_grad,
        small[:, 0],
        small[:, 1 : 1 + E_ALL],
        small[:, 9 : 9 + 2 * NCONST],
        jnp.transpose(small[:, 13 : 13 + NCONST]),
        w_gu_grad,
        w_down_grad,
    )


def solution(mesh):
    dp = mesh.shape["dp"]
    devices = mesh.devices.reshape(dp // SPAN, 4, 2, 2, mesh.shape["tensor"])
    inner = Mesh(devices, ("s", "z", "y", "x", "t"))
    d = ("s", "z", "y", "x")
    return jax.shard_map(
        local,
        mesh=inner,
        in_specs=(
            P(d, None),
            P(d),
            P(d, None),
            P(d, None),
            P(),
            P(None, None, "t"),
            P("t", None),
            P(),
            P(),
            P(),
            P(),
            P(None, None, None, "t"),
            P(None, "t", None),
            P(d, None),
        ),
        out_specs=(
            P(d, None),
            P(d, None),
            P(d, None),
            P(d),
            P(None, d, "t"),
            P("t", d),
            P(d),
            P(d, None),
            P(d, None),
            P(None, d),
            P(None, None, d, "t"),
            P(None, "t", d),
        ),
        check_vma=False,
    )
```

```python
import functools
import math

import jax
import jax.numpy as jnp
import numpy as np
from jax import lax
from jax.experimental import pallas as pl
from jax.experimental.pallas import tpu as pltpu
from jax.sharding import Mesh
from jax.sharding import PartitionSpec as P

f32 = jnp.float32
bf = jnp.bfloat16
E_FFN = 4
NCONST = 2
E_ALL = 8
SPAN = 16
SEQ_LEN = 8192
EPSILON = 1e-05
HIGHEST = lax.Precision.HIGHEST
GROUP = ("z", "y", "x")
GATE_ROWS = 16


HD = 64
NEG = -1e30
WIDE = (4, 2, 1)


def dotf(a, b, ca, cb):
    return lax.dot_general(a, b, (((ca,), (cb,)), ((), ())), preferred_element_type=f32)


def key_places(t, blocks, half):
    r = lax.broadcasted_iota(jnp.int32, (blocks * 2 * half, half), 0)
    inside = r % (2 * half)
    return r - inside + jnp.where(inside < half, t * half + inside, (1 - t) * half + inside - half)


def fwd_kernel(nb, half, sc, start_ref, own_ref, oth_ref, o_ref, of_ref, lse_ref, ktm, vt):
    keys = 2 * half
    t = sc[0]

    def prep(j, _):
        at = pl.ds(pl.multiple_of(j * keys, keys), half)
        more = pl.ds(pl.multiple_of(j * keys + half, half), half)
        ktm[at, :] = own_ref[j, HD : 2 * HD, :].T
        ktm[more, :] = oth_ref[j, 0:HD, :].T
        vt[:, at] = own_ref[j, 2 * HD : 3 * HD, :]
        vt[:, more] = oth_ref[j, HD : 2 * HD, :]
        return 0

    lax.fori_loop(0, nb, prep, 0)
    lane = lax.broadcasted_iota(jnp.int32, (1, half), 1)

    def qblock(s, _):
        q = own_ref[s, 0:HD, :] * bf(0.125)
        start_row = start_ref[s]
        last_row = s * keys + t * half + lane
        lo, ml = sc[1 + s], jnp.minimum(sc[1 + nb + s], s)

        def scores(j, n):
            return dotf(ktm[pl.ds(pl.multiple_of(j * keys, keys), n * keys), :], q, 1, 0)

        def allowed(j, n):
            place = key_places(t, n, half) + j * keys
            return (place >= start_row) & (place <= last_row)

        def values(j, n):
            return vt[:, pl.ds(pl.multiple_of(j * keys, keys), n * keys)]

        def emit(o, lse):
            o_ref[s] = o.astype(bf)
            of_ref[s] = o
            lse_ref[s] = lse

        def plain(j, n, c, masked):
            l, acc = c
            p = jnp.exp(scores(j, n))
            if masked:
                p = jnp.where(allowed(j, n), p, 0.0)
            return l + jnp.sum(p, axis=0, keepdims=True), acc + dotf(values(j, n), p.astype(bf), 1, 0)

        c = (jnp.zeros((1, half), f32), jnp.zeros((HD, half), f32))
        c = plain(s, 1, c, True)
        for masked, first, end in ((True, lo, ml), (False, jnp.maximum(lo, ml), s)):
            for n in (8,) + WIDE:
                count = jnp.maximum(end - first, 0) // n
                c = lax.fori_loop(0, count, lambda i, c: plain(first + i * n, n, c, masked), c)
                first = first + count * n
        l, acc = c
        emit(acc / l, jnp.log(l))
        fine = (jnp.min(l) > 1e-25) & (jnp.max(l) < 1e25)

        @pl.when(jnp.logical_not(fine))
        def _():
            def shifted(j, c):
                m, l, acc = c
                sco = jnp.where(allowed(j, 1), scores(j, 1), NEG)
                mn = jnp.maximum(m, jnp.max(sco, axis=0, keepdims=True))
                p = jnp.exp(sco - mn)
                al = jnp.exp(m - mn)
                return mn, l * al + jnp.sum(p, axis=0, keepdims=True), acc * al + dotf(values(j, 1), p.astype(bf), 1, 0)

            c = (jnp.full((1, half), NEG, f32), jnp.zeros((1, half), f32), jnp.zeros((HD, half), f32))
            c = shifted(s, c)
            m, l, acc = lax.fori_loop(lo, s, shifted, c)
            emit(acc / l, m + jnp.log(l))

        return 0

    lax.fori_loop(0, nb, qblock, 0)


def flash_fwd(sc, start, own, oth):
    nb, _, half = own.shape
    v = pl.BlockSpec(memory_space=pltpu.VMEM)
    return pl.pallas_call(
        functools.partial(fwd_kernel, nb, half),
        out_shape=(
            jax.ShapeDtypeStruct((nb, HD, half), bf),
            jax.ShapeDtypeStruct((nb, HD, half), f32),
            jax.ShapeDtypeStruct((nb, 1, half), f32),
        ),
        in_specs=[pl.BlockSpec(memory_space=pltpu.SMEM), v, v, v],
        out_specs=(v, v, v),
        scratch_shapes=[pltpu.VMEM((nb * 2 * half, HD), bf), pltpu.VMEM((HD, nb * 2 * half), bf)],
        compiler_params=pltpu.CompilerParams(vmem_limit_bytes=48 << 20),
        cost_estimate=pl.CostEstimate(flops=10**9, bytes_accessed=4 << 20, transcendentals=10**6),
        name="flash_fwd",
    )(sc, start, own, oth)


def bwd_kernel(
    nb, half, j0, j1, sc, start_ref, own_ref, oth_ref, do_ref, of_ref, lse_ref,
    dq_ref, dko_ref, dkx_ref, ktm, vtm, kt, qt, dot, dq_acc, dotm, qtm, stats,
):
    keys = 2 * half
    t = sc[0]

    def prep(j, _):
        k = j - j0
        ktm[k, 0:half, :] = own_ref[j, HD : 2 * HD, :].T
        ktm[k, half:keys, :] = oth_ref[j, 0:HD, :].T
        vtm[k, 0:half, :] = own_ref[j, 2 * HD : 3 * HD, :].T
        vtm[k, half:keys, :] = oth_ref[j, HD : 2 * HD, :].T
        kt[k, :, 0:half] = own_ref[j, HD : 2 * HD, :]
        kt[k, :, half:keys] = oth_ref[j, 0:HD, :]
        return 0

    lax.fori_loop(j0, j1, prep, 0)

    def prep_q(s, _):
        at = pl.ds(pl.multiple_of(s * half, half), half)
        q = own_ref[s, 0:HD, :] * bf(0.125)
        qt[:, at] = q
        qtm[at, :] = q.T
        dot[:, at] = do_ref[s]
        dotm[at, :] = do_ref[s].T
        dq_acc[:, at] = jnp.zeros((HD, half), f32)
        stats[0:1, at] = lse_ref[s]
        stats[1:2, at] = jnp.sum(do_ref[s].astype(f32) * of_ref[s], axis=0, keepdims=True)
        return 0

    lax.fori_loop(j0, nb, prep_q, 0)
    lane = lax.broadcasted_iota(jnp.int32, (1, half), 1)

    def kblock(j, _):
        k = j - j0
        kj, vj, ktj = ktm[k], vtm[k], kt[k]

        def tile(s, n, c, masked):
            dk, dv = c
            at = pl.ds(pl.multiple_of(s * half, half), n * half)
            sco = dotf(kj, qt[:, at], 1, 0)
            if masked:
                place = key_places(t, 1, half) + j * keys
                last_row = s * keys + t * half + lane
                sco = jnp.where((place >= start_ref[s]) & (place <= last_row), sco, NEG)
            p = jnp.exp(sco - stats[0:1, at])
            dp = dotf(vj, dot[:, at], 1, 0)
            ds = (p * (dp - stats[1:2, at])).astype(bf)
            dv = dv + dotf(p.astype(bf), dotm[at, :], 1, 0)
            dk = dk + dotf(ds, qtm[at, :], 1, 0)
            dq_acc[:, at] += dotf(ktj, ds, 1, 0)
            return dk, dv

        c = (jnp.zeros((keys, HD), f32), jnp.zeros((keys, HD), f32))
        c = tile(j, 1, c, True)
        mid, hi = sc[1 + 2 * nb + j], sc[1 + 3 * nb + j]
        first = j + 1
        for n in WIDE:
            count = jnp.maximum(mid - first, 0) // n
            c = lax.fori_loop(0, count, lambda i, c: tile(first + i * n, n, c, False), c)
            first = first + count * n
        dk, dv = lax.fori_loop(jnp.maximum(j + 1, mid), hi, lambda s, c: tile(s, 1, c, True), c)
        dk = dk.T
        dv = dv.T
        dko_ref[k, 0:HD, :] = dk[:, 0:half]
        dko_ref[k, HD : 2 * HD, :] = dv[:, 0:half]
        dkx_ref[k, 0:HD, :] = dk[:, half:keys].astype(bf)
        dkx_ref[k, HD : 2 * HD, :] = dv[:, half:keys].astype(bf)
        return 0

    lax.fori_loop(j0, j1, kblock, 0)

    def finish(s, _):
        at = pl.ds(pl.multiple_of(s * half, half), half)
        dq_ref[s] = (dq_acc[:, at] * 0.125).astype(bf)
        return 0

    def nothing(s, _):
        dq_ref[s] = jnp.zeros((HD, half), bf)
        return 0

    lax.fori_loop(0, j0, nothing, 0)
    lax.fori_loop(j0, nb, finish, 0)


def flash_bwd(sc, start, own, oth, do, of, lse, j0=0, j1=SPAN):
    nb, _, half = own.shape
    v = pl.BlockSpec(memory_space=pltpu.VMEM)
    n = j1 - j0
    return pl.pallas_call(
        functools.partial(bwd_kernel, nb, half, j0, j1),
        out_shape=(
            jax.ShapeDtypeStruct((nb, HD, half), bf),
            jax.ShapeDtypeStruct((n, 2 * HD, half), f32),
            jax.ShapeDtypeStruct((n, 2 * HD, half), bf),
        ),
        in_specs=[pl.BlockSpec(memory_space=pltpu.SMEM)] + [v] * 6,
        out_specs=(v, v, v),
        scratch_shapes=[
            pltpu.VMEM((n, 2 * half, HD), bf),
            pltpu.VMEM((n, 2 * half, HD), bf),
            pltpu.VMEM((n, HD, 2 * half), bf),
            pltpu.VMEM((HD, nb * half), bf),
            pltpu.VMEM((HD, nb * half), bf),
            pltpu.VMEM((HD, nb * half), f32),
            pltpu.VMEM((nb * half, HD), bf),
            pltpu.VMEM((nb * half, HD), bf),
            pltpu.VMEM((8, nb * half), f32),
        ],
        compiler_params=pltpu.CompilerParams(vmem_limit_bytes=56 << 20),
        cost_estimate=pl.CostEstimate(flops=10**9, bytes_accessed=4 << 20, transcendentals=10**6),
        name="flash_bwd",
    )(sc, start, own, oth, do, of, lse)


def bounds(start_all, t, nb, HB):
    st=start_all.reshape(nb,2,HB)
    mine=lax.dynamic_index_in_dim(st,t,1,keepdims=False)
    first=mine[:,0]; last=mine[:,HB-1]
    B=2*HB
    lo=first//B
    ml=(last+B-1)//B
    j=jnp.arange(nb)
    mid=jnp.sum((last[None,:]<=j[:,None]*B).astype(jnp.int32),axis=1)
    hi=jnp.sum((lo[None,:]<=j[:,None]).astype(jnp.int32),axis=1)
    mid=jnp.minimum(mid,hi)
    sc=jnp.concatenate([jnp.full((1,),t,jnp.int32),lo,ml,mid,hi]).astype(jnp.int32)
    return sc,mine[:,None,:]


def ffn_kernel(e_ref, u_ref, wgu_ref, wd_ref, *refs):
    pieces = refs[:8]
    x_out_ref, g_ref, wh_ref, mine_ref, other_ref, out_mine_ref, out_other_ref, held = refs[8:]
    half = u_ref.shape[1]
    width = x_out_ref.shape[2]
    hidden_units = wgu_ref.shape[3]
    e = e_ref[0]
    step = pl.program_id(0)
    for k in range(8):

        @pl.when(step == k)
        def _(k=k):
            held[...] = pieces[k][...]

    gates = held[half : half + GATE_ROWS, 0:half].astype(f32)
    row = lax.broadcasted_iota(jnp.int32, gates.shape, 0)
    gate_row = jnp.sum(jnp.where((row == e) | (row == e + E_FFN), gates, 0.0), axis=0, keepdims=True)
    gate = jnp.broadcast_to(gate_row, (8, half)).T[:, 0:1]
    x = held[0:half, :]
    x_out_ref[0] = x
    g = dotf(x, wgu_ref[0, 0], 1, 0)
    up = dotf(x, wgu_ref[0, 1], 1, 0)
    raw = u_ref[0].astype(f32)
    sig = 0.5 * jnp.tanh(0.5 * g) + 0.5
    silu = g * sig
    hid = silu * up
    hg = gate * raw
    g_ref[0, :, 0:hidden_units] = (hg * up * (sig + silu * (1.0 - sig))).astype(bf)
    g_ref[0, :, hidden_units : 2 * hidden_units] = (hg * silu).astype(bf)
    wh_ref[0] = (gate * hid).astype(bf)
    dots = jnp.broadcast_to(jnp.sum(hid * raw, axis=-1, keepdims=True), (half, 128)).T[0:8]
    total = dotf(g_ref[0, :, 0:hidden_units], wgu_ref[0, 0], 1, 1)
    total = total + dotf(g_ref[0, :, hidden_units : 2 * hidden_units], wgu_ref[0, 1], 1, 1)
    result = dotf(wh_ref[0], wd_ref[0], 1, 0)
    drow = lax.broadcasted_iota(jnp.int32, (GATE_ROWS, half), 0)
    placed = jnp.where(drow == e, jnp.broadcast_to(dots[0:1, :], (GATE_ROWS, half)), 0.0).astype(bf)

    def put(ref):
        ref[0, 0:half, :] = total.astype(bf)
        ref[0, half : half + GATE_ROWS, :] = jnp.zeros((GATE_ROWS, width), bf)
        ref[0, half : half + GATE_ROWS, 0:half] = placed

    @pl.when(step < 4)
    def _():
        put(mine_ref)
        out_mine_ref[0] = result.astype(bf)

    @pl.when(step >= 4)
    def _():
        put(other_ref)
        out_other_ref[0] = result.astype(bf)


def expert_pass(e, pieces, raw_all, wgu, wdown):
    rows, width = pieces[0].shape
    half = rows - GATE_ROWS
    hidden_units = wgu.shape[3]
    flops = 8 * half * width * hidden_units * 2 * 4
    return pl.pallas_call(
        ffn_kernel,
        out_shape=(
            jax.ShapeDtypeStruct((8, half, width), bf),
            jax.ShapeDtypeStruct((8, half, 2 * hidden_units), bf),
            jax.ShapeDtypeStruct((8, half, hidden_units), bf),
            jax.ShapeDtypeStruct((4, rows, width), bf),
            jax.ShapeDtypeStruct((4, rows, width), bf),
            jax.ShapeDtypeStruct((4, half, width), bf),
            jax.ShapeDtypeStruct((4, half, width), bf),
        ),
        grid_spec=pltpu.PrefetchScalarGridSpec(
            num_scalar_prefetch=1,
            grid=(8,),
            in_specs=[
                pl.BlockSpec((1, half, hidden_units), lambda i, e: (i, 0, 0)),
                pl.BlockSpec((1, 2, width, hidden_units), lambda i, e: (e[0], 0, 0, 0)),
                pl.BlockSpec((1, hidden_units, width), lambda i, e: (e[0], 0, 0)),
            ]
            + [pl.BlockSpec((rows, width), lambda i, e: (0, 0))] * 8,
            out_specs=(
                pl.BlockSpec((1, half, width), lambda i, e: (i, 0, 0)),
                pl.BlockSpec((1, half, 2 * hidden_units), lambda i, e: (i, 0, 0)),
                pl.BlockSpec((1, half, hidden_units), lambda i, e: (i, 0, 0)),
                pl.BlockSpec((1, rows, width), lambda i, e: (jnp.minimum(i, 3), 0, 0)),
                pl.BlockSpec((1, rows, width), lambda i, e: (jnp.maximum(i - 4, 0), 0, 0)),
                pl.BlockSpec((1, half, width), lambda i, e: (jnp.minimum(i, 3), 0, 0)),
                pl.BlockSpec((1, half, width), lambda i, e: (jnp.maximum(i - 4, 0), 0, 0)),
            ),
            scratch_shapes=[pltpu.VMEM((rows, width), bf)],
        ),
        compiler_params=pltpu.CompilerParams(vmem_limit_bytes=48 << 20),
        cost_estimate=pl.CostEstimate(flops=flops, bytes_accessed=40 << 20, transcendentals=2 << 20),
        name="expert_pass",
    )(e, raw_all, wgu, wdown, *pieces)


def hidden_cotangent_kernel(at_ref, w_ref, rows_ref, up_ref, raw_ref):
    rows = rows_ref[0]
    up_ref[0] = rows
    raw_ref[0] = dotf(rows, w_ref[0], 1, 1).astype(bf)


def hidden_cotangent(at, rows, w_down):
    pieces, half, width = rows.shape
    hidden_units = w_down.shape[1]
    return pl.pallas_call(
        hidden_cotangent_kernel,
        out_shape=(
            jax.ShapeDtypeStruct((pieces, half, width), bf),
            jax.ShapeDtypeStruct((pieces, half, hidden_units), bf),
        ),
        grid_spec=pltpu.PrefetchScalarGridSpec(
            num_scalar_prefetch=1,
            grid=(pieces,),
            in_specs=[
                pl.BlockSpec((1, hidden_units, width), lambda i, at: (at[0], 0, 0)),
                pl.BlockSpec((1, half, width), lambda i, at: (at[1 + i], 0, 0)),
            ],
            out_specs=(
                pl.BlockSpec((1, half, width), lambda i, at: (i, 0, 0)),
                pl.BlockSpec((1, half, hidden_units), lambda i, at: (i, 0, 0)),
            ),
        ),
        compiler_params=pltpu.CompilerParams(vmem_limit_bytes=40 << 20),
        cost_estimate=pl.CostEstimate(flops=32 * 10**8, bytes_accessed=12 << 20, transcendentals=0),
        name="hidden_cotangent",
    )(at, w_down, rows)


def exact(a, b, ca, cb):
    return lax.dot_general(a, b, (((ca,), (cb,)), ((), ())), precision=HIGHEST, preferred_element_type=f32)


def back_rows_kernel(
    first_ref, p0, p1, p2, p3, residual_ref, up_ref, gain_ref, rows_ref, small_ref, const_ref, own_ref, other_ref,
    grad_ref, low_ref, cot_ref, logit_ref, gain_out_ref,
):
    half, width = residual_ref.shape
    dx = p0[...].astype(f32) + p1[...].astype(f32) + p2[...].astype(f32) + p3[...].astype(f32)
    gating = dx[half : half + E_ALL, 0:half]
    dx = dx[0:half]
    residual, gain = residual_ref[...], gain_ref[...]
    up = up_ref[...].astype(f32)
    inverse = lax.rsqrt(jnp.mean(residual * residual, axis=-1, keepdims=True) + EPSILON)
    probs, hot = rows_ref[0:8], rows_ref[8:16]
    blend_one, blend_two, const_weight = rows_ref[16:18], rows_ref[18:20], rows_ref[20:22]
    kept = rows_ref[22:23]
    copy_dot = exact(jnp.ones((8, width), f32), up * (residual * inverse * gain), 1, 1)[0:1]
    vector_dot = exact(const_ref[...], up, 1, 1)[0:NCONST]
    const_dot = blend_one * copy_dot + blend_two * vector_dot
    row = lax.broadcasted_iota(jnp.int32, (8, half), 0)
    dots = jnp.where(row < E_FFN, gating, 0.0)
    dots = jnp.where(row == E_FFN + 1, copy_dot, dots)
    for c in range(NCONST):
        dots = jnp.where(row == E_FFN + 2 + c, const_dot[c : c + 1], dots)
    probs_grad = dots * hot
    logit_ref[0:8] = probs * (probs_grad - jnp.sum(probs * probs_grad, axis=0, keepdims=True))
    grad_one = const_weight * copy_dot
    grad_two = const_weight * vector_dot
    inner = blend_one * grad_one + blend_two * grad_two
    grad_one = blend_one * (grad_one - inner)
    grad_two = blend_two * (grad_two - inner)
    const_grad = jnp.zeros((8, half), f32)
    for c in range(NCONST):
        const_grad = jnp.where(row == 2 * c, grad_one[c : c + 1], const_grad)
        const_grad = jnp.where(row == 2 * c + 1, grad_two[c : c + 1], const_grad)
    logit_ref[8:16] = const_grad
    kept_column = jnp.broadcast_to(kept, (8, half)).T[:, 0:1]
    normed_grad = dx + exact(logit_ref[...], small_ref[...], 0, 0) + kept_column * up
    gain_out_ref[...] = jnp.sum(normed_grad * residual * inverse, axis=0, keepdims=True)
    scaled = normed_grad * gain
    mean = jnp.mean(scaled * residual, axis=-1, keepdims=True)
    grad = up + inverse * scaled - residual * (inverse * inverse * inverse * mean)
    grad_ref[...] = grad
    low = grad.astype(bf)
    low_ref[...] = low
    heads = own_ref.shape[0] // HD
    cot_ref[...] = jnp.zeros(cot_ref.shape, bf)
    for n, ref in enumerate((own_ref, other_ref)):
        rows = dotf(ref[...], low, 1, 1).astype(bf)
        for h in range(heads):
            cot_ref[first_ref[n] + h] = rows[h * HD : (h + 1) * HD]


def back_rows(first, parts, residual, up, gain, rows, small, const, own, other):
    half, width = residual.shape
    v = pl.BlockSpec(memory_space=pltpu.VMEM)
    return pl.pallas_call(
        back_rows_kernel,
        out_shape=(
            jax.ShapeDtypeStruct((half, width), f32),
            jax.ShapeDtypeStruct((half, width), bf),
            jax.ShapeDtypeStruct((SPAN, HD, half), bf),
            jax.ShapeDtypeStruct((16, half), f32),
            jax.ShapeDtypeStruct((1, width), f32),
        ),
        in_specs=[pl.BlockSpec(memory_space=pltpu.SMEM)] + [v] * 12,
        out_specs=(v,) * 5,
        compiler_params=pltpu.CompilerParams(vmem_limit_bytes=60 << 20),
        cost_estimate=pl.CostEstimate(flops=4 * 10**8, bytes_accessed=5 << 20, transcendentals=0),
        name="back_rows",
    )(first, *parts, residual, up, gain.reshape(1, width), rows, small, const, own, other)


def token_rows_kernel(first_ref, arrived_ref, own_ref, other_ref, grad_ref, x_ref, gain_ref, whole_ref, out_ref, rows):
    heads = own_ref.shape[2] // HD
    upstream = jnp.zeros(out_ref.shape, f32)
    for n, ref in enumerate((own_ref, other_ref)):
        for s in range(3):
            for h in range(heads):
                rows[h * HD : (h + 1) * HD, :] = arrived_ref[first_ref[n] + h, s * HD : (s + 1) * HD, :]
            upstream = upstream + dotf(rows[...], ref[s], 0, 1)
    x = x_ref[...].astype(f32)
    inverse = lax.rsqrt(jnp.mean(x * x, axis=-1, keepdims=True) + EPSILON)
    scaled = upstream * gain_ref[...]
    mean = jnp.mean(scaled * x, axis=-1, keepdims=True)
    out = grad_ref[...] + inverse * scaled - x * (inverse * inverse * inverse * mean)
    out_ref[...] = out
    whole_ref[pl.ds(pl.multiple_of(first_ref[2], out.shape[0]), out.shape[0]), :] = out


def token_rows(first, arrived, own, other, grad, x, gain):
    half, width = x.shape
    v = pl.BlockSpec(memory_space=pltpu.VMEM)
    return pl.pallas_call(
        token_rows_kernel,
        out_shape=(jax.ShapeDtypeStruct((2 * half, width), f32), jax.ShapeDtypeStruct((half, width), f32)),
        in_specs=[pl.BlockSpec(memory_space=pltpu.SMEM)] + [v] * 6,
        out_specs=(v, v),
        scratch_shapes=[pltpu.VMEM((own.shape[2], half), bf)],
        compiler_params=pltpu.CompilerParams(vmem_limit_bytes=60 << 20),
        cost_estimate=pl.CostEstimate(flops=10**9, bytes_accessed=6 << 20, transcendentals=0),
        name="token_rows",
    )(first, arrived, own, other, grad, x, gain.reshape(1, width))


def heads_kernel(first_ref, x_ref, gain_ref, w_ref, cos_ref, sin_ref, *refs):
    buffer_ref, normed_ref = refs[-2:]
    x = x_ref[...].astype(f32)
    inverse = lax.rsqrt(jnp.mean(x * x, axis=-1, keepdims=True) + EPSILON)
    normed = (x * inverse * gain_ref[...]).astype(bf)
    normed_ref[...] = normed
    cosine, sine = cos_ref[...], sin_ref[...]
    heads = w_ref.shape[2] // HD
    first = first_ref[0]
    buffer_ref[...] = refs[0][...] if len(refs) == 3 else jnp.zeros(buffer_ref.shape, bf)
    for s in range(3):
        rows = dotf(normed, w_ref[s], 1, 0).T
        for h in range(heads):
            part = rows[h * HD : (h + 1) * HD]
            if s < 2:
                one, two = part[: HD // 2], part[HD // 2 :]
                part = jnp.concatenate([one * cosine - two * sine, two * cosine + one * sine], axis=0)
            buffer_ref[first + h, s * HD : (s + 1) * HD, :] = part.astype(bf)


def head_rows(first, x, gain, w, cosine, sine, buffer=None):
    half, width = x.shape
    v = pl.BlockSpec(memory_space=pltpu.VMEM)
    given = [] if buffer is None else [buffer]
    return pl.pallas_call(
        heads_kernel,
        out_shape=(
            jax.ShapeDtypeStruct((SPAN, 3 * HD, half), bf),
            jax.ShapeDtypeStruct((half, width), bf),
        ),
        in_specs=[pl.BlockSpec(memory_space=pltpu.SMEM)] + [v] * 5 + [v] * len(given),
        out_specs=(v, v),
        compiler_params=pltpu.CompilerParams(vmem_limit_bytes=40 << 20),
        cost_estimate=pl.CostEstimate(flops=5 * 10**8, bytes_accessed=4 << 20, transcendentals=0),
        name="head_rows",
    )(first, x, gain.reshape(1, width), w, cosine, sine, *given)


def head_grad_kernel(at_ref, dq_ref, own_ref, other_ref, cos_ref, sin_ref, w_ref, *refs):
    pieces, out_ref, turned_rows = refs[:-2], refs[-2], refs[-1]
    half, width = pieces[0].shape[-2:]
    blocks = out_ref.shape[0]

    def back(rows, block):
        one, two = rows[: HD // 2], rows[HD // 2 :]
        cosine, sine = cos_ref[block], sin_ref[block]
        return jnp.concatenate([one * cosine + two * sine, two * cosine - one * sine], axis=0)

    acc = jnp.zeros((3 * HD, width), f32)
    n = 0
    for ref in pieces:
        places = list(np.ndindex(*ref.shape[:-2]))
        for k in range(len(places)):
            block = at_ref[n]
            dkv = own_ref[block] + other_ref[block].astype(f32)
            rows = jnp.concatenate(
                [back(dq_ref[block].astype(f32), block), back(dkv[:HD], block), dkv[HD:]], axis=0
            ).astype(bf)
            out_ref[block, 0 : 3 * HD, :] = rows
            turned_rows[:, k * half : (k + 1) * half] = rows
            n += 1
        count = len(places) * half
        acc = acc + dotf(turned_rows[:, 0:count], ref[...].reshape(count, width), 1, 0)
    gain_row = jnp.sum(acc * w_ref[...].astype(f32), axis=0, keepdims=True)
    turned = jnp.concatenate([acc, jnp.broadcast_to(gain_row, (8, width))], axis=0).T.astype(bf)
    rows = turned.shape[0] // blocks
    for block in range(blocks):
        out_ref[block, 3 * HD :, :] = jnp.zeros((rows, out_ref.shape[2]), bf)
        out_ref[block, 3 * HD :, 0 : 3 * HD + 8] = turned[block * rows : (block + 1) * rows]


def head_grad(at, dq, own, other, cosine, sine, w_head, pieces):
    v = pl.BlockSpec(memory_space=pltpu.VMEM)
    half, width = pieces[0].shape[-2:]
    blocks = dq.shape[0]
    return pl.pallas_call(
        head_grad_kernel,
        out_shape=jax.ShapeDtypeStruct((blocks, 3 * HD + width // blocks, half), bf),
        in_specs=[pl.BlockSpec(memory_space=pltpu.SMEM)] + [v] * (6 + len(pieces)),
        out_specs=v,
        scratch_shapes=[pltpu.VMEM((3 * HD, 4 * half), bf)],
        compiler_params=pltpu.CompilerParams(vmem_limit_bytes=60 << 20),
        cost_estimate=pl.CostEstimate(flops=12 * 10**8, bytes_accessed=12 << 20, transcendentals=0),
        name="head_grad",
    )(at, dq, own, other, cosine, sine, w_head, *pieces)


def finish_kernel(e_ref, *refs):
    parts, (gu_ref, down_ref, sum_ref) = refs[:4], refs[4:]
    units = down_ref.shape[1]
    rest = 3 * units
    rows = [p[...].astype(f32) for p in parts]
    sum_ref[...] = rows[0][:, rest:] + rows[1][:, rest:] + rows[2][:, rest:] + rows[3][:, rest:]
    for k in range(E_FFN):
        distance = e_ref[0] ^ k
        low = jnp.where(distance == 0, rows[0][:, :rest], rows[1][:, :rest])
        high = jnp.where(distance == 2, rows[2][:, :rest], rows[3][:, :rest])
        one = jnp.where(distance < 2, low, high)
        gu_ref[k, 0] = one[:, 0:units]
        gu_ref[k, 1] = one[:, units : 2 * units]
        down_ref[k] = one[:, 2 * units :].T


def finish(e, parts, units):
    slab, columns = parts[0].shape
    v = pl.BlockSpec(memory_space=pltpu.VMEM)
    return pl.pallas_call(
        finish_kernel,
        out_shape=(
            jax.ShapeDtypeStruct((E_FFN, 2, slab, units), f32),
            jax.ShapeDtypeStruct((E_FFN, units, slab), f32),
            jax.ShapeDtypeStruct((slab, columns - 3 * units), f32),
        ),
        in_specs=[pl.BlockSpec(memory_space=pltpu.SMEM)] + [v] * 4,
        out_specs=(v, v, v),
        compiler_params=pltpu.CompilerParams(vmem_limit_bytes=40 << 20),
        cost_estimate=pl.CostEstimate(flops=10**5, bytes_accessed=10**5, transcendentals=0),
        name="finish",
    )(e, *parts)


def swap(value, axis):
    return lax.ppermute(value, axis, [(0, 1), (1, 0)])


def plane_diagonal(value):
    return lax.ppermute(value, ("y", "x"), [(i, 3 - i) for i in range(4)])


def plane_gather(piece):
    mine = [piece, swap(piece, "x"), swap(piece, "y"), plane_diagonal(piece)]
    return mine + [swap(p, "t") for p in mine]


def plane_scatter(mine, other, later):
    held = [(mine[k].astype(f32) + other[k].astype(f32)).astype(bf) for k in range(4)]
    held, later = lax.optimization_barrier((held, later))
    return [held[0], swap(held[1], "x"), swap(held[2], "y"), plane_diagonal(held[3])], later


def over_z(value, distance):
    return lax.ppermute(value, "z", [(i, i ^ distance) for i in range(4)])


def total(parts):
    first, rest = parts
    return first.astype(f32) + sum(p.astype(f32) for p in rest)


def plane_rows(chunks):
    b = lax.axis_index(("y", "x"))
    pick = lambda d: lax.dynamic_index_in_dim(chunks, b ^ d, 0, keepdims=False)
    return pick(0), [swap(pick(1), "x"), swap(pick(2), "y"), plane_diagonal(pick(3))]


def after(value, *others):
    return lax.optimization_barrier((value, others))[0]


def over_sequences(rows):
    if lax.axis_size("s") == 1:
        return rows
    return lax.psum_scatter(rows, "s", scatter_dimension=0, tiled=True)


def first_tokens(segments):
    def gathered(value, moved, places):
        low, high = places
        first = jnp.where(low == 0, jnp.stack([value, moved[0]]), jnp.stack([moved[0], value]))
        second = jnp.where(low == 0, jnp.stack([moved[1], moved[2]]), jnp.stack([moved[2], moved[1]]))
        return jnp.where(high == 0, jnp.stack([first, second]), jnp.stack([second, first]))

    z = lax.axis_index("z")
    plane = [swap(segments, "x"), swap(segments, "y"), plane_diagonal(segments)]
    ids = gathered(segments, plane, (lax.axis_index("x"), lax.axis_index("y"))).reshape(-1)
    ids = gathered(ids, [over_z(ids, d) for d in (1, 2, 3)], (z % 2, z // 2)).reshape(-1)
    count = ids.shape[0]
    index = jnp.arange(count, dtype=jnp.int32)
    before = jnp.concatenate([ids[:1], ids[:-1]])
    opens = jnp.where(ids != before, index, 0).reshape(-1, 256)
    n = opens.shape[0]
    lane = jnp.arange(256, dtype=jnp.int32)
    within = jnp.max(jnp.where(lane[None, None, :] <= lane[None, :, None], opens[:, None, :], 0), axis=-1)
    block = jnp.arange(n, dtype=jnp.int32)
    top = jnp.max(opens, axis=1)
    carry = jnp.max(jnp.where(block[None, :] < block[:, None], top[None, :], 0), axis=1)
    return jnp.maximum(within, carry[:, None]).reshape(-1)


def rotary_tables(position, half_dim):
    inv_freq = jnp.exp(jnp.arange(half_dim).astype(f32) * (-math.log(10000.0) / half_dim))
    phases = inv_freq[:, None] * position.astype(f32)[None, :]
    return jnp.cos(phases), jnp.sin(phases)


def rotate(values, cosine, sine):
    half_dim = values.shape[-2] // 2
    one, two = values[..., :half_dim, :], values[..., half_dim:, :]
    return jnp.concatenate([one * cosine - two * sine, two * cosine + one * sine], axis=-2)


def norm_forward(values, gain):
    inverse = lax.rsqrt(jnp.mean(values * values, axis=-1, keepdims=True) + EPSILON)
    return values * inverse * gain, inverse


def norm_backward(values, inverse, gain, upstream):
    scaled = upstream * gain
    inner = jnp.mean(scaled * values, axis=-1, keepdims=True)
    return (
        inverse * scaled - values * inverse * inverse * inverse * inner,
        jnp.sum(upstream * values * inverse, axis=0),
    )


def local(
    tokens,
    segments,
    routes,
    prev_logits,
    attn_gain,
    w_qkv,
    w_out,
    ffn_gain,
    w_router,
    w_const,
    v_const,
    w_gu,
    w_down,
    cotangent,
):
    tok_count, width = tokens.shape
    half = tok_count // 2
    features = w_qkv.shape[2]
    heads = features // HD
    t = lax.axis_index("t")
    place = lax.axis_index(GROUP)
    expert = lax.axis_index(("y", "x"))

    def mine(value):
        return lax.dynamic_slice_in_dim(value, t * half, half, 0)

    def both_halves(value):
        other = swap(value, "t")
        whole = jnp.zeros((tok_count,) + value.shape[1:], value.dtype)
        whole = lax.dynamic_update_slice_in_dim(whole, value, t * half, 0)
        return lax.dynamic_update_slice_in_dim(whole, other, (1 - t) * half, 0)

    w_qkv_other = swap(w_qkv, "t")
    w_out_other = swap(w_out, "t")
    inputs = mine(tokens).astype(f32)
    upstream_low = mine(cotangent)
    upstream = upstream_low.astype(f32)
    my_routes = jnp.transpose(mine(routes))
    my_prev = jnp.transpose(mine(prev_logits))
    kinds = jnp.arange(E_ALL, dtype=jnp.int32)[:, None]
    hot = (my_routes[0:1] == kinds).astype(f32) + (my_routes[1:2] == kinds).astype(f32)
    position = (place * tok_count + t * half + jnp.arange(half, dtype=jnp.int32)) % SEQ_LEN
    cosine, sine = rotary_tables(position, HD // 2)
    tokens_mine = mine(tokens)
    first = (t * heads).astype(jnp.int32).reshape(1)
    other_first = ((1 - t) * heads).astype(jnp.int32).reshape(1)
    buffer, normed_low = head_rows(first, tokens_mine, attn_gain, w_qkv, cosine, sine)
    buffer, _ = head_rows(other_first, tokens_mine, attn_gain, w_qkv_other, cosine, sine, buffer)

    def of_heads(buffer):
        return (
            lax.dynamic_slice_in_dim(buffer, t * heads, heads, 0),
            lax.dynamic_slice_in_dim(buffer, (1 - t) * heads, heads, 0),
        )

    def exchange(buffer):
        return lax.all_to_all(buffer, GROUP, 0, 0, tiled=True)

    upstream_sent, segments, buffer = lax.optimization_barrier((upstream_low, segments, buffer))
    start_all = first_tokens(segments)
    sc, start_rows = bounds(start_all, t, SPAN, half)
    own = exchange(buffer)
    oth = swap(own[:, HD:], "t")
    up_gathered = lax.all_gather(upstream_sent, ("y", "x", "t"))
    piece_rank = jnp.bitwise_xor(2 * expert + t, jnp.array((0, 2, 4, 6, 1, 3, 5, 7), jnp.int32))
    expert_at = expert.astype(jnp.int32).reshape(1)
    normed_sent, own_q, sc, start_rows = lax.optimization_barrier((normed_low, own, sc, start_rows))
    along_z = [normed_sent] + [over_z(normed_sent, d) for d in (1, 2, 3)]
    heads_rows, heads_full, lse = flash_fwd(sc, start_rows, own_q, oth)
    heads_rows, up_gathered, along_z = lax.optimization_barrier((heads_rows, up_gathered, along_z))
    back = exchange(heads_rows)
    up_all, raw_all = hidden_cotangent(
        jnp.concatenate([expert_at, piece_rank.astype(jnp.int32)]), up_gathered, w_down
    )
    back, raw_all = lax.optimization_barrier((back, raw_all))
    heads_own, heads_other = (v.reshape(features, half) for v in of_heads(back))
    branch = dotf(heads_own, w_out, 0, 0) + dotf(heads_other, w_out_other, 0, 0)
    residual = inputs + branch
    normed_ffn, inverse_ffn = norm_forward(residual, ffn_gain)
    ffn_low = normed_ffn.astype(bf)
    w_small = jnp.concatenate([w_router, w_const], axis=1)
    logits = dotf(w_small, ffn_low, 0, 1)
    router_probs = jax.nn.softmax(logits[:E_ALL] + my_prev, axis=0)
    expert_weight = router_probs * hot
    gate_rows = expert_weight[:E_FFN]
    gate_high = gate_rows.astype(bf)
    gate_low = (gate_rows - gate_high.astype(f32)).astype(bf)
    gate_block = jnp.pad(
        jnp.concatenate([gate_high, gate_low]), ((0, GATE_ROWS - 2 * E_FFN), (0, width - half))
    )
    x_all = plane_gather(jnp.concatenate([ffn_low, gate_block]))
    w_held, w_other_held, t_late = after((w_qkv, w_qkv_other, t), ffn_low)
    all_position = (jnp.arange(SPAN, dtype=jnp.int32)[:, None] * tok_count + t_late * half)[:, :, None] + jnp.arange(half, dtype=jnp.int32)
    all_cosine, all_sine = rotary_tables(all_position.reshape(-1), HD // 2)
    by_block = lambda table: jnp.transpose(table.reshape(HD // 2, SPAN, half), (1, 0, 2))
    all_cosine, all_sine = by_block(all_cosine), by_block(all_sine)
    pair_a, pair_b = jnp.stack(along_z[:2]), jnp.stack(along_z[2:])
    near = (0, 4, 8, 12, 1, 5, 10, 14, 2, 6, 3, 7, 9, 13, 11, 15)
    at = jnp.bitwise_xor(place, jnp.array(near, jnp.int32)).astype(jnp.int32)
    head_first = jnp.minimum(place, 2 * heads - 1) % heads * HD
    of_head = lambda w: lax.dynamic_slice_in_dim(w, head_first, HD, 2)
    w_head = jnp.where(jnp.minimum(place // heads, 1) == t, of_head(w_held), of_head(w_other_held))
    w_head = jnp.swapaxes(w_head, 1, 2).reshape(3 * HD, width)
    x_all, all_cosine, all_sine, pair_a, pair_b, at, w_head = lax.optimization_barrier(
        (x_all, all_cosine, all_sine, pair_a, pair_b, at, w_head)
    )
    pair_ax, pair_by = swap(pair_a, "x"), swap(pair_b, "y")
    x_only, g_all, weighted, dx_mine, dx_other, out_mine, out_beside = expert_pass(
        expert_at, x_all, raw_all, w_gu, w_down
    )
    dx_mine, dx_other, pair_ax, pair_by = lax.optimization_barrier((dx_mine, dx_other, pair_ax, pair_by))
    dx_other = swap(dx_other, "t")
    hidden_units = w_down.shape[1]
    received, (weighted, g_all) = plane_scatter(dx_mine, dx_other, (weighted, g_all))
    down_part = jnp.einsum("ptd,ptf->df", up_all, weighted, preferred_element_type=f32).astype(bf)
    gu_part = jnp.einsum("ptd,ptf->df", x_only, g_all, preferred_element_type=f32).astype(bf)
    expert_part = over_sequences(jnp.concatenate([gu_part, down_part], axis=1))
    slab = expert_part.shape[0] // SPAN
    received, expert_part = lax.optimization_barrier((received, expert_part))
    expert_sum = lax.psum_scatter(expert_part, "z", scatter_dimension=0, tiled=True)

    pairs = logits[E_ALL:].reshape(NCONST, 2, half)
    blend_one = jax.nn.sigmoid(pairs[:, 0] - pairs[:, 1])
    blend_two = jax.nn.sigmoid(pairs[:, 1] - pairs[:, 0])
    const_weight = expert_weight[E_FFN + 2 :]
    kept = expert_weight[E_FFN + 1 : E_FFN + 2] + jnp.sum(const_weight * blend_one, axis=0, keepdims=True)
    added = const_weight * blend_two
    columns = jnp.transpose(jnp.concatenate([kept, added]))
    kept_column, added_columns = columns[:, 0:1], columns[:, 1:]

    pad_rows = lambda v, n: jnp.pad(v, ((0, n - v.shape[0]), (0, 0)))
    row_pack = pad_rows(jnp.concatenate([router_probs, hot, blend_one, blend_two, const_weight, kept]), 24)
    small_rows = pad_rows(jnp.transpose(w_small).astype(f32), 16)
    residual_grad, branch_cot, cot, logit_grad, ffn_gain_part = back_rows(
        jnp.concatenate([first, other_first]),
        received,
        residual,
        upstream_low,
        ffn_gain,
        row_pack,
        small_rows,
        pad_rows(v_const, 8),
        w_out,
        w_out_other,
    )
    logit_grad = logit_grad[: E_ALL + 2 * NCONST]
    prev_grad = logit_grad[:E_ALL]
    out_beside, added = after((out_beside, added), cot)
    small = jnp.concatenate(
        [
            ffn_gain_part,
            jnp.dot(logit_grad, ffn_low.astype(f32), precision=HIGHEST),
            jnp.dot(added, upstream, precision=HIGHEST),
        ]
    )
    small = jnp.transpose(jnp.pad(small, ((0, 128 - small.shape[0]), (0, 0)))).astype(bf)
    out_own = dotf(branch_cot, heads_own, 0, 1).astype(bf)
    out_other = dotf(branch_cot, heads_other, 0, 1).astype(bf)
    out_part = (out_own.astype(f32) + swap(out_other, "t").astype(f32)).astype(bf)
    out_part = over_sequences(jnp.concatenate([out_part, small], axis=1))
    out_z = lax.psum_scatter(out_part, "z", scatter_dimension=0, tiled=True)
    out_beside = swap(out_beside, "t")
    held = [(out_mine[k].astype(f32) + out_beside[k].astype(f32)).astype(bf) for k in range(4)]

    cot = exchange(cot)
    stack_a, stack_b = jnp.stack([pair_a, pair_ax]), jnp.stack([pair_b, pair_by])
    cot, held, out_part, stack_a, stack_b = lax.optimization_barrier((cot, held, out_part, stack_a, stack_b))
    pair_ya, pair_xb = swap(stack_a, "y"), swap(stack_b, "x")
    moved_out = [swap(held[1], "x"), swap(held[2], "y"), plane_diagonal(held[3])]
    dq, dkv_own, dkv_oth = flash_bwd(sc, start_rows, own, oth, cot, heads_full, lse)
    dkv_oth, pair_ya, pair_xb, moved_out = lax.optimization_barrier((dkv_oth, pair_ya, pair_xb, moved_out))
    dkv_oth = swap(dkv_oth, "t")
    sent = head_grad(
        at, dq, dkv_own, dkv_oth, all_cosine, all_sine, w_head, [pair_a, pair_b, pair_ax, pair_by, pair_ya, pair_xb]
    )
    if lax.axis_size("s") > 1:
        head_part = over_sequences(sent[:, 3 * HD :].reshape(width, half))
        sent = jnp.concatenate([sent[:, : 3 * HD], head_part.reshape(SPAN, slab, half)], axis=1)
    sent, held, expert_sum, out_z, prev_grad = lax.optimization_barrier((sent, held, expert_sum, out_z, prev_grad))
    arrived = exchange(sent)
    d_first = (lax.axis_index("s") * SPAN + place) * slab

    prev_both = both_halves(jnp.transpose(prev_grad))
    parts = jnp.concatenate([expert_sum, out_z], axis=1)
    own_rows, got_rows = plane_rows(parts.reshape(4, slab, parts.shape[1]))
    held, moved_out = after((held, moved_out), parts)
    ffn_sum = sum(v.astype(f32) for v in [held[0]] + moved_out)
    mixture = residual + ffn_sum + kept_column * normed_ffn + jnp.dot(added_columns, v_const, precision=HIGHEST)
    output = both_halves(mixture.astype(bf))
    w_gu_grad, w_down_grad, out_done = finish(expert_at, [own_rows] + got_rows, hidden_units)
    token_at = jnp.concatenate([first, other_first, (t * half).astype(jnp.int32).reshape(1)])
    arrived, prev_both, w_gu_grad, w_down_grad, out_done, token_at = lax.optimization_barrier(
        (arrived, prev_both, w_gu_grad, w_down_grad, out_done, token_at)
    )
    w_out_grad = jnp.transpose(out_done[:, :features])
    small = out_done[:, features:]
    small = small + swap(small, "t")
    arrived_own, arrived_other = of_heads(arrived)
    part_own, part_other = arrived_own[:, 3 * HD :, : 3 * HD], arrived_other[:, 3 * HD :, : 3 * HD]
    head_sum = part_own.astype(f32) + swap(part_other, "t").astype(f32)
    w_qkv_grad = jnp.transpose(head_sum.reshape(heads, slab, 3, HD), (2, 1, 0, 3)).reshape(3, slab, features)
    gain_part = jnp.sum(arrived[: 2 * heads, 3 * HD :, 3 * HD].astype(f32), axis=0)
    attn_gain_grad = (gain_part + swap(gain_part, "t")) / lax.dynamic_slice_in_dim(attn_gain, d_first, slab, 0)

    tokens_grad, grad_half = token_rows(
        token_at, arrived, w_qkv, w_qkv_other, residual_grad, tokens_mine, attn_gain
    )
    tokens_grad = lax.dynamic_update_slice_in_dim(tokens_grad, swap(grad_half, "t"), (1 - t) * half, 0)
    return (
        output,
        tokens_grad,
        prev_both,
        attn_gain_grad,
        w_qkv_grad,
        w_out_grad,
        small[:, 0],
        small[:, 1 : 1 + E_ALL],
        small[:, 9 : 9 + 2 * NCONST],
        jnp.transpose(small[:, 13 : 13 + NCONST]),
        w_gu_grad,
        w_down_grad,
    )


def solution(mesh):
    dp = mesh.shape["dp"]
    devices = mesh.devices.reshape(dp // SPAN, 4, 2, 2, mesh.shape["tensor"])
    inner = Mesh(devices, ("s", "z", "y", "x", "t"))
    d = ("s", "z", "y", "x")
    return jax.shard_map(
        local,
        mesh=inner,
        in_specs=(
            P(d, None),
            P(d),
            P(d, None),
            P(d, None),
            P(),
            P(None, None, "t"),
            P("t", None),
            P(),
            P(),
            P(),
            P(),
            P(None, None, None, "t"),
            P(None, "t", None),
            P(d, None),
        ),
        out_specs=(
            P(d, None),
            P(d, None),
            P(d, None),
            P(d),
            P(None, d, "t"),
            P("t", d),
            P(d),
            P(d, None),
            P(d, None),
            P(None, d),
            P(None, None, d, "t"),
            P(None, "t", d),
        ),
        check_vma=False,
    )
```
